512 devices in a mesh: grp: 64 (over y, z), tp: 8 (over x, core).
Axes of the slice: x: 4, y: 8, z: 8, core: 2. Of those that a mesh axis runs over, the one named last changes fastest.
Arguments:
- queries: bfloat16 [512, 2048], P('grp', 'tp'), may hold values from -8 to 8
- new_kv: bfloat16 [512, 2, 512], P('grp', None, 'tp'), may hold values from -6 to 6
- home_cache: bfloat16 [512, 2, 8, 512, 128], P('grp', None, 'tp'), may hold values from -28 to 28
- help_cache: bfloat16 [256, 2, 8, 512, 128], P('grp', None, 'tp'), may hold values from -6 to 6
- lengths: int32 [512], P('grp'), may hold values from 2 to 2048, as said below
- split_at: int32 [512], P('grp'), may hold values from 1 to 1024, as said below
- helper_req: int32 [256], P('grp'), may hold values from 0 to 511, as said below
- out_weight: bfloat16 [2048, 2048], P('tp'), may hold values from -0.125 to 0.125
Outputs:
- attn_out: bfloat16 [512, 2048], P('grp', 'tp')
The draws below stay inside these ranges and needn't reach their ends.
Inputs may be any that keep to these rules, and one draw needn't show every extreme that they name: `lengths`: in each aligned block of 8 requests exactly 4 have more than 1024 cached positions. `split_at`: equal to the length for requests of 1024 positions or fewer; otherwise between length - 1024 and min(1024, length - 1). `helper_req`: groups come in pairs; the 4 helper slots of a group serve, in increasing order, the requests of its partner group that have more than 1024 positions, so each such request has exactly one helper slot and all values are distinct.
All inputs are finite; a program needn't handle non-finite values.
Results may differ from the reference program's by a relative error of at most 0.007.
Values may be sent and summed in bfloat16 or wider, within the bound.
A program may use at most 192 MiB of HBM per device.

```python
import jax
import jax.numpy as jnp
from jax import lax

D = 2048
H = 32
KVH = 8
HD = 64
CTX = 1024
REQ_G = 8
HELP_G = 4
REQUESTS = 512
HELP = 256


def query_values(key):
    source = jax.random.fold_in(key, 101)
    drawn = jnp.clip(2.0 * jax.random.normal(source, (REQUESTS, H * HD), jnp.float32), -8.0, 8.0)
    return drawn.astype(jnp.bfloat16).astype(jnp.float32)


def draw_queries(key, part):
    return query_values(key).astype(jnp.bfloat16)


def draw_home_cache(key, part):
    shape = (REQUESTS, 2, KVH, CTX // 2, 2 * HD)
    base = jnp.clip(jax.random.normal(jax.random.fold_in(key, 102), shape, jnp.float32), -6.0, 6.0)
    return base.astype(jnp.bfloat16)


def request_plan(key):
    groups = REQUESTS // REQ_G
    group_keys = jax.random.split(jax.random.fold_in(key, 201), groups)
    ranks = jax.vmap(lambda item: jax.random.permutation(item, REQ_G))(group_keys)
    spanning = ranks < HELP_G
    short_len = jax.random.randint(jax.random.fold_in(key, 202), (groups, REQ_G), 2, CTX + 1)
    long_len = jax.random.randint(jax.random.fold_in(key, 203), (groups, REQ_G), CTX + 1, 2 * CTX + 1)
    all_len = jnp.where(spanning, long_len, short_len).reshape(-1)
    span_flat = spanning.reshape(-1)
    forced_group = jax.random.randint(jax.random.fold_in(key, 204), (), 0, groups)
    forced = forced_group * REQ_G + jnp.argmax(ranks[forced_group] == 0).astype(jnp.int32)
    ident = jnp.arange(REQUESTS, dtype=jnp.int32)
    all_len = jnp.where(ident == forced, 2 * CTX, all_len)
    lower = jnp.maximum(all_len - CTX, 1)
    upper = jnp.minimum(CTX, all_len - 1)
    cut_at = jax.random.randint(jax.random.fold_in(key, 205), (REQUESTS,), lower, upper + 1)
    splits = jnp.where(span_flat, cut_at, all_len)
    splits = jnp.where(ident == forced, CTX, splits)
    order = jax.random.permutation(jax.random.fold_in(key, 206), groups)
    places = jnp.argsort(order, stable=True)
    partner = order[jnp.bitwise_xor(places, 1)]
    score_keys = jnp.where(spanning, 0, 1) * REQ_G + jnp.arange(REQ_G, dtype=jnp.int32)[None, :]
    slot_order = jnp.argsort(score_keys, axis=1, stable=True)[:, :HELP_G]
    helpers = (partner[:, None] * REQ_G + slot_order[partner]).reshape(-1)
    return (all_len.astype(jnp.int32), splits.astype(jnp.int32), helpers.astype(jnp.int32))


def draw_lengths(key, part):
    return request_plan(key)[0]


def draw_split_at(key, part):
    return request_plan(key)[1]


def draw_helper_req(key, part):
    return request_plan(key)[2]


def block_levels(key, dims, shards, least, largest):
    def one(position, blocks):
        steps = jax.random.uniform(jax.random.fold_in(jax.random.fold_in(key, 6), position), (blocks,), jnp.float32, least / len(shards), largest / len(shards))
        return jnp.repeat(jnp.exp(steps), dims[position] // blocks).reshape((-1,) + (1,) * (len(dims) - position - 1))

    loudness = one(*shards[0])
    for cut in shards[1:]:
        loudness = loudness * one(*cut)
    return loudness


def bell_draw(rng, dims, deviation, most, pieces=(), held_as=jnp.bfloat16):
    values = deviation * jax.random.normal(rng, dims, jnp.float32)
    if pieces:
        values = values * block_levels(rng, dims, pieces, -0.22, 0.18)
    return jnp.clip(values, -most, most).astype(held_as)


def setup_inputs(seed: int = 0) -> dict:
    streams_of = jax.random.split(jax.random.key(seed), 9)
    queries = draw_queries(jax.random.fold_in(streams_of[8], 71), 0)
    new_kv = bell_draw(streams_of[1], (REQUESTS, 2, KVH * HD), 1.0, 6.0, ((0, 64), (2, 8)))
    home_cache = draw_home_cache(jax.random.fold_in(streams_of[8], 71), 0)
    help_cache = bell_draw(streams_of[3], (HELP, 2, KVH, CTX // 2, 2 * HD), 1.0, 6.0, ((0, 64), (2, 8)))
    lengths = draw_lengths(jax.random.fold_in(streams_of[8], 71), 0)
    split_at = draw_split_at(jax.random.fold_in(streams_of[8], 71), 0)
    helper_req = draw_helper_req(jax.random.fold_in(streams_of[8], 71), 0)
    out_weight = bell_draw(streams_of[7], (H * HD, D), (H * HD) ** -0.5, 0.125, ((0, 8),))
    return {"queries": queries, "new_kv": new_kv, "home_cache": home_cache, "help_cache": help_cache, "lengths": lengths, "split_at": split_at, "helper_req": helper_req, "out_weight": out_weight}


def attend(queries, cache, count, fresh):
    row_count = queries.shape[0]
    kv_heads = cache.shape[2]
    head_width = cache.shape[4] // 2
    context = cache.shape[3] * 2
    group_size = queries.shape[1] // (kv_heads * head_width)
    score_scale = head_width ** -0.5
    head_rows = queries.astype(jnp.float32).reshape(row_count, kv_heads, group_size, head_width)
    key_rows = cache[:, 0].astype(jnp.float32).reshape(row_count, kv_heads, context, head_width)
    value_rows = cache[:, 1].astype(jnp.float32).reshape(row_count, kv_heads, context, head_width)
    scores = jnp.einsum("nkgd,nkpd->nkgp", head_rows, key_rows) * score_scale
    inside = (jnp.arange(context)[None, :] < count[:, None])[:, None, None, :]
    top_score = jnp.max(jnp.where(inside, scores, -1e30), axis=-1)
    if fresh is not None:
        fresh_key = fresh[:, 0].astype(jnp.float32).reshape(row_count, kv_heads, head_width)
        fresh_score = jnp.einsum("nkgd,nkd->nkg", head_rows, fresh_key) * score_scale
        top_score = jnp.maximum(top_score, fresh_score)
    weights = jnp.where(inside, jnp.exp(scores - top_score[..., None]), 0.0).astype(jnp.bfloat16)
    weight_sum = jnp.sum(weights.astype(jnp.float32), axis=-1)
    mixed_sum = jnp.einsum("nkgp,nkpd->nkgd", weights.astype(jnp.float32), value_rows)
    if fresh is not None:
        fresh_weight = lax.optimization_barrier(jnp.exp(fresh_score - top_score).astype(jnp.bfloat16)).astype(jnp.float32)
        weight_sum = weight_sum + fresh_weight
        fresh_value = fresh[:, 1].astype(jnp.float32).reshape(row_count, kv_heads, 1, head_width)
        mixed_sum = mixed_sum + fresh_weight[..., None] * fresh_value
    return (top_score.reshape(row_count, -1), weight_sum.reshape(row_count, -1),
            mixed_sum.reshape(row_count, -1, head_width))


def blocked(queries, cache, count, fresh, blocks):
    def shape_in(array):
        return array.reshape((blocks, array.shape[0] // blocks) + array.shape[1:])

    def flat_out(array):
        return array.reshape((array.shape[0] * array.shape[1],) + array.shape[2:])

    if fresh is None:
        parts = lax.map(lambda items: attend(items[0], items[1], items[2], None),
                        (shape_in(queries), shape_in(cache), shape_in(count)))
    else:
        parts = lax.map(lambda items: attend(items[0], items[1], items[2], items[3]),
                        (shape_in(queries), shape_in(cache), shape_in(count), shape_in(fresh)))
    return flat_out(parts[0]), flat_out(parts[1]), flat_out(parts[2])


def reference(queries, new_kv, home_cache, help_cache, lengths, split_at, helper_req, out_weight):
    blocks = REQUESTS // REQ_G
    home_m, home_l, home_u = blocked(queries, home_cache, split_at, new_kv, blocks)
    help_count = (lengths[helper_req] - split_at[helper_req]).astype(jnp.int32)
    help_m, help_l, help_u = blocked(queries[helper_req], help_cache, help_count, None, blocks)
    far_m = jnp.full(home_m.shape, -1e30, jnp.float32).astype(home_m.dtype).at[helper_req].set(help_m)
    far_l = jnp.zeros_like(home_l).at[helper_req].set(help_l)
    far_u = jnp.zeros_like(home_u).at[helper_req].set(help_u)
    top_score = jnp.maximum(home_m, far_m)
    home_e = jnp.exp(home_m - top_score)
    far_e = jnp.exp(far_m - top_score)
    numerator = home_u * home_e[..., None] + far_u * far_e[..., None]
    denominator = home_l * home_e + far_l * far_e
    mix = (numerator / denominator[..., None]).reshape(REQUESTS, H * HD).astype(jnp.bfloat16)
    return jnp.dot(mix, out_weight, preferred_element_type=jnp.float32).astype(jnp.bfloat16)
```

```python
import functools

import jax
import jax.numpy as jnp
from jax import lax
from jax.experimental import pallas as pl
from jax.experimental.pallas import tpu as pltpu
from jax.sharding import PartitionSpec as P

MESH = pl.DeviceIdType.MESH
LONG_AT = 1024


def attend(queries, cache, count, fresh):
    row_count = queries.shape[0]
    kv_heads = cache.shape[2]
    head_width = cache.shape[4] // 2
    context = cache.shape[3] * 2
    group_size = queries.shape[1] // (kv_heads * head_width)
    score_scale = head_width ** (-0.5)
    head_rows = queries.reshape(row_count, kv_heads, group_size, head_width)
    key_rows = cache[:, 0].reshape(row_count, kv_heads, context, head_width)
    value_rows = cache[:, 1].reshape(row_count, kv_heads, context, head_width)
    scores = (
        jnp.einsum("nkgd,nkpd->nkgp", head_rows, key_rows, preferred_element_type=jnp.float32)
        * score_scale
    )
    inside = (jnp.arange(context)[None, :] < count[:, None])[:, None, None, :]
    top_score = jnp.max(jnp.where(inside, scores, -1e30), axis=-1)
    if fresh is not None:
        fresh_key = fresh[:, 0].reshape(row_count, kv_heads, head_width)
        fresh_score = (
            jnp.einsum("nkgd,nkd->nkg", head_rows, fresh_key, preferred_element_type=jnp.float32)
            * score_scale
        )
        top_score = jnp.maximum(top_score, fresh_score)
    weights = jnp.where(inside, jnp.exp(scores - top_score[..., None]), 0.0).astype(jnp.bfloat16)
    weight_sum = jnp.sum(weights.astype(jnp.float32), axis=-1)
    mixed_sum = jnp.einsum(
        "nkgp,nkpd->nkgd", weights, value_rows, preferred_element_type=jnp.float32
    )
    if fresh is not None:
        fresh_weight = lax.optimization_barrier(
            jnp.exp(fresh_score - top_score).astype(jnp.bfloat16)
        ).astype(jnp.float32)
        weight_sum = weight_sum + fresh_weight
        fresh_value = fresh[:, 1].reshape(row_count, kv_heads, 1, head_width).astype(jnp.float32)
        mixed_sum = mixed_sum + fresh_weight[..., None] * fresh_value
    return (
        top_score.reshape(row_count, -1),
        weight_sum.reshape(row_count, -1),
        mixed_sum.reshape(row_count, -1, head_width),
    )


def gather_kernel(n, x_ref, out_ref, held, send_sem, recv_sem):
    me = lax.axis_index("grp")
    col = lax.axis_index("tp")

    barrier = pltpu.get_barrier_semaphore()

    def greet(k, carry):
        peer = lax.rem(me + k, n)
        pl.semaphore_signal(barrier, inc=1, device_id=(peer, col), device_id_type=MESH)
        return carry

    lax.fori_loop(1, n, greet, 0)
    pl.semaphore_wait(barrier, n - 1)

    def copy_to(k):
        peer = lax.rem(me + k, n)
        return pltpu.make_async_remote_copy(
            src_ref=x_ref,
            dst_ref=held.at[me],
            send_sem=send_sem.at[k],
            recv_sem=recv_sem.at[k],
            device_id=(peer, col),
            device_id_type=MESH,
        )

    def copy_from(k):
        source = lax.rem(me + n - k, n)
        return pltpu.make_async_remote_copy(
            src_ref=x_ref,
            dst_ref=held.at[source],
            send_sem=send_sem.at[k],
            recv_sem=recv_sem.at[k],
            device_id=(source, col),
            device_id_type=MESH,
        )

    def start(k, carry):
        copy_to(k).start()
        return carry

    lax.fori_loop(1, n, start, 0)

    def finish(k, carry):
        copy_to(k).wait_send()
        copy_from(k).wait_recv()
        return carry

    lax.fori_loop(1, n, finish, 0)
    held[me] = x_ref[...]
    out_ref[...] = held[...]


def gather_grp(x, n, cid):
    return pl.pallas_call(
        functools.partial(gather_kernel, n),
        out_shape=jax.ShapeDtypeStruct((n,) + x.shape, x.dtype),
        in_specs=[pl.BlockSpec(memory_space=pltpu.VMEM)],
        out_specs=pl.BlockSpec(memory_space=pltpu.VMEM),
        scratch_shapes=[
            pltpu.VMEM((n,) + x.shape, x.dtype),
            pltpu.SemaphoreType.DMA((n,)),
            pltpu.SemaphoreType.DMA((n,)),
        ],
        compiler_params=pltpu.CompilerParams(collective_id=cid, has_side_effects=True),
    )(x)


def scatter_kernel(n, x_ref, out_ref, held, send_sem, recv_sem):
    me = lax.axis_index("tp")
    row = lax.axis_index("grp")
    width = out_ref.shape[1]

    barrier = pltpu.get_barrier_semaphore()
    for k in range(1, n):
        peer = lax.rem(me + k, n)
        pl.semaphore_signal(barrier, inc=1, device_id=(row, peer), device_id_type=MESH)
    pl.semaphore_wait(barrier, n - 1)

    copies = []
    for k in range(1, n):
        peer = lax.rem(me + k, n)
        cols = pl.ds(pl.multiple_of(peer * width, width), width)
        copy = pltpu.make_async_remote_copy(
            src_ref=x_ref.at[:, cols],
            dst_ref=held.at[k],
            send_sem=send_sem.at[k],
            recv_sem=recv_sem.at[k],
            device_id=(row, peer),
            device_id_type=MESH,
        )
        copy.start()
        copies.append(copy)
    own = pl.ds(pl.multiple_of(me * width, width), width)
    total = x_ref[:, own]
    for copy in copies:
        copy.wait_send()
        copy.wait_recv()
    for k in range(1, n):
        total = total + held[k]
    out_ref[...] = total.astype(out_ref.dtype)


def scatter_tp(x, n, cid):
    rows, cols = x.shape
    width = cols // n
    return pl.pallas_call(
        functools.partial(scatter_kernel, n),
        out_shape=jax.ShapeDtypeStruct((rows, width), jnp.bfloat16),
        in_specs=[pl.BlockSpec(memory_space=pltpu.VMEM)],
        out_specs=pl.BlockSpec(memory_space=pltpu.VMEM),
        scratch_shapes=[
            pltpu.VMEM((n, rows, width), jnp.float32),
            pltpu.SemaphoreType.DMA((n,)),
            pltpu.SemaphoreType.DMA((n,)),
        ],
        compiler_params=pltpu.CompilerParams(collective_id=cid, has_side_effects=True),
    )(x)


def per_device(queries, new_kv, home_cache, help_cache, lengths, split_at, helper_req, out_weight):
    n_grp = lax.axis_size("grp")
    n_tp = lax.axis_size("tp")
    row_count, width = queries.shape
    slots = help_cache.shape[0]
    heads = width // 64
    head_width = 64

    is_long = lengths > LONG_AT
    order = jnp.argsort(jnp.where(is_long, 0, 1), stable=True)[:slots]
    long_count = (lengths - split_at)[order]
    hi = (long_count // 32).astype(jnp.bfloat16)
    lo = (long_count % 32).astype(jnp.bfloat16)
    pad = 128
    extra = jnp.zeros((slots, pad), jnp.bfloat16).at[:, 0].set(hi).at[:, 1].set(lo)
    sent = jnp.concatenate([queries[order], extra], axis=1)

    partner = helper_req[0] // row_count
    got = gather_grp(sent, n_grp, 0)
    mine = lax.dynamic_index_in_dim(got, partner, axis=0, keepdims=False)
    help_queries = mine[:, :width]
    help_count = (
        mine[:, width].astype(jnp.int32) * 32 + mine[:, width + 1].astype(jnp.int32)
    )

    home_m, home_l, home_u = attend(queries, home_cache, split_at, new_kv)
    help_m, help_l, help_u = attend(help_queries, help_cache, help_count, None)

    back = jnp.concatenate(
        [
            help_u.reshape(slots, heads * head_width),
            help_m,
            help_l,
            jnp.zeros((slots, pad - 2 * heads), jnp.float32),
        ],
        axis=1,
    )
    got_back = gather_grp(back, n_grp, 1)
    theirs = lax.dynamic_index_in_dim(got_back, partner, axis=0, keepdims=False)
    t_u = theirs[:, : heads * head_width].reshape(slots, heads, head_width)
    t_m = theirs[:, heads * head_width : heads * head_width + heads]
    t_l = theirs[:, heads * head_width + heads : heads * head_width + 2 * heads]

    own_sel = (jnp.arange(row_count)[:, None] == order[None, :]) & is_long[order][None, :]
    far_m = jnp.max(jnp.where(own_sel[:, :, None], t_m[None], -1e30), axis=1)
    far_l = jnp.sum(jnp.where(own_sel[:, :, None], t_l[None], 0.0), axis=1)
    far_u = jnp.sum(jnp.where(own_sel[:, :, None, None], t_u[None], 0.0), axis=1)
    top_score = jnp.maximum(home_m, far_m)
    home_e = jnp.exp(home_m - top_score)
    far_e = jnp.exp(far_m - top_score)
    numerator = home_u * home_e[..., None] + far_u * far_e[..., None]
    denominator = home_l * home_e + far_l * far_e
    heads_out = numerator / denominator[..., None]
    mix = heads_out.reshape(row_count, -1).astype(jnp.bfloat16)
    partial_out = jnp.dot(mix, out_weight, preferred_element_type=jnp.float32)
    return scatter_tp(partial_out, n_tp, 2)


def solution(mesh):
    return jax.shard_map(
        per_device,
        mesh=mesh,
        in_specs=(
            P("grp", "tp"),
            P("grp", None, "tp"),
            P("grp", None, "tp", None, None),
            P("grp", None, "tp", None, None),
            P("grp"),
            P("grp"),
            P("grp"),
            P("tp", None),
        ),
        out_specs=P("grp", "tp"),
        check_vma=False,
    )
```

```python
import functools

import jax
import jax.numpy as jnp
from jax import lax
from jax.experimental import pallas as pl
from jax.experimental.pallas import tpu as pltpu
from jax.sharding import PartitionSpec as P

MESH = pl.DeviceIdType.MESH
LONG_AT = 1024


def attend(queries, cache, count, fresh):
    row_count = queries.shape[0]
    kv_heads = cache.shape[2]
    head_width = cache.shape[4] // 2
    context = cache.shape[3] * 2
    group_size = queries.shape[1] // (kv_heads * head_width)
    score_scale = head_width ** (-0.5)
    head_rows = queries.reshape(row_count, kv_heads, group_size, head_width)
    key_rows = cache[:, 0].reshape(row_count, kv_heads, context, head_width)
    value_rows = cache[:, 1].reshape(row_count, kv_heads, context, head_width)
    scores = (
        jnp.einsum("nkgd,nkpd->nkgp", head_rows, key_rows, preferred_element_type=jnp.float32)
        * score_scale
    )
    inside = (jnp.arange(context)[None, :] < count[:, None])[:, None, None, :]
    top_score = jnp.max(jnp.where(inside, scores, -1e30), axis=-1)
    if fresh is not None:
        fresh_key = fresh[:, 0].reshape(row_count, kv_heads, head_width)
        fresh_score = (
            jnp.einsum("nkgd,nkd->nkg", head_rows, fresh_key, preferred_element_type=jnp.float32)
            * score_scale
        )
        top_score = jnp.maximum(top_score, fresh_score)
    weights = jnp.where(inside, jnp.exp(scores - top_score[..., None]), 0.0).astype(jnp.bfloat16)
    weight_sum = jnp.sum(weights.astype(jnp.float32), axis=-1)
    mixed_sum = jnp.einsum(
        "nkgp,nkpd->nkgd", weights, value_rows, preferred_element_type=jnp.float32
    )
    if fresh is not None:
        fresh_weight = lax.optimization_barrier(
            jnp.exp(fresh_score - top_score).astype(jnp.bfloat16)
        ).astype(jnp.float32)
        weight_sum = weight_sum + fresh_weight
        fresh_value = fresh[:, 1].reshape(row_count, kv_heads, 1, head_width).astype(jnp.float32)
        mixed_sum = mixed_sum + fresh_weight[..., None] * fresh_value
    return (
        top_score.reshape(row_count, -1),
        weight_sum.reshape(row_count, -1),
        mixed_sum.reshape(row_count, -1, head_width),
    )


def gather_kernel(ny, nz, x_ref, out_ref, held, copy_sem, send1, recv1, send2, recv2):
    me = lax.axis_index("grp")
    col = lax.axis_index("tp")
    my_y = me // nz
    my_z = me % nz

    barrier = pltpu.get_barrier_semaphore()
    for k in range(1, nz):
        peer = my_y * nz + lax.rem(my_z + k, nz)
        pl.semaphore_signal(barrier, inc=1, device_id=(peer, col), device_id_type=MESH)
    for k in range(1, ny):
        peer = lax.rem(my_y + k, ny) * nz + my_z
        pl.semaphore_signal(barrier, inc=1, device_id=(peer, col), device_id_type=MESH)
    pl.semaphore_wait(barrier, (nz - 1) + (ny - 1))

    local = pltpu.make_async_copy(x_ref, held.at[my_y, my_z], copy_sem)
    local.start()
    first = []
    for k in range(1, nz):
        peer_z = lax.rem(my_z + k, nz)
        copy = pltpu.make_async_remote_copy(
            src_ref=x_ref,
            dst_ref=held.at[my_y, my_z],
            send_sem=send1.at[k],
            recv_sem=recv1.at[k],
            device_id=(my_y * nz + peer_z, col),
            device_id_type=MESH,
        )
        copy.start()
        first.append(copy)
    for k in range(1, nz):
        first[k - 1].wait_send()
        src_z = lax.rem(my_z + nz - k, nz)
        pltpu.make_async_remote_copy(
            src_ref=x_ref,
            dst_ref=held.at[my_y, src_z],
            send_sem=send1.at[k],
            recv_sem=recv1.at[k],
            device_id=(my_y * nz + src_z, col),
            device_id_type=MESH,
        ).wait_recv()
    local.wait()

    second = []
    for k in range(1, ny):
        peer_y = lax.rem(my_y + k, ny)
        copy = pltpu.make_async_remote_copy(
            src_ref=held.at[my_y],
            dst_ref=held.at[my_y],
            send_sem=send2.at[k],
            recv_sem=recv2.at[k],
            device_id=(peer_y * nz + my_z, col),
            device_id_type=MESH,
        )
        copy.start()
        second.append(copy)
    for k in range(1, ny):
        second[k - 1].wait_send()
        src_y = lax.rem(my_y + ny - k, ny)
        pltpu.make_async_remote_copy(
            src_ref=held.at[src_y],
            dst_ref=held.at[src_y],
            send_sem=send2.at[k],
            recv_sem=recv2.at[k],
            device_id=(src_y * nz + my_z, col),
            device_id_type=MESH,
        ).wait_recv()
    out_ref[...] = held[...]


def gather_grp(x, ny, nz, cid):
    out = pl.pallas_call(
        functools.partial(gather_kernel, ny, nz),
        out_shape=jax.ShapeDtypeStruct((ny, nz) + x.shape, x.dtype),
        in_specs=[pl.BlockSpec(memory_space=pltpu.VMEM)],
        out_specs=pl.BlockSpec(memory_space=pltpu.VMEM),
        scratch_shapes=[
            pltpu.VMEM((ny, nz) + x.shape, x.dtype),
            pltpu.SemaphoreType.DMA(()),
            pltpu.SemaphoreType.DMA((nz,)),
            pltpu.SemaphoreType.DMA((nz,)),
            pltpu.SemaphoreType.DMA((ny,)),
            pltpu.SemaphoreType.DMA((ny,)),
        ],
        compiler_params=pltpu.CompilerParams(collective_id=cid, has_side_effects=True),
    )(x)
    return out.reshape((ny * nz,) + x.shape)


def scatter_kernel(n, x_ref, out_ref, held, send_sem, recv_sem):
    me = lax.axis_index("tp")
    row = lax.axis_index("grp")
    width = out_ref.shape[1]

    barrier = pltpu.get_barrier_semaphore()
    for k in range(1, n):
        peer = lax.rem(me + k, n)
        pl.semaphore_signal(barrier, inc=1, device_id=(row, peer), device_id_type=MESH)
    pl.semaphore_wait(barrier, n - 1)

    copies = []
    for k in range(1, n):
        peer = lax.rem(me + k, n)
        cols = pl.ds(pl.multiple_of(peer * width, width), width)
        copy = pltpu.make_async_remote_copy(
            src_ref=x_ref.at[:, cols],
            dst_ref=held.at[k],
            send_sem=send_sem.at[k],
            recv_sem=recv_sem.at[k],
            device_id=(row, peer),
            device_id_type=MESH,
        )
        copy.start()
        copies.append(copy)
    own = pl.ds(pl.multiple_of(me * width, width), width)
    total = x_ref[:, own]
    for copy in copies:
        copy.wait_send()
        copy.wait_recv()
    for k in range(1, n):
        total = total + held[k]
    out_ref[...] = total.astype(out_ref.dtype)


def scatter_tp(x, n, cid):
    rows, cols = x.shape
    width = cols // n
    return pl.pallas_call(
        functools.partial(scatter_kernel, n),
        out_shape=jax.ShapeDtypeStruct((rows, width), jnp.bfloat16),
        in_specs=[pl.BlockSpec(memory_space=pltpu.VMEM)],
        out_specs=pl.BlockSpec(memory_space=pltpu.VMEM),
        scratch_shapes=[
            pltpu.VMEM((n, rows, width), jnp.float32),
            pltpu.SemaphoreType.DMA((n,)),
            pltpu.SemaphoreType.DMA((n,)),
        ],
        compiler_params=pltpu.CompilerParams(collective_id=cid, has_side_effects=True),
    )(x)


def per_device(ny, nz, queries, new_kv, home_cache, help_cache, lengths, split_at, helper_req, out_weight):
    n_grp = lax.axis_size("grp")
    n_tp = lax.axis_size("tp")
    row_count, width = queries.shape
    slots = help_cache.shape[0]
    heads = width // 64
    head_width = 64

    is_long = lengths > LONG_AT
    order = jnp.argsort(jnp.where(is_long, 0, 1), stable=True)[:slots]
    long_count = (lengths - split_at)[order]
    hi = (long_count // 32).astype(jnp.bfloat16)
    lo = (long_count % 32).astype(jnp.bfloat16)
    pad = 128
    extra = jnp.zeros((slots, pad), jnp.bfloat16).at[:, 0].set(hi).at[:, 1].set(lo)
    sent = jnp.concatenate([queries[order], extra], axis=1)

    partner = helper_req[0] // row_count
    got = gather_grp(sent, ny, nz, 0)
    mine = lax.dynamic_index_in_dim(got, partner, axis=0, keepdims=False)
    help_queries = mine[:, :width]
    help_count = (
        mine[:, width].astype(jnp.int32) * 32 + mine[:, width + 1].astype(jnp.int32)
    )

    home_m, home_l, home_u = attend(queries, home_cache, split_at, new_kv)
    help_m, help_l, help_u = attend(help_queries, help_cache, help_count, None)

    back = jnp.concatenate(
        [
            help_u.reshape(slots, heads * head_width),
            help_m,
            help_l,
            jnp.zeros((slots, pad - 2 * heads), jnp.float32),
        ],
        axis=1,
    )
    got_back = gather_grp(back, ny, nz, 1)
    theirs = lax.dynamic_index_in_dim(got_back, partner, axis=0, keepdims=False)
    t_u = theirs[:, : heads * head_width].reshape(slots, heads, head_width)
    t_m = theirs[:, heads * head_width : heads * head_width + heads]
    t_l = theirs[:, heads * head_width + heads : heads * head_width + 2 * heads]

    own_sel = (jnp.arange(row_count)[:, None] == order[None, :]) & is_long[order][None, :]
    far_m = jnp.max(jnp.where(own_sel[:, :, None], t_m[None], -1e30), axis=1)
    far_l = jnp.sum(jnp.where(own_sel[:, :, None], t_l[None], 0.0), axis=1)
    far_u = jnp.sum(jnp.where(own_sel[:, :, None, None], t_u[None], 0.0), axis=1)
    top_score = jnp.maximum(home_m, far_m)
    home_e = jnp.exp(home_m - top_score)
    far_e = jnp.exp(far_m - top_score)
    numerator = home_u * home_e[..., None] + far_u * far_e[..., None]
    denominator = home_l * home_e + far_l * far_e
    heads_out = numerator / denominator[..., None]
    mix = heads_out.reshape(row_count, -1).astype(jnp.bfloat16)
    partial_out = jnp.dot(mix, out_weight, preferred_element_type=jnp.float32)
    return scatter_tp(partial_out, n_tp, 2)


def grp_rows(mesh):
    column = list(mesh.devices[:, 0])
    n = len(column)
    coords = [getattr(d, "coords", None) for d in column]
    if coords[0] is not None:
        nz = 1
        while nz < n and coords[nz][1] == coords[0][1]:
            nz += 1
    else:
        nz = 1
        while nz * nz < n:
            nz *= 2
    return n // nz, nz


def solution(mesh):
    ny, nz = grp_rows(mesh)
    return jax.shard_map(
        functools.partial(per_device, ny, nz),
        mesh=mesh,
        in_specs=(
            P("grp", "tp"),
            P("grp", None, "tp"),
            P("grp", None, "tp", None, None),
            P("grp", None, "tp", None, None),
            P("grp"),
            P("grp"),
            P("grp"),
            P("tp", None),
        ),
        out_specs=P("grp", "tp"),
        check_vma=False,
    )
```

```python
import functools

import jax
import jax.numpy as jnp
from jax import lax
from jax.experimental import pallas as pl
from jax.experimental.pallas import tpu as pltpu
from jax.sharding import PartitionSpec as P

MESH = pl.DeviceIdType.MESH
LONG_AT = 1024


def attend(queries, cache, count, fresh):
    row_count = queries.shape[0]
    kv_heads = cache.shape[2]
    head_width = cache.shape[4] // 2
    half = cache.shape[3]
    group_size = queries.shape[1] // (kv_heads * head_width)
    score_scale = head_width ** (-0.5)
    head_rows = queries.reshape(row_count, kv_heads, group_size, head_width)
    blank = jnp.zeros_like(head_rows)
    wide_rows = jnp.stack(
        [
            jnp.concatenate([head_rows, blank], axis=-1),
            jnp.concatenate([blank, head_rows], axis=-1),
        ],
        axis=3,
    )
    key_rows = cache[:, 0]
    value_rows = cache[:, 1]
    scores = (
        jnp.einsum("nkgjc,nkpc->nkgjp", wide_rows, key_rows, preferred_element_type=jnp.float32)
        * score_scale
    )
    position = 2 * jnp.arange(half)[None, :] + jnp.arange(2)[:, None]
    inside = (position[None] < count[:, None, None])[:, None, None]
    top_score = jnp.max(jnp.where(inside, scores, -1e30), axis=(-2, -1))
    if fresh is not None:
        fresh_key = fresh[:, 0].reshape(row_count, kv_heads, head_width)
        fresh_score = (
            jnp.einsum("nkgd,nkd->nkg", head_rows, fresh_key, preferred_element_type=jnp.float32)
            * score_scale
        )
        top_score = jnp.maximum(top_score, fresh_score)
    weights = jnp.where(
        inside, jnp.exp(scores - top_score[..., None, None]), 0.0
    ).astype(jnp.bfloat16)
    weight_sum = jnp.sum(weights.astype(jnp.float32), axis=(-2, -1))
    both = jnp.einsum(
        "nkgjp,nkpc->nkgjc", weights, value_rows, preferred_element_type=jnp.float32
    )
    mixed_sum = both[..., 0, :head_width] + both[..., 1, head_width:]
    if fresh is not None:
        fresh_weight = lax.optimization_barrier(
            jnp.exp(fresh_score - top_score).astype(jnp.bfloat16)
        ).astype(jnp.float32)
        weight_sum = weight_sum + fresh_weight
        fresh_value = fresh[:, 1].reshape(row_count, kv_heads, 1, head_width).astype(jnp.float32)
        mixed_sum = mixed_sum + fresh_weight[..., None] * fresh_value
    return (
        top_score.reshape(row_count, -1),
        weight_sum.reshape(row_count, -1),
        mixed_sum.reshape(row_count, -1, head_width),
    )


def gather_kernel(ny, nz, x_ref, out_ref, held, copy_sem, send1, recv1, send2, recv2):
    me = lax.axis_index("grp")
    col = lax.axis_index("tp")
    my_y = me // nz
    my_z = me % nz

    barrier = pltpu.get_barrier_semaphore()
    for k in range(1, nz):
        peer = my_y * nz + lax.rem(my_z + k, nz)
        pl.semaphore_signal(barrier, inc=1, device_id=(peer, col), device_id_type=MESH)
    for k in range(1, ny):
        peer = lax.rem(my_y + k, ny) * nz + my_z
        pl.semaphore_signal(barrier, inc=1, device_id=(peer, col), device_id_type=MESH)
    pl.semaphore_wait(barrier, (nz - 1) + (ny - 1))

    local = pltpu.make_async_copy(x_ref, held.at[my_y, my_z], copy_sem)
    local.start()
    first = []
    for k in range(1, nz):
        peer_z = lax.rem(my_z + k, nz)
        copy = pltpu.make_async_remote_copy(
            src_ref=x_ref,
            dst_ref=held.at[my_y, my_z],
            send_sem=send1.at[k],
            recv_sem=recv1.at[k],
            device_id=(my_y * nz + peer_z, col),
            device_id_type=MESH,
        )
        copy.start()
        first.append(copy)
    for k in range(1, nz):
        first[k - 1].wait_send()
        src_z = lax.rem(my_z + nz - k, nz)
        pltpu.make_async_remote_copy(
            src_ref=x_ref,
            dst_ref=held.at[my_y, src_z],
            send_sem=send1.at[k],
            recv_sem=recv1.at[k],
            device_id=(my_y * nz + src_z, col),
            device_id_type=MESH,
        ).wait_recv()
    local.wait()

    second = []
    for k in range(1, ny):
        peer_y = lax.rem(my_y + k, ny)
        copy = pltpu.make_async_remote_copy(
            src_ref=held.at[my_y],
            dst_ref=held.at[my_y],
            send_sem=send2.at[k],
            recv_sem=recv2.at[k],
            device_id=(peer_y * nz + my_z, col),
            device_id_type=MESH,
        )
        copy.start()
        second.append(copy)
    for k in range(1, ny):
        second[k - 1].wait_send()
        src_y = lax.rem(my_y + ny - k, ny)
        pltpu.make_async_remote_copy(
            src_ref=held.at[src_y],
            dst_ref=held.at[src_y],
            send_sem=send2.at[k],
            recv_sem=recv2.at[k],
            device_id=(src_y * nz + my_z, col),
            device_id_type=MESH,
        ).wait_recv()
    out_ref[...] = held[...]


def gather_grp(x, ny, nz, cid):
    out = pl.pallas_call(
        functools.partial(gather_kernel, ny, nz),
        out_shape=jax.ShapeDtypeStruct((ny, nz) + x.shape, x.dtype),
        in_specs=[pl.BlockSpec(memory_space=pltpu.VMEM)],
        out_specs=pl.BlockSpec(memory_space=pltpu.VMEM),
        scratch_shapes=[
            pltpu.VMEM((ny, nz) + x.shape, x.dtype),
            pltpu.SemaphoreType.DMA(()),
            pltpu.SemaphoreType.DMA((nz,)),
            pltpu.SemaphoreType.DMA((nz,)),
            pltpu.SemaphoreType.DMA((ny,)),
            pltpu.SemaphoreType.DMA((ny,)),
        ],
        compiler_params=pltpu.CompilerParams(collective_id=cid, has_side_effects=True),
    )(x)
    return out.reshape((ny * nz,) + x.shape)


def scatter_kernel(n, x_ref, out_ref, held, send_sem, recv_sem):
    me = lax.axis_index("tp")
    row = lax.axis_index("grp")
    width = out_ref.shape[1]

    barrier = pltpu.get_barrier_semaphore()
    for k in range(1, n):
        peer = lax.rem(me + k, n)
        pl.semaphore_signal(barrier, inc=1, device_id=(row, peer), device_id_type=MESH)
    pl.semaphore_wait(barrier, n - 1)

    copies = []
    for k in range(1, n):
        peer = lax.rem(me + k, n)
        cols = pl.ds(pl.multiple_of(peer * width, width), width)
        copy = pltpu.make_async_remote_copy(
            src_ref=x_ref.at[:, cols],
            dst_ref=held.at[k],
            send_sem=send_sem.at[k],
            recv_sem=recv_sem.at[k],
            device_id=(row, peer),
            device_id_type=MESH,
        )
        copy.start()
        copies.append(copy)
    own = pl.ds(pl.multiple_of(me * width, width), width)
    total = x_ref[:, own]
    for copy in copies:
        copy.wait_send()
        copy.wait_recv()
    for k in range(1, n):
        total = total + held[k]
    out_ref[...] = total.astype(out_ref.dtype)


def scatter_tp(x, n, cid):
    rows, cols = x.shape
    width = cols // n
    return pl.pallas_call(
        functools.partial(scatter_kernel, n),
        out_shape=jax.ShapeDtypeStruct((rows, width), jnp.bfloat16),
        in_specs=[pl.BlockSpec(memory_space=pltpu.VMEM)],
        out_specs=pl.BlockSpec(memory_space=pltpu.VMEM),
        scratch_shapes=[
            pltpu.VMEM((n, rows, width), jnp.float32),
            pltpu.SemaphoreType.DMA((n,)),
            pltpu.SemaphoreType.DMA((n,)),
        ],
        compiler_params=pltpu.CompilerParams(collective_id=cid, has_side_effects=True),
    )(x)


def per_device(ny, nz, queries, new_kv, home_cache, help_cache, lengths, split_at, helper_req, out_weight):
    n_grp = lax.axis_size("grp")
    n_tp = lax.axis_size("tp")
    row_count, width = queries.shape
    slots = help_cache.shape[0]
    heads = width // 64
    head_width = 64

    is_long = lengths > LONG_AT
    order = jnp.argsort(jnp.where(is_long, 0, 1), stable=True)[:slots]
    long_count = (lengths - split_at)[order]
    hi = (long_count // 32).astype(jnp.bfloat16)
    lo = (long_count % 32).astype(jnp.bfloat16)
    pad = 128
    extra = jnp.zeros((slots, pad), jnp.bfloat16).at[:, 0].set(hi).at[:, 1].set(lo)
    sent = jnp.concatenate([queries[order], extra], axis=1)

    partner = helper_req[0] // row_count
    got = gather_grp(sent, ny, nz, 0)
    mine = lax.dynamic_index_in_dim(got, partner, axis=0, keepdims=False)
    help_queries = mine[:, :width]
    help_count = (
        mine[:, width].astype(jnp.int32) * 32 + mine[:, width + 1].astype(jnp.int32)
    )

    home_m, home_l, home_u = attend(queries, home_cache, split_at, new_kv)
    help_m, help_l, help_u = attend(help_queries, help_cache, help_count, None)

    back = jnp.concatenate(
        [
            help_u.reshape(slots, heads * head_width),
            help_m,
            help_l,
            jnp.zeros((slots, pad - 2 * heads), jnp.float32),
        ],
        axis=1,
    )
    got_back = gather_grp(back, ny, nz, 1)
    theirs = lax.dynamic_index_in_dim(got_back, partner, axis=0, keepdims=False)
    t_u = theirs[:, : heads * head_width].reshape(slots, heads, head_width)
    t_m = theirs[:, heads * head_width : heads * head_width + heads]
    t_l = theirs[:, heads * head_width + heads : heads * head_width + 2 * heads]

    own_sel = (jnp.arange(row_count)[:, None] == order[None, :]) & is_long[order][None, :]
    far_m = jnp.max(jnp.where(own_sel[:, :, None], t_m[None], -1e30), axis=1)
    far_l = jnp.sum(jnp.where(own_sel[:, :, None], t_l[None], 0.0), axis=1)
    far_u = jnp.sum(jnp.where(own_sel[:, :, None, None], t_u[None], 0.0), axis=1)
    top_score = jnp.maximum(home_m, far_m)
    home_e = jnp.exp(home_m - top_score)
    far_e = jnp.exp(far_m - top_score)
    numerator = home_u * home_e[..., None] + far_u * far_e[..., None]
    denominator = home_l * home_e + far_l * far_e
    heads_out = numerator / denominator[..., None]
    mix = heads_out.reshape(row_count, -1).astype(jnp.bfloat16)
    partial_out = jnp.dot(mix, out_weight, preferred_element_type=jnp.float32)
    return scatter_tp(partial_out, n_tp, 2)


def grp_rows(mesh):
    column = list(mesh.devices[:, 0])
    n = len(column)
    coords = [getattr(d, "coords", None) for d in column]
    if coords[0] is not None:
        nz = 1
        while nz < n and coords[nz][1] == coords[0][1]:
            nz += 1
    else:
        nz = 1
        while nz * nz < n:
            nz *= 2
    return n // nz, nz


def solution(mesh):
    ny, nz = grp_rows(mesh)
    return jax.shard_map(
        functools.partial(per_device, ny, nz),
        mesh=mesh,
        in_specs=(
            P("grp", "tp"),
            P("grp", None, "tp"),
            P("grp", None, "tp", None, None),
            P("grp", None, "tp", None, None),
            P("grp"),
            P("grp"),
            P("grp"),
            P("tp", None),
        ),
        out_specs=P("grp", "tp"),
        check_vma=False,
    )
```

```python
import functools

import jax
import jax.numpy as jnp
from jax import lax
from jax.experimental import pallas as pl
from jax.experimental.pallas import tpu as pltpu
from jax.sharding import PartitionSpec as P

MESH = pl.DeviceIdType.MESH
LONG_AT = 1024


def attend(queries, cache, count, fresh):
    row_count = queries.shape[0]
    kv_heads = cache.shape[2]
    head_width = cache.shape[4] // 2
    half = cache.shape[3]
    group_size = queries.shape[1] // (kv_heads * head_width)
    score_scale = head_width ** (-0.5)
    head_rows = queries.reshape(row_count, kv_heads, group_size, head_width)
    blank = jnp.zeros_like(head_rows)
    wide_rows = jnp.stack(
        [
            jnp.concatenate([head_rows, blank], axis=-1),
            jnp.concatenate([blank, head_rows], axis=-1),
        ],
        axis=3,
    )
    key_rows = cache[:, 0]
    value_rows = cache[:, 1]
    scores = (
        jnp.einsum("nkgjc,nkpc->nkgjp", wide_rows, key_rows, preferred_element_type=jnp.float32)
        * score_scale
    )
    position = 2 * jnp.arange(half)[None, :] + jnp.arange(2)[:, None]
    inside = (position[None] < count[:, None, None])[:, None, None]
    top_score = jnp.max(jnp.where(inside, scores, -1e30), axis=(-2, -1))
    if fresh is not None:
        fresh_key = fresh[:, 0].reshape(row_count, kv_heads, head_width)
        fresh_score = (
            jnp.einsum("nkgd,nkd->nkg", head_rows, fresh_key, preferred_element_type=jnp.float32)
            * score_scale
        )
        top_score = jnp.maximum(top_score, fresh_score)
    weights = jnp.where(
        inside, jnp.exp(scores - top_score[..., None, None]), 0.0
    ).astype(jnp.bfloat16)
    weight_sum = jnp.sum(weights.astype(jnp.float32), axis=(-2, -1))
    both = jnp.einsum(
        "nkgjp,nkpc->nkgjc", weights, value_rows, preferred_element_type=jnp.float32
    )
    mixed_sum = both[..., 0, :head_width] + both[..., 1, head_width:]
    if fresh is not None:
        fresh_weight = lax.optimization_barrier(
            jnp.exp(fresh_score - top_score).astype(jnp.bfloat16)
        ).astype(jnp.float32)
        weight_sum = weight_sum + fresh_weight
        fresh_value = fresh[:, 1].reshape(row_count, kv_heads, 1, head_width).astype(jnp.float32)
        mixed_sum = mixed_sum + fresh_weight[..., None] * fresh_value
    return (
        top_score.reshape(row_count, -1),
        weight_sum.reshape(row_count, -1),
        mixed_sum.reshape(row_count, -1, head_width),
    )


def gather_kernel(ny, nz, x_ref, out_ref, held, copy_sem, send1, recv1, send2, recv2):
    me = lax.axis_index("grp")
    col = lax.axis_index("tp")
    my_y = me // nz
    my_z = me % nz

    barrier = pltpu.get_barrier_semaphore()
    for k in range(1, nz):
        peer = my_y * nz + lax.rem(my_z + k, nz)
        pl.semaphore_signal(barrier, inc=1, device_id=(peer, col), device_id_type=MESH)
    for k in range(1, ny):
        peer = lax.rem(my_y + k, ny) * nz + my_z
        pl.semaphore_signal(barrier, inc=1, device_id=(peer, col), device_id_type=MESH)
    pl.semaphore_wait(barrier, (nz - 1) + (ny - 1))

    local = pltpu.make_async_copy(x_ref, held.at[my_y, my_z], copy_sem)
    local.start()
    first = []
    for k in range(1, nz):
        peer_z = lax.rem(my_z + k, nz)
        copy = pltpu.make_async_remote_copy(
            src_ref=x_ref,
            dst_ref=held.at[my_y, my_z],
            send_sem=send1.at[k],
            recv_sem=recv1.at[k],
            device_id=(my_y * nz + peer_z, col),
            device_id_type=MESH,
        )
        copy.start()
        first.append(copy)
    for k in range(1, nz):
        first[k - 1].wait_send()
        src_z = lax.rem(my_z + nz - k, nz)
        pltpu.make_async_remote_copy(
            src_ref=x_ref,
            dst_ref=held.at[my_y, src_z],
            send_sem=send1.at[k],
            recv_sem=recv1.at[k],
            device_id=(my_y * nz + src_z, col),
            device_id_type=MESH,
        ).wait_recv()
    local.wait()

    second = []
    for k in range(1, ny):
        peer_y = lax.rem(my_y + k, ny)
        copy = pltpu.make_async_remote_copy(
            src_ref=held.at[my_y],
            dst_ref=held.at[my_y],
            send_sem=send2.at[k],
            recv_sem=recv2.at[k],
            device_id=(peer_y * nz + my_z, col),
            device_id_type=MESH,
        )
        copy.start()
        second.append(copy)
    for k in range(1, ny):
        second[k - 1].wait_send()
        src_y = lax.rem(my_y + ny - k, ny)
        pltpu.make_async_remote_copy(
            src_ref=held.at[src_y],
            dst_ref=held.at[src_y],
            send_sem=send2.at[k],
            recv_sem=recv2.at[k],
            device_id=(src_y * nz + my_z, col),
            device_id_type=MESH,
        ).wait_recv()
    out_ref[...] = held[...]


def gather_grp(x, ny, nz, cid):
    out = pl.pallas_call(
        functools.partial(gather_kernel, ny, nz),
        out_shape=jax.ShapeDtypeStruct((ny, nz) + x.shape, x.dtype),
        in_specs=[pl.BlockSpec(memory_space=pltpu.VMEM)],
        out_specs=pl.BlockSpec(memory_space=pltpu.VMEM),
        scratch_shapes=[
            pltpu.VMEM((ny, nz) + x.shape, x.dtype),
            pltpu.SemaphoreType.DMA(()),
            pltpu.SemaphoreType.DMA((nz,)),
            pltpu.SemaphoreType.DMA((nz,)),
            pltpu.SemaphoreType.DMA((ny,)),
            pltpu.SemaphoreType.DMA((ny,)),
        ],
        compiler_params=pltpu.CompilerParams(collective_id=cid, has_side_effects=True),
    )(x)
    return out.reshape((ny * nz,) + x.shape)


def final_kernel(n, n_tp, partner_ref, back_ref, home_ref, fsel_ref, w_ref, out_ref,
                 got, part, held, send2, recv2, send3, recv3):
    me = lax.axis_index("grp")
    col = lax.axis_index("tp")
    heads, slots = back_ref.shape[0], back_ref.shape[1]
    head_width = w_ref.shape[0] // heads
    width = out_ref.shape[1]

    barrier = pltpu.get_barrier_semaphore()

    def greet(k, carry):
        peer = lax.rem(me + k, n)
        pl.semaphore_signal(barrier, inc=1, device_id=(peer, col), device_id_type=MESH)
        return carry

    lax.fori_loop(1, n, greet, 0)
    for k in range(1, n_tp):
        peer = lax.rem(col + k, n_tp)
        pl.semaphore_signal(barrier, inc=1, device_id=(me, peer), device_id_type=MESH)
    pl.semaphore_wait(barrier, (n - 1) + (n_tp - 1))

    def copy_to(k):
        peer = lax.rem(me + k, n)
        return pltpu.make_async_remote_copy(
            src_ref=back_ref,
            dst_ref=got.at[me],
            send_sem=send2.at[k],
            recv_sem=recv2.at[k],
            device_id=(peer, col),
            device_id_type=MESH,
        )

    def copy_from(k):
        source = lax.rem(me + n - k, n)
        return pltpu.make_async_remote_copy(
            src_ref=back_ref,
            dst_ref=got.at[source],
            send_sem=send2.at[k],
            recv_sem=recv2.at[k],
            device_id=(source, col),
            device_id_type=MESH,
        )

    def start(k, carry):
        copy_to(k).start()
        return carry

    lax.fori_loop(1, n, start, 0)

    def finish(k, carry):
        copy_to(k).wait_send()
        copy_from(k).wait_recv()
        return carry

    lax.fori_loop(1, n, finish, 0)

    block = got[partner_ref[0]]
    fsel = fsel_ref[...]
    has = fsel[:, 0:1]
    for k in range(1, slots):
        has = has + fsel[:, k : k + 1]
    acc = jnp.zeros(part.shape, jnp.float32)
    for g in range(heads):
        theirs = block[g]
        far = fsel[:, 0:1] * theirs[0:1, :]
        for k in range(1, slots):
            far = far + fsel[:, k : k + 1] * theirs[k : k + 1, :]
        home = home_ref[g]
        home_m = home[:, head_width : head_width + 1]
        home_l = home[:, head_width + 1 : head_width + 2]
        far_m = jnp.where(has > 0.0, far[:, head_width : head_width + 1], -1e30)
        far_l = far[:, head_width + 1 : head_width + 2]
        top = jnp.maximum(home_m, far_m)
        home_e = jnp.exp(home_m - top)
        far_e = jnp.exp(far_m - top)
        mix = (home * home_e + far * far_e) / (home_l * home_e + far_l * far_e)
        acc = acc + jnp.dot(
            mix[:, :head_width].astype(jnp.bfloat16),
            w_ref[g * head_width : (g + 1) * head_width, :],
            preferred_element_type=jnp.float32,
        )
    part[...] = acc

    sends = []
    for k in range(1, n_tp):
        peer = lax.rem(col + k, n_tp)
        cols = pl.ds(pl.multiple_of(peer * width, width), width)
        copy = pltpu.make_async_remote_copy(
            src_ref=part.at[:, cols],
            dst_ref=held.at[k],
            send_sem=send3.at[k],
            recv_sem=recv3.at[k],
            device_id=(me, peer),
            device_id_type=MESH,
        )
        copy.start()
        sends.append(copy)
    own = pl.ds(pl.multiple_of(col * width, width), width)
    total = part[:, own]
    for copy in sends:
        copy.wait_send()
        copy.wait_recv()
    for k in range(1, n_tp):
        total = total + held[k]
    out_ref[...] = total.astype(out_ref.dtype)


def finish_call(n, n_tp, partner, back, home, fsel, out_weight, cid):
    rows = home.shape[1]
    width = out_weight.shape[1] // n_tp
    vmem = pl.BlockSpec(memory_space=pltpu.VMEM)
    return pl.pallas_call(
        functools.partial(final_kernel, n, n_tp),
        out_shape=jax.ShapeDtypeStruct((rows, width), jnp.bfloat16),
        in_specs=[pl.BlockSpec(memory_space=pltpu.SMEM), vmem, vmem, vmem, vmem],
        out_specs=vmem,
        scratch_shapes=[
            pltpu.VMEM((n,) + back.shape, jnp.float32),
            pltpu.VMEM((rows, out_weight.shape[1]), jnp.float32),
            pltpu.VMEM((n_tp, rows, width), jnp.float32),
            pltpu.SemaphoreType.DMA((n,)),
            pltpu.SemaphoreType.DMA((n,)),
            pltpu.SemaphoreType.DMA((n_tp,)),
            pltpu.SemaphoreType.DMA((n_tp,)),
        ],
        compiler_params=pltpu.CompilerParams(collective_id=cid, has_side_effects=True),
    )(partner, back, home, fsel, out_weight)


def pack(m, l, u):
    rows, heads, hw = u.shape
    lanes = 128
    packed = jnp.concatenate(
        [u, m[..., None], l[..., None], jnp.zeros((rows, heads, lanes - hw - 2), jnp.float32)],
        axis=-1,
    )
    return packed.transpose(1, 0, 2)


def per_device(ny, nz, queries, new_kv, home_cache, help_cache, lengths, split_at, helper_req, out_weight):
    n_grp = lax.axis_size("grp")
    n_tp = lax.axis_size("tp")
    row_count, width = queries.shape

    count = lengths - split_at
    lanes = 128
    extra = (
        jnp.zeros((row_count, lanes), jnp.bfloat16)
        .at[:, 0]
        .set((count // 32).astype(jnp.bfloat16))
        .at[:, 1]
        .set((count % 32).astype(jnp.bfloat16))
    )
    sent = jnp.concatenate([queries, extra], axis=1)
    got = gather_grp(sent, ny, nz, 0).reshape(n_grp * row_count, width + lanes)
    picked = got[helper_req]
    help_queries = picked[:, :width]
    help_count = (
        picked[:, width].astype(jnp.int32) * 32 + picked[:, width + 1].astype(jnp.int32)
    )
    help_m, help_l, help_u = attend(help_queries, help_cache, help_count, None)
    back = pack(help_m, help_l, help_u)

    home_m, home_l, home_u = attend(queries, home_cache, split_at, new_kv)
    home = pack(home_m, home_l, home_u)

    slots = help_cache.shape[0]
    is_long = lengths > LONG_AT
    before = jnp.arange(row_count)[None, :] < jnp.arange(row_count)[:, None]
    rank = jnp.sum(jnp.where(before, is_long[None, :], False), axis=1)
    fsel = (is_long[:, None] & (rank[:, None] == jnp.arange(slots)[None, :])).astype(jnp.float32)
    partner = (helper_req[:1] // row_count).astype(jnp.int32)
    return finish_call(n_grp, n_tp, partner, back, home, fsel, out_weight, 1)


def grp_rows(mesh):
    column = list(mesh.devices[:, 0])
    n = len(column)
    coords = [getattr(d, "coords", None) for d in column]
    if coords[0] is not None:
        nz = 1
        while nz < n and coords[nz][1] == coords[0][1]:
            nz += 1
    else:
        nz = 1
        while nz * nz < n:
            nz *= 2
    return n // nz, nz


def solution(mesh):
    ny, nz = grp_rows(mesh)
    return jax.shard_map(
        functools.partial(per_device, ny, nz),
        mesh=mesh,
        in_specs=(
            P("grp", "tp"),
            P("grp", None, "tp"),
            P("grp", None, "tp", None, None),
            P("grp", None, "tp", None, None),
            P("grp"),
            P("grp"),
            P("grp"),
            P("tp", None),
        ),
        out_specs=P("grp", "tp"),
        check_vma=False,
    )
```

```python
import functools

import jax
import jax.numpy as jnp
from jax import lax
from jax.experimental import pallas as pl
from jax.experimental.pallas import tpu as pltpu
from jax.sharding import PartitionSpec as P

MESH = pl.DeviceIdType.MESH
LONG_AT = 1024


def attend(queries, cache, count, fresh):
    row_count = queries.shape[0]
    kv_heads = cache.shape[2]
    head_width = cache.shape[4] // 2
    half = cache.shape[3]
    group_size = queries.shape[1] // (kv_heads * head_width)
    score_scale = head_width ** (-0.5)
    head_rows = queries.reshape(row_count, kv_heads, group_size, head_width)
    blank = jnp.zeros_like(head_rows)
    wide_rows = jnp.stack(
        [
            jnp.concatenate([head_rows, blank], axis=-1),
            jnp.concatenate([blank, head_rows], axis=-1),
        ],
        axis=3,
    )
    key_rows = cache[:, 0]
    value_rows = cache[:, 1]
    scores = (
        jnp.einsum("nkgjc,nkpc->nkgjp", wide_rows, key_rows, preferred_element_type=jnp.float32)
        * score_scale
    )
    position = 2 * jnp.arange(half)[None, :] + jnp.arange(2)[:, None]
    inside = (position[None] < count[:, None, None])[:, None, None]
    top_score = jnp.max(jnp.where(inside, scores, -1e30), axis=(-2, -1))
    if fresh is not None:
        fresh_key = fresh[:, 0].reshape(row_count, kv_heads, head_width)
        fresh_score = (
            jnp.einsum("nkgd,nkd->nkg", head_rows, fresh_key, preferred_element_type=jnp.float32)
            * score_scale
        )
        top_score = jnp.maximum(top_score, fresh_score)
    weights = jnp.where(
        inside, jnp.exp(scores - top_score[..., None, None]), 0.0
    ).astype(jnp.bfloat16)
    weight_sum = jnp.sum(weights.astype(jnp.float32), axis=(-2, -1))
    both = jnp.einsum(
        "nkgjp,nkpc->nkgjc", weights, value_rows, preferred_element_type=jnp.float32
    )
    mixed_sum = both[..., 0, :head_width] + both[..., 1, head_width:]
    if fresh is not None:
        fresh_weight = lax.optimization_barrier(
            jnp.exp(fresh_score - top_score).astype(jnp.bfloat16)
        ).astype(jnp.float32)
        weight_sum = weight_sum + fresh_weight
        fresh_value = fresh[:, 1].reshape(row_count, kv_heads, 1, head_width).astype(jnp.float32)
        mixed_sum = mixed_sum + fresh_weight[..., None] * fresh_value
    return (
        top_score.reshape(row_count, -1),
        weight_sum.reshape(row_count, -1),
        mixed_sum.reshape(row_count, -1, head_width),
    )


def gather_kernel(n, x_ref, out_ref, held, send_sem, recv_sem):
    me = lax.axis_index("grp")
    col = lax.axis_index("tp")

    barrier = pltpu.get_barrier_semaphore()

    def greet(k, carry):
        peer = lax.rem(me + k, n)
        pl.semaphore_signal(barrier, inc=1, device_id=(peer, col), device_id_type=MESH)
        return carry

    lax.fori_loop(1, n, greet, 0)
    pl.semaphore_wait(barrier, n - 1)

    def copy_to(k):
        peer = lax.rem(me + k, n)
        return pltpu.make_async_remote_copy(
            src_ref=x_ref,
            dst_ref=held.at[me],
            send_sem=send_sem.at[k],
            recv_sem=recv_sem.at[k],
            device_id=(peer, col),
            device_id_type=MESH,
        )

    def copy_from(k):
        source = lax.rem(me + n - k, n)
        return pltpu.make_async_remote_copy(
            src_ref=x_ref,
            dst_ref=held.at[source],
            send_sem=send_sem.at[k],
            recv_sem=recv_sem.at[k],
            device_id=(source, col),
            device_id_type=MESH,
        )

    def start(k, carry):
        copy_to(k).start()
        return carry

    lax.fori_loop(1, n, start, 0)

    def finish(k, carry):
        copy_to(k).wait_send()
        copy_from(k).wait_recv()
        return carry

    lax.fori_loop(1, n, finish, 0)
    held[me] = x_ref[...]
    out_ref[...] = held[...]


def gather_grp(x, n, cid):
    return pl.pallas_call(
        functools.partial(gather_kernel, n),
        out_shape=jax.ShapeDtypeStruct((n,) + x.shape, x.dtype),
        in_specs=[pl.BlockSpec(memory_space=pltpu.VMEM)],
        out_specs=pl.BlockSpec(memory_space=pltpu.VMEM),
        scratch_shapes=[
            pltpu.VMEM((n,) + x.shape, x.dtype),
            pltpu.SemaphoreType.DMA((n,)),
            pltpu.SemaphoreType.DMA((n,)),
        ],
        compiler_params=pltpu.CompilerParams(collective_id=cid, has_side_effects=True),
    )(x)


def final_kernel(n, n_tp, heads, slots, stat_row, partner_ref, back_ref, home_ref, hm_ref, hl_ref,
                 fsel_ref, fwide_ref, w_ref, out_ref, got, part, held, send2, recv2, send3, recv3):
    me = lax.axis_index("grp")
    col = lax.axis_index("tp")
    head_width = w_ref.shape[0] // heads
    width = out_ref.shape[1]

    barrier = pltpu.get_barrier_semaphore()

    def greet(k, carry):
        peer = lax.rem(me + k, n)
        pl.semaphore_signal(barrier, inc=1, device_id=(peer, col), device_id_type=MESH)
        return carry

    lax.fori_loop(1, n, greet, 0)
    for k in range(1, n_tp):
        peer = lax.rem(col + k, n_tp)
        pl.semaphore_signal(barrier, inc=1, device_id=(me, peer), device_id_type=MESH)
    pl.semaphore_wait(barrier, (n - 1) + (n_tp - 1))

    def copy_to(k):
        peer = lax.rem(me + k, n)
        return pltpu.make_async_remote_copy(
            src_ref=back_ref,
            dst_ref=got.at[me],
            send_sem=send2.at[k],
            recv_sem=recv2.at[k],
            device_id=(peer, col),
            device_id_type=MESH,
        )

    def copy_from(k):
        source = lax.rem(me + n - k, n)
        return pltpu.make_async_remote_copy(
            src_ref=back_ref,
            dst_ref=got.at[source],
            send_sem=send2.at[k],
            recv_sem=recv2.at[k],
            device_id=(source, col),
            device_id_type=MESH,
        )

    def start(k, carry):
        copy_to(k).start()
        return carry

    lax.fori_loop(1, n, start, 0)

    def finish(k, carry):
        copy_to(k).wait_send()
        copy_from(k).wait_recv()
        return carry

    lax.fori_loop(1, n, finish, 0)

    block = got[partner_ref[0]].astype(jnp.float32)
    fsel = fsel_ref[...]
    wide = fwide_ref[...]
    stats = block[stat_row : stat_row + 1, :]
    n_st = slots * heads

    def parts(base):
        return (
            stats[:, base : base + n_st]
            + stats[:, base + n_st : base + 2 * n_st]
            + stats[:, base + 2 * n_st : base + 3 * n_st]
        )

    def per_head(x):
        y = x[:, 0:heads]
        for k in range(1, slots):
            y = y + x[:, k * heads : (k + 1) * heads]
        return y

    has = per_head(wide)[:, 0:1] * 0.0
    for k in range(slots):
        has = has + fsel[:, k : k + 1]
    far_m = jnp.where(has > 0.0, per_head(wide * parts(0)), -1e30)
    far_l = per_head(wide * parts(3 * n_st))
    home_m_all = hm_ref[...]
    home_l_all = hl_ref[...]
    lane = lax.broadcasted_iota(jnp.int32, (fsel.shape[0], 2 * head_width), 1)
    left = lane < head_width

    def spread(x, h):
        return jnp.where(left, x[:, 2 * h : 2 * h + 1], x[:, 2 * h + 1 : 2 * h + 2])

    acc = jnp.zeros(part.shape, jnp.float32)
    for h in range(heads // 2):
        far = fsel[:, 0:1] * block[h : h + 1, :]
        for k in range(1, slots):
            far = far + fsel[:, k : k + 1] * block[2 * k + h : 2 * k + h + 1, :]
        home = home_ref[h]
        home_m = spread(home_m_all, h)
        home_l = spread(home_l_all, h)
        fm = spread(far_m, h)
        fl = spread(far_l, h)
        top = jnp.maximum(home_m, fm)
        home_e = jnp.exp(home_m - top)
        far_e = jnp.exp(fm - top)
        mix = (home * home_e + far * far_e) / (home_l * home_e + fl * far_e)
        acc = acc + jnp.dot(
            mix.astype(jnp.bfloat16),
            w_ref[h * 2 * head_width : (h + 1) * 2 * head_width, :],
            preferred_element_type=jnp.float32,
        )
    part[...] = acc

    sends = []
    for k in range(1, n_tp):
        peer = lax.rem(col + k, n_tp)
        cols = pl.ds(pl.multiple_of(peer * width, width), width)
        copy = pltpu.make_async_remote_copy(
            src_ref=part.at[:, cols],
            dst_ref=held.at[k],
            send_sem=send3.at[k],
            recv_sem=recv3.at[k],
            device_id=(me, peer),
            device_id_type=MESH,
        )
        copy.start()
        sends.append(copy)
    own = pl.ds(pl.multiple_of(col * width, width), width)
    total = part[:, own]
    for copy in sends:
        copy.wait_send()
        copy.wait_recv()
    for k in range(1, n_tp):
        total = total + held[k]
    out_ref[...] = total.astype(out_ref.dtype)


def finish_call(n, n_tp, heads, slots, stat_row, partner, back, home, home_m, home_l, fsel, fwide,
                out_weight, cid):
    rows = home.shape[1]
    width = out_weight.shape[1] // n_tp
    vmem = pl.BlockSpec(memory_space=pltpu.VMEM)
    return pl.pallas_call(
        functools.partial(final_kernel, n, n_tp, heads, slots, stat_row),
        out_shape=jax.ShapeDtypeStruct((rows, width), jnp.bfloat16),
        in_specs=[pl.BlockSpec(memory_space=pltpu.SMEM)] + [vmem] * 7,
        out_specs=vmem,
        scratch_shapes=[
            pltpu.VMEM((n,) + back.shape, back.dtype),
            pltpu.VMEM((rows, out_weight.shape[1]), jnp.float32),
            pltpu.VMEM((n_tp, rows, width), jnp.float32),
            pltpu.SemaphoreType.DMA((n,)),
            pltpu.SemaphoreType.DMA((n,)),
            pltpu.SemaphoreType.DMA((n_tp,)),
            pltpu.SemaphoreType.DMA((n_tp,)),
        ],
        compiler_params=pltpu.CompilerParams(collective_id=cid, has_side_effects=True),
    )(partner, back, home, home_m, home_l, fsel, fwide, out_weight)


def three_way(x):
    hi = x.astype(jnp.bfloat16)
    rest = x - hi.astype(jnp.float32)
    mid = rest.astype(jnp.bfloat16)
    lo = (rest - mid.astype(jnp.float32)).astype(jnp.bfloat16)
    return [hi, mid, lo]


def tile(rows_of, extra):
    lanes = rows_of.shape[1]
    rows = rows_of.shape[0]
    stat = jnp.zeros((1, lanes), jnp.bfloat16).at[0, : extra.shape[0]].set(extra)
    pad = jnp.zeros((16 - rows - 1, lanes), jnp.bfloat16)
    return jnp.concatenate([rows_of, stat, pad], axis=0)


def per_device(ny, nz, queries, new_kv, home_cache, help_cache, lengths, split_at, helper_req, out_weight):
    n_grp = lax.axis_size("grp")
    n_tp = lax.axis_size("tp")
    row_count, width = queries.shape
    slots = help_cache.shape[0]
    heads = width // 64
    lanes = 128

    is_long = lengths > LONG_AT
    before = jnp.arange(row_count)[None, :] < jnp.arange(row_count)[:, None]
    rank = jnp.sum(jnp.where(before, is_long[None, :], False), axis=1)
    pick = is_long[None, :] & (rank[None, :] == jnp.arange(slots)[:, None])
    long_q = jnp.dot(
        pick.astype(jnp.bfloat16), queries, preferred_element_type=jnp.float32
    ).astype(jnp.bfloat16)
    long_count = jnp.sum(jnp.where(pick, (lengths - split_at)[None, :], 0), axis=1)
    counts = jnp.concatenate([long_count // 32, long_count % 32]).astype(jnp.bfloat16)
    stat_row = slots * width // lanes
    sent = tile(long_q.reshape(stat_row, lanes), counts)

    partner = helper_req[0] // row_count
    got = gather_grp(sent, n_grp, 0)
    mine = lax.dynamic_index_in_dim(got, partner, axis=0, keepdims=False)
    help_queries = mine[:stat_row].reshape(slots, width)
    code = mine[stat_row].astype(jnp.int32)
    help_count = code[:slots] * 32 + code[slots : 2 * slots]
    help_m, help_l, help_u = attend(help_queries, help_cache, help_count, None)
    stat_parts = three_way(help_m.reshape(-1)) + three_way(help_l.reshape(-1))
    back = tile(
        help_u.astype(jnp.bfloat16).reshape(stat_row, lanes), jnp.concatenate(stat_parts)
    )

    home_m, home_l, home_u = attend(queries, home_cache, split_at, new_kv)
    home = home_u.reshape(row_count, heads // 2, lanes).transpose(1, 0, 2)
    fsel = (is_long[:, None] & (rank[:, None] == jnp.arange(slots)[None, :])).astype(jnp.float32)
    fwide = jnp.repeat(fsel, heads, axis=1)
    partner_arr = (helper_req[:1] // row_count).astype(jnp.int32)
    return finish_call(
        n_grp, n_tp, heads, slots, stat_row, partner_arr, back, home, home_m, home_l, fsel, fwide,
        out_weight, 1,
    )


def grp_rows(mesh):
    column = list(mesh.devices[:, 0])
    n = len(column)
    coords = [getattr(d, "coords", None) for d in column]
    if coords[0] is not None:
        nz = 1
        while nz < n and coords[nz][1] == coords[0][1]:
            nz += 1
    else:
        nz = 1
        while nz * nz < n:
            nz *= 2
    return n // nz, nz


def solution(mesh):
    ny, nz = grp_rows(mesh)
    return jax.shard_map(
        functools.partial(per_device, ny, nz),
        mesh=mesh,
        in_specs=(
            P("grp", "tp"),
            P("grp", None, "tp"),
            P("grp", None, "tp", None, None),
            P("grp", None, "tp", None, None),
            P("grp"),
            P("grp"),
            P("grp"),
            P("tp", None),
        ),
        out_specs=P("grp", "tp"),
        check_vma=False,
    )
```

```python
import functools

import jax
import jax.numpy as jnp
from jax import lax
from jax.experimental import pallas as pl
from jax.experimental.pallas import tpu as pltpu
from jax.sharding import PartitionSpec as P

MESH = pl.DeviceIdType.MESH
LONG_AT = 1024


def attend(queries, cache, count, fresh):
    row_count = queries.shape[0]
    kv_heads = cache.shape[2]
    head_width = cache.shape[4] // 2
    half = cache.shape[3]
    group_size = queries.shape[1] // (kv_heads * head_width)
    score_scale = head_width ** (-0.5)
    head_rows = queries.reshape(row_count, kv_heads, group_size, head_width)
    blank = jnp.zeros_like(head_rows)
    wide_rows = jnp.stack(
        [
            jnp.concatenate([head_rows, blank], axis=-1),
            jnp.concatenate([blank, head_rows], axis=-1),
        ],
        axis=3,
    )
    key_rows = cache[:, 0]
    value_rows = cache[:, 1]
    scores = (
        jnp.einsum("nkgjc,nkpc->nkgjp", wide_rows, key_rows, preferred_element_type=jnp.float32)
        * score_scale
    )
    position = 2 * jnp.arange(half)[None, :] + jnp.arange(2)[:, None]
    inside = (position[None] < count[:, None, None])[:, None, None]
    top_score = jnp.max(jnp.where(inside, scores, -1e30), axis=(-2, -1))
    if fresh is not None:
        fresh_key = fresh[:, 0].reshape(row_count, kv_heads, head_width)
        fresh_score = (
            jnp.einsum("nkgd,nkd->nkg", head_rows, fresh_key, preferred_element_type=jnp.float32)
            * score_scale
        )
        top_score = jnp.maximum(top_score, fresh_score)
    weights = jnp.where(
        inside, jnp.exp(scores - top_score[..., None, None]), 0.0
    ).astype(jnp.bfloat16)
    weight_sum = jnp.sum(weights.astype(jnp.float32), axis=(-2, -1))
    both = jnp.einsum(
        "nkgjp,nkpc->nkgjc", weights, value_rows, preferred_element_type=jnp.float32
    )
    mixed_sum = both[..., 0, :head_width] + both[..., 1, head_width:]
    if fresh is not None:
        fresh_weight = lax.optimization_barrier(
            jnp.exp(fresh_score - top_score).astype(jnp.bfloat16)
        ).astype(jnp.float32)
        weight_sum = weight_sum + fresh_weight
        fresh_value = fresh[:, 1].reshape(row_count, kv_heads, 1, head_width).astype(jnp.float32)
        mixed_sum = mixed_sum + fresh_weight[..., None] * fresh_value
    return (
        top_score.reshape(row_count, -1),
        weight_sum.reshape(row_count, -1),
        mixed_sum.reshape(row_count, -1, head_width),
    )


def gather_kernel(n, x_ref, out_ref, held, send_sem, recv_sem):
    me = lax.axis_index("grp")
    col = lax.axis_index("tp")

    barrier = pltpu.get_barrier_semaphore()

    def greet(k, carry):
        peer = lax.rem(me + k, n)
        pl.semaphore_signal(barrier, inc=1, device_id=(peer, col), device_id_type=MESH)
        return carry

    lax.fori_loop(1, n, greet, 0)
    pl.semaphore_wait(barrier, n - 1)

    def copy_to(k):
        peer = lax.rem(me + k, n)
        return pltpu.make_async_remote_copy(
            src_ref=x_ref,
            dst_ref=held.at[me],
            send_sem=send_sem.at[k],
            recv_sem=recv_sem.at[k],
            device_id=(peer, col),
            device_id_type=MESH,
        )

    def copy_from(k):
        source = lax.rem(me + n - k, n)
        return pltpu.make_async_remote_copy(
            src_ref=x_ref,
            dst_ref=held.at[source],
            send_sem=send_sem.at[k],
            recv_sem=recv_sem.at[k],
            device_id=(source, col),
            device_id_type=MESH,
        )

    def start(k, carry):
        copy_to(k).start()
        return carry

    lax.fori_loop(1, n, start, 0)

    def finish(k, carry):
        copy_to(k).wait_send()
        copy_from(k).wait_recv()
        return carry

    lax.fori_loop(1, n, finish, 0)
    held[me] = x_ref[...]
    out_ref[...] = held[...]


def gather_grp(x, n, cid):
    return pl.pallas_call(
        functools.partial(gather_kernel, n),
        out_shape=jax.ShapeDtypeStruct((n,) + x.shape, x.dtype),
        in_specs=[pl.BlockSpec(memory_space=pltpu.VMEM)],
        out_specs=pl.BlockSpec(memory_space=pltpu.VMEM),
        scratch_shapes=[
            pltpu.VMEM((n,) + x.shape, x.dtype),
            pltpu.SemaphoreType.DMA((n,)),
            pltpu.SemaphoreType.DMA((n,)),
        ],
        compiler_params=pltpu.CompilerParams(collective_id=cid, has_side_effects=True),
    )(x)


def fanout(n, me, col, src, dst, send, recv):
    def copy(k, peer, slot):
        return pltpu.make_async_remote_copy(
            src_ref=src,
            dst_ref=dst.at[slot],
            send_sem=send.at[k],
            recv_sem=recv.at[k],
            device_id=(peer, col),
            device_id_type=MESH,
        )

    def start(k, carry):
        copy(k, lax.rem(me + k, n), me).start()
        return carry

    lax.fori_loop(1, n, start, 0)

    def finish():
        def one(k, carry):
            copy(k, lax.rem(me + k, n), me).wait_send()
            source = lax.rem(me + n - k, n)
            copy(k, source, source).wait_recv()
            return carry

        lax.fori_loop(1, n, one, 0)

    return finish


def attend_tile(wide, keys, values, count, fresh_k=None, fresh_v=None):
    rows = wide.shape[0]
    scores = lax.dot_general(
        wide, keys, (((1,), (1,)), ((), ())), preferred_element_type=jnp.float32
    ) * 0.125
    half = rows // 2
    row = lax.broadcasted_iota(jnp.int32, scores.shape, 0)
    lane = lax.broadcasted_iota(jnp.int32, scores.shape, 1)
    position = 2 * lane + jnp.where(row >= half, 1, 0)
    inside = position.astype(jnp.float32) < count
    top = jnp.max(jnp.where(inside, scores, -1e30), axis=1, keepdims=True)
    top = jnp.maximum(top, pltpu.roll(top, half, 0))
    if fresh_k is not None:
        fresh_score = jnp.sum(
            wide.astype(jnp.float32) * fresh_k.astype(jnp.float32), axis=1, keepdims=True
        ) * 0.125
        top = jnp.maximum(top, fresh_score)
    weights = jnp.where(inside, jnp.exp(scores - top), 0.0).astype(jnp.bfloat16)
    total = jnp.sum(weights.astype(jnp.float32), axis=1, keepdims=True)
    total = total + pltpu.roll(total, half, 0)
    both = jnp.dot(weights, values, preferred_element_type=jnp.float32)
    mixed = both + pltpu.roll(pltpu.roll(both, half, 0), 64, 1)
    if fresh_k is not None:
        fresh_w = jnp.exp(fresh_score - top).astype(jnp.bfloat16).astype(jnp.float32)
        total = total + fresh_w
        mixed = mixed + fresh_w * fresh_v
    return top, total, mixed


def pair_rows(top, total, mixed, h):
    lane = lax.broadcasted_iota(jnp.int32, (1, mixed.shape[1]), 1)
    left = lane < 64
    g = 2 * h
    u = jnp.where(left, mixed[g : g + 1, :], mixed[g + 5 : g + 6, :])
    m = jnp.where(left, top[g : g + 1, :], top[g + 1 : g + 2, :])
    l = jnp.where(left, total[g : g + 1, :], total[g + 1 : g + 2, :])
    return u, m, l


def whole_kernel(n, n_tp, slots, partner_ref, sent_ref, home_wide_ref, home_cnt_ref, fresh_k_ref,
                 fresh_v_ref, home_ref, help_ref, fsel_ref, w_ref, out_ref,
                 got1, got2, back, stat, part, held, send1, recv1, send2, recv2, send3, recv3):
    me = lax.axis_index("grp")
    col = lax.axis_index("tp")
    rows = home_wide_ref.shape[0]
    pairs = w_ref.shape[0] // 128
    width = out_ref.shape[1]

    barrier = pltpu.get_barrier_semaphore()

    def greet(k, carry):
        peer = lax.rem(me + k, n)
        pl.semaphore_signal(barrier, inc=1, device_id=(peer, col), device_id_type=MESH)
        return carry

    lax.fori_loop(1, n, greet, 0)
    for k in range(1, n_tp):
        peer = lax.rem(col + k, n_tp)
        pl.semaphore_signal(barrier, inc=1, device_id=(me, peer), device_id_type=MESH)
    pl.semaphore_wait(barrier, (n - 1) + (n_tp - 1))

    wait1 = fanout(n, me, col, sent_ref, got1, send1, recv1)
    for r in range(rows):
        top, total, mixed = attend_tile(
            home_wide_ref[r],
            home_ref[r, 0, 0],
            home_ref[r, 1, 0],
            home_cnt_ref[r : r + 1, 0:1],
            fresh_k_ref[r : r + 1, :],
            fresh_v_ref[r : r + 1, :],
        )
        for h in range(pairs):
            u, m, l = pair_rows(top, total, mixed, h)
            stat[0, h, r : r + 1, :] = u
            stat[1, h, r : r + 1, :] = m
            stat[2, h, r : r + 1, :] = l
    wait1()

    block = got1[partner_ref[0]]
    code = block[8 * slots : 8 * slots + 1, :].astype(jnp.float32)
    for k in range(slots):
        count = code[:, k : k + 1] * 32.0 + code[:, slots + k : slots + k + 1]
        top, total, mixed = attend_tile(
            block[8 * k : 8 * k + 8, :], help_ref[k, 0, 0], help_ref[k, 1, 0], count
        )
        for h in range(pairs):
            u, m, l = pair_rows(top, total, mixed, h)
            back[k * pairs + h : k * pairs + h + 1, :] = u
            back[(slots + k) * pairs + h : (slots + k) * pairs + h + 1, :] = m
            back[(2 * slots + k) * pairs + h : (2 * slots + k) * pairs + h + 1, :] = l

    wait2 = fanout(n, me, col, back, got2, send2, recv2)
    wait2()

    theirs = got2[partner_ref[0]]
    fsel = fsel_ref[...]
    has = fsel[:, 0:1]
    for k in range(1, slots):
        has = has + fsel[:, k : k + 1]
    acc = jnp.zeros(part.shape, jnp.float32)
    for h in range(pairs):

        def pick(base):
            x = fsel[:, 0:1] * theirs[base + h : base + h + 1, :]
            for k in range(1, slots):
                r0 = base + k * pairs + h
                x = x + fsel[:, k : k + 1] * theirs[r0 : r0 + 1, :]
            return x

        far_u = pick(0)
        far_m = jnp.where(has > 0.0, pick(slots * pairs), -1e30)
        far_l = pick(2 * slots * pairs)
        home_u = stat[0, h]
        home_m = stat[1, h]
        home_l = stat[2, h]
        top = jnp.maximum(home_m, far_m)
        home_e = jnp.exp(home_m - top)
        far_e = jnp.exp(far_m - top)
        mix = (home_u * home_e + far_u * far_e) / (home_l * home_e + far_l * far_e)
        acc = acc + jnp.dot(
            mix.astype(jnp.bfloat16),
            w_ref[h * 128 : (h + 1) * 128, :],
            preferred_element_type=jnp.float32,
        )
    part[...] = acc

    sends = []
    for k in range(1, n_tp):
        peer = lax.rem(col + k, n_tp)
        cols = pl.ds(pl.multiple_of(peer * width, width), width)
        copy = pltpu.make_async_remote_copy(
            src_ref=part.at[:, cols],
            dst_ref=held.at[k],
            send_sem=send3.at[k],
            recv_sem=recv3.at[k],
            device_id=(me, peer),
            device_id_type=MESH,
        )
        copy.start()
        sends.append(copy)
    own = pl.ds(pl.multiple_of(col * width, width), width)
    total = part[:, own]
    for copy in sends:
        copy.wait_send()
        copy.wait_recv()
    for k in range(1, n_tp):
        total = total + held[k]
    out_ref[...] = total.astype(out_ref.dtype)


def per_device(ny, nz, queries, new_kv, home_cache, help_cache, lengths, split_at, helper_req, out_weight):
    n_grp = lax.axis_size("grp")
    n_tp = lax.axis_size("tp")
    row_count, width = queries.shape
    slots = help_cache.shape[0]
    heads = width // 64
    pairs = heads // 2
    lanes = 128

    def widen(q):
        q = q.reshape(q.shape[0], heads, 64)
        blank = jnp.zeros_like(q)
        return jnp.concatenate(
            [jnp.concatenate([q, blank], -1), jnp.concatenate([blank, q], -1)], axis=1
        )

    is_long = lengths > LONG_AT
    before = jnp.arange(row_count)[None, :] < jnp.arange(row_count)[:, None]
    rank = jnp.sum(jnp.where(before, is_long[None, :], False), axis=1)
    pick = is_long[None, :] & (rank[None, :] == jnp.arange(slots)[:, None])
    long_q = jnp.dot(
        pick.astype(jnp.bfloat16), queries, preferred_element_type=jnp.float32
    ).astype(jnp.bfloat16)
    long_count = jnp.sum(jnp.where(pick, (lengths - split_at)[None, :], 0), axis=1)
    code = jnp.zeros((16, lanes), jnp.bfloat16)
    code = code.at[0, :slots].set((long_count // 32).astype(jnp.bfloat16))
    code = code.at[0, slots : 2 * slots].set((long_count % 32).astype(jnp.bfloat16))
    sent = jnp.concatenate([widen(long_q).reshape(slots * 2 * heads, lanes), code], axis=0)

    home_wide = widen(queries)
    home_cnt = jnp.broadcast_to(split_at.astype(jnp.float32)[:, None], (row_count, lanes))
    fresh_k = jnp.concatenate([new_kv[:, 0], new_kv[:, 0]], axis=-1)
    fresh_v = jnp.concatenate([new_kv[:, 1], new_kv[:, 1]], axis=-1).astype(jnp.float32)
    fsel = (is_long[:, None] & (rank[:, None] == jnp.arange(slots)[None, :])).astype(jnp.float32)
    partner = (helper_req[:1] // row_count).astype(jnp.int32)

    out_cols = out_weight.shape[1] // n_tp
    vmem = pl.BlockSpec(memory_space=pltpu.VMEM)
    back_rows = 3 * slots * pairs
    return pl.pallas_call(
        functools.partial(whole_kernel, n_grp, n_tp, slots),
        out_shape=jax.ShapeDtypeStruct((row_count, out_cols), jnp.bfloat16),
        in_specs=[pl.BlockSpec(memory_space=pltpu.SMEM)] + [vmem] * 9,
        out_specs=vmem,
        scratch_shapes=[
            pltpu.VMEM((n_grp,) + sent.shape, jnp.bfloat16),
            pltpu.VMEM((n_grp, back_rows, lanes), jnp.float32),
            pltpu.VMEM((back_rows, lanes), jnp.float32),
            pltpu.VMEM((3, pairs, row_count, lanes), jnp.float32),
            pltpu.VMEM((row_count, out_weight.shape[1]), jnp.float32),
            pltpu.VMEM((n_tp, row_count, out_cols), jnp.float32),
            pltpu.SemaphoreType.DMA((n_grp,)),
            pltpu.SemaphoreType.DMA((n_grp,)),
            pltpu.SemaphoreType.DMA((n_grp,)),
            pltpu.SemaphoreType.DMA((n_grp,)),
            pltpu.SemaphoreType.DMA((n_tp,)),
            pltpu.SemaphoreType.DMA((n_tp,)),
        ],
        compiler_params=pltpu.CompilerParams(collective_id=0, has_side_effects=True),
    )(partner, sent, home_wide, home_cnt, fresh_k, fresh_v, home_cache, help_cache, fsel, out_weight)


def grp_rows(mesh):
    column = list(mesh.devices[:, 0])
    n = len(column)
    coords = [getattr(d, "coords", None) for d in column]
    if coords[0] is not None:
        nz = 1
        while nz < n and coords[nz][1] == coords[0][1]:
            nz += 1
    else:
        nz = 1
        while nz * nz < n:
            nz *= 2
    return n // nz, nz


def solution(mesh):
    ny, nz = grp_rows(mesh)
    return jax.shard_map(
        functools.partial(per_device, ny, nz),
        mesh=mesh,
        in_specs=(
            P("grp", "tp"),
            P("grp", None, "tp"),
            P("grp", None, "tp", None, None),
            P("grp", None, "tp", None, None),
            P("grp"),
            P("grp"),
            P("grp"),
            P("tp", None),
        ),
        out_specs=P("grp", "tp"),
        check_vma=False,
    )
```

```python
import functools

import jax
import jax.numpy as jnp
from jax import lax
from jax.experimental import pallas as pl
from jax.experimental.pallas import tpu as pltpu
from jax.sharding import PartitionSpec as P

MESH = pl.DeviceIdType.MESH
LONG_AT = 1024


def attend(queries, cache, count, fresh):
    row_count = queries.shape[0]
    kv_heads = cache.shape[2]
    head_width = cache.shape[4] // 2
    half = cache.shape[3]
    group_size = queries.shape[1] // (kv_heads * head_width)
    score_scale = head_width ** (-0.5)
    head_rows = queries.reshape(row_count, kv_heads, group_size, head_width)
    blank = jnp.zeros_like(head_rows)
    wide_rows = jnp.stack(
        [
            jnp.concatenate([head_rows, blank], axis=-1),
            jnp.concatenate([blank, head_rows], axis=-1),
        ],
        axis=3,
    )
    key_rows = cache[:, 0]
    value_rows = cache[:, 1]
    scores = (
        jnp.einsum("nkgjc,nkpc->nkgjp", wide_rows, key_rows, preferred_element_type=jnp.float32)
        * score_scale
    )
    position = 2 * jnp.arange(half)[None, :] + jnp.arange(2)[:, None]
    inside = (position[None] < count[:, None, None])[:, None, None]
    top_score = jnp.max(jnp.where(inside, scores, -1e30), axis=(-2, -1))
    if fresh is not None:
        fresh_key = fresh[:, 0].reshape(row_count, kv_heads, head_width)
        fresh_score = (
            jnp.einsum("nkgd,nkd->nkg", head_rows, fresh_key, preferred_element_type=jnp.float32)
            * score_scale
        )
        top_score = jnp.maximum(top_score, fresh_score)
    weights = jnp.where(
        inside, jnp.exp(scores - top_score[..., None, None]), 0.0
    ).astype(jnp.bfloat16)
    weight_sum = jnp.sum(weights.astype(jnp.float32), axis=(-2, -1))
    both = jnp.einsum(
        "nkgjp,nkpc->nkgjc", weights, value_rows, preferred_element_type=jnp.float32
    )
    mixed_sum = both[..., 0, :head_width] + both[..., 1, head_width:]
    if fresh is not None:
        fresh_weight = lax.optimization_barrier(
            jnp.exp(fresh_score - top_score).astype(jnp.bfloat16)
        ).astype(jnp.float32)
        weight_sum = weight_sum + fresh_weight
        fresh_value = fresh[:, 1].reshape(row_count, kv_heads, 1, head_width).astype(jnp.float32)
        mixed_sum = mixed_sum + fresh_weight[..., None] * fresh_value
    return (
        top_score.reshape(row_count, -1),
        weight_sum.reshape(row_count, -1),
        mixed_sum.reshape(row_count, -1, head_width),
    )


def gather_kernel(n, x_ref, out_ref, held, send_sem, recv_sem):
    me = lax.axis_index("grp")
    col = lax.axis_index("tp")

    barrier = pltpu.get_barrier_semaphore()

    def greet(k, carry):
        peer = lax.rem(me + k, n)
        pl.semaphore_signal(barrier, inc=1, device_id=(peer, col), device_id_type=MESH)
        return carry

    lax.fori_loop(1, n, greet, 0)
    pl.semaphore_wait(barrier, n - 1)

    def copy_to(k):
        peer = lax.rem(me + k, n)
        return pltpu.make_async_remote_copy(
            src_ref=x_ref,
            dst_ref=held.at[me],
            send_sem=send_sem.at[k],
            recv_sem=recv_sem.at[k],
            device_id=(peer, col),
            device_id_type=MESH,
        )

    def copy_from(k):
        source = lax.rem(me + n - k, n)
        return pltpu.make_async_remote_copy(
            src_ref=x_ref,
            dst_ref=held.at[source],
            send_sem=send_sem.at[k],
            recv_sem=recv_sem.at[k],
            device_id=(source, col),
            device_id_type=MESH,
        )

    def start(k, carry):
        copy_to(k).start()
        return carry

    lax.fori_loop(1, n, start, 0)

    def finish(k, carry):
        copy_to(k).wait_send()
        copy_from(k).wait_recv()
        return carry

    lax.fori_loop(1, n, finish, 0)
    held[me] = x_ref[...]
    out_ref[...] = held[...]


def gather_grp(x, n, cid):
    return pl.pallas_call(
        functools.partial(gather_kernel, n),
        out_shape=jax.ShapeDtypeStruct((n,) + x.shape, x.dtype),
        in_specs=[pl.BlockSpec(memory_space=pltpu.VMEM)],
        out_specs=pl.BlockSpec(memory_space=pltpu.VMEM),
        scratch_shapes=[
            pltpu.VMEM((n,) + x.shape, x.dtype),
            pltpu.SemaphoreType.DMA((n,)),
            pltpu.SemaphoreType.DMA((n,)),
        ],
        compiler_params=pltpu.CompilerParams(collective_id=cid, has_side_effects=True),
    )(x)


def fanout(n, me, col, src, dst, send, recv):
    def copy(k, peer, slot):
        return pltpu.make_async_remote_copy(
            src_ref=src,
            dst_ref=dst.at[slot],
            send_sem=send.at[k],
            recv_sem=recv.at[k],
            device_id=(peer, col),
            device_id_type=MESH,
        )

    def start(k, carry):
        copy(k, lax.rem(me + k, n), me).start()
        return carry

    lax.fori_loop(1, n, start, 0)

    def finish():
        def one(k, carry):
            copy(k, lax.rem(me + k, n), me).wait_send()
            source = lax.rem(me + n - k, n)
            copy(k, source, source).wait_recv()
            return carry

        lax.fori_loop(1, n, one, 0)

    return finish


def attend_tile(wide, keys, values, count, fresh_k=None, fresh_v=None):
    rows = wide.shape[0]
    scores = lax.dot_general(
        wide, keys, (((1,), (1,)), ((), ())), preferred_element_type=jnp.float32
    ) * 0.125
    half = rows // 2
    row = lax.broadcasted_iota(jnp.int32, scores.shape, 0)
    lane = lax.broadcasted_iota(jnp.int32, scores.shape, 1)
    position = 2 * lane + jnp.where(row >= half, 1, 0)
    inside = position.astype(jnp.float32) < count
    top = jnp.max(jnp.where(inside, scores, -1e30), axis=1, keepdims=True)
    top = jnp.maximum(top, pltpu.roll(top, half, 0))
    if fresh_k is not None:
        fresh_score = jnp.sum(
            wide.astype(jnp.float32) * fresh_k.astype(jnp.float32), axis=1, keepdims=True
        ) * 0.125
        top = jnp.maximum(top, fresh_score)
    weights = jnp.where(inside, jnp.exp(scores - top), 0.0).astype(jnp.bfloat16)
    total = jnp.sum(weights.astype(jnp.float32), axis=1, keepdims=True)
    total = total + pltpu.roll(total, half, 0)
    both = jnp.dot(weights, values, preferred_element_type=jnp.float32)
    mixed = both + pltpu.roll(pltpu.roll(both, half, 0), 64, 1)
    if fresh_k is not None:
        fresh_w = jnp.exp(fresh_score - top).astype(jnp.bfloat16).astype(jnp.float32)
        total = total + fresh_w
        mixed = mixed + fresh_w * fresh_v
    return top, total, mixed


def pair_rows(top, total, mixed, h):
    lane = lax.broadcasted_iota(jnp.int32, (1, mixed.shape[1]), 1)
    left = lane < 64
    g = 2 * h
    u = jnp.where(left, mixed[g : g + 1, :], mixed[g + 5 : g + 6, :])
    m = jnp.where(left, top[g : g + 1, :], top[g + 1 : g + 2, :])
    l = jnp.where(left, total[g : g + 1, :], total[g + 1 : g + 2, :])
    return u, m, l


def widen(q, heads):
    lane = lax.broadcasted_iota(jnp.int32, (2 * heads, 128), 1)
    row = lax.broadcasted_iota(jnp.int32, (2 * heads, 128), 0)
    low = lane < 64
    wide = jnp.zeros((2 * heads, 128), jnp.float32)
    for h in range(heads // 2):
        a = q[:, h * 128 : (h + 1) * 128]
        turned = pltpu.roll(a, 64, 1)
        g = 2 * h
        wide = jnp.where((row == g) & low, a, wide)
        wide = jnp.where((row == g + 1) & low, turned, wide)
        wide = jnp.where((row == heads + g) & ~low, turned, wide)
        wide = jnp.where((row == heads + g + 1) & ~low, a, wide)
    return wide.astype(jnp.bfloat16)


def whole_kernel(n, n_tp, slots, lengths_ref, splits_ref, helpers_ref, sent_ref, queries_ref,
                 kv_ref, home_ref, help_ref, w_ref, out_ref,
                 got1, got2, back, stat, part, held, send1, recv1, send2, recv2, send3, recv3):
    me = lax.axis_index("grp")
    col = lax.axis_index("tp")
    rows = queries_ref.shape[0]
    heads = queries_ref.shape[1] // 64
    pairs = w_ref.shape[0] // 128
    width = out_ref.shape[1]

    barrier = pltpu.get_barrier_semaphore()

    def greet(k, carry):
        peer = lax.rem(me + k, n)
        pl.semaphore_signal(barrier, inc=1, device_id=(peer, col), device_id_type=MESH)
        return carry

    lax.fori_loop(1, n, greet, 0)
    for k in range(1, n_tp):
        peer = lax.rem(col + k, n_tp)
        pl.semaphore_signal(barrier, inc=1, device_id=(me, peer), device_id_type=MESH)
    pl.semaphore_wait(barrier, (n - 1) + (n_tp - 1))

    wait1 = fanout(n, me, col, sent_ref, got1, send1, recv1)
    lane = lax.broadcasted_iota(jnp.int32, (1, 128), 1)
    low = lane < 64
    for r in range(rows):
        kv = kv_ref[r : r + 1, :].astype(jnp.float32)
        turned = pltpu.roll(kv, 64, 1)
        fresh_k = jnp.where(low, kv, turned).astype(jnp.bfloat16)
        fresh_v = jnp.where(low, turned, kv)
        count = splits_ref[r].astype(jnp.float32)
        top, total, mixed = attend_tile(
            widen(queries_ref[r : r + 1, :].astype(jnp.float32), heads),
            home_ref[r, 0, 0],
            home_ref[r, 1, 0],
            count,
            fresh_k,
            fresh_v,
        )
        for h in range(pairs):
            u, m, l = pair_rows(top, total, mixed, h)
            stat[0, h, r : r + 1, :] = u
            stat[1, h, r : r + 1, :] = m
            stat[2, h, r : r + 1, :] = l
    wait1()

    partner = helpers_ref[0] // rows
    block = got1[partner]
    pick_row = lax.broadcasted_iota(jnp.int32, (slots, rows), 0)
    pick_col = lax.broadcasted_iota(jnp.int32, (slots, rows), 1)
    pick = jnp.zeros((slots, rows), jnp.float32)
    for k in range(slots):
        pick = jnp.where((pick_row == k) & (pick_col == helpers_ref[k] % rows), 1.0, pick)
    chosen = jnp.dot(pick.astype(jnp.bfloat16), block, preferred_element_type=jnp.float32)
    qw = heads * 64
    for k in range(slots):
        count = chosen[k : k + 1, qw : qw + 1] * 32.0 + chosen[k : k + 1, qw + 1 : qw + 2]
        top, total, mixed = attend_tile(
            widen(chosen[k : k + 1, :qw], heads), help_ref[k, 0, 0], help_ref[k, 1, 0], count
        )
        for h in range(pairs):
            u, m, l = pair_rows(top, total, mixed, h)
            back[k * pairs + h : k * pairs + h + 1, :] = u
            back[(slots + k) * pairs + h : (slots + k) * pairs + h + 1, :] = m
            back[(2 * slots + k) * pairs + h : (2 * slots + k) * pairs + h + 1, :] = l

    wait2 = fanout(n, me, col, back, got2, send2, recv2)

    sel_row = lax.broadcasted_iota(jnp.int32, (rows, slots), 0)
    sel_col = lax.broadcasted_iota(jnp.int32, (rows, slots), 1)
    fsel = jnp.zeros((rows, slots), jnp.float32)
    rank = jnp.int32(0)
    for r in range(rows):
        is_long = lengths_ref[r] > LONG_AT
        fsel = jnp.where((sel_row == r) & (sel_col == rank) & is_long, 1.0, fsel)
        rank = rank + is_long.astype(jnp.int32)
    has = fsel[:, 0:1]
    for k in range(1, slots):
        has = has + fsel[:, k : k + 1]
    wait2()

    theirs = got2[partner]
    acc = jnp.zeros(part.shape, jnp.float32)
    for h in range(pairs):

        def pick_far(base):
            x = fsel[:, 0:1] * theirs[base + h : base + h + 1, :]
            for k in range(1, slots):
                r0 = base + k * pairs + h
                x = x + fsel[:, k : k + 1] * theirs[r0 : r0 + 1, :]
            return x

        far_u = pick_far(0)
        far_m = jnp.where(has > 0.0, pick_far(slots * pairs), -1e30)
        far_l = pick_far(2 * slots * pairs)
        home_u = stat[0, h]
        home_m = stat[1, h]
        home_l = stat[2, h]
        top = jnp.maximum(home_m, far_m)
        home_e = jnp.exp(home_m - top)
        far_e = jnp.exp(far_m - top)
        mix = (home_u * home_e + far_u * far_e) / (home_l * home_e + far_l * far_e)
        acc = acc + jnp.dot(
            mix.astype(jnp.bfloat16),
            w_ref[h * 128 : (h + 1) * 128, :],
            preferred_element_type=jnp.float32,
        )
    part[...] = acc

    sends = []
    for k in range(1, n_tp):
        peer = lax.rem(col + k, n_tp)
        cols = pl.ds(pl.multiple_of(peer * width, width), width)
        copy = pltpu.make_async_remote_copy(
            src_ref=part.at[:, cols],
            dst_ref=held.at[k],
            send_sem=send3.at[k],
            recv_sem=recv3.at[k],
            device_id=(me, peer),
            device_id_type=MESH,
        )
        copy.start()
        sends.append(copy)
    own = pl.ds(pl.multiple_of(col * width, width), width)
    total = part[:, own]
    for copy in sends:
        copy.wait_send()
        copy.wait_recv()
    for k in range(1, n_tp):
        total = total + held[k]
    out_ref[...] = total.astype(out_ref.dtype)


def per_device(ny, nz, queries, new_kv, home_cache, help_cache, lengths, split_at, helper_req, out_weight):
    n_grp = lax.axis_size("grp")
    n_tp = lax.axis_size("tp")
    row_count, width = queries.shape
    slots = help_cache.shape[0]
    pairs = width // 128
    lanes = 128

    count = lengths - split_at
    lane = jnp.arange(lanes)[None, :]
    code = jnp.where(
        lane == 0, (count // 32)[:, None], jnp.where(lane == 1, (count % 32)[:, None], 0)
    ).astype(jnp.bfloat16)
    sent = jnp.concatenate([queries, code], axis=1)
    kv = new_kv.reshape(row_count, 2 * new_kv.shape[2])

    out_cols = out_weight.shape[1] // n_tp
    vmem = pl.BlockSpec(memory_space=pltpu.VMEM)
    smem = pl.BlockSpec(memory_space=pltpu.SMEM)
    back_rows = 3 * slots * pairs
    return pl.pallas_call(
        functools.partial(whole_kernel, n_grp, n_tp, slots),
        out_shape=jax.ShapeDtypeStruct((row_count, out_cols), jnp.bfloat16),
        in_specs=[smem] * 3 + [vmem] * 6,
        out_specs=vmem,
        scratch_shapes=[
            pltpu.VMEM((n_grp,) + sent.shape, jnp.bfloat16),
            pltpu.VMEM((n_grp, back_rows, lanes), jnp.float32),
            pltpu.VMEM((back_rows, lanes), jnp.float32),
            pltpu.VMEM((3, pairs, row_count, lanes), jnp.float32),
            pltpu.VMEM((row_count, out_weight.shape[1]), jnp.float32),
            pltpu.VMEM((n_tp, row_count, out_cols), jnp.float32),
            pltpu.SemaphoreType.DMA((n_grp,)),
            pltpu.SemaphoreType.DMA((n_grp,)),
            pltpu.SemaphoreType.DMA((n_grp,)),
            pltpu.SemaphoreType.DMA((n_grp,)),
            pltpu.SemaphoreType.DMA((n_tp,)),
            pltpu.SemaphoreType.DMA((n_tp,)),
        ],
        compiler_params=pltpu.CompilerParams(collective_id=0, has_side_effects=True),
    )(lengths, split_at, helper_req, sent, queries, kv, home_cache, help_cache, out_weight)


def grp_rows(mesh):
    column = list(mesh.devices[:, 0])
    n = len(column)
    coords = [getattr(d, "coords", None) for d in column]
    if coords[0] is not None:
        nz = 1
        while nz < n and coords[nz][1] == coords[0][1]:
            nz += 1
    else:
        nz = 1
        while nz * nz < n:
            nz *= 2
    return n // nz, nz


def solution(mesh):
    ny, nz = grp_rows(mesh)
    return jax.shard_map(
        functools.partial(per_device, ny, nz),
        mesh=mesh,
        in_specs=(
            P("grp", "tp"),
            P("grp", None, "tp"),
            P("grp", None, "tp", None, None),
            P("grp", None, "tp", None, None),
            P("grp"),
            P("grp"),
            P("grp"),
            P("tp", None),
        ),
        out_specs=P("grp", "tp"),
        check_vma=False,
    )
```

```python
import functools

import jax
import jax.numpy as jnp
from jax import lax
from jax.experimental import pallas as pl
from jax.experimental.pallas import tpu as pltpu
from jax.sharding import PartitionSpec as P

MESH = pl.DeviceIdType.MESH
LONG_AT = 1024


def attend(queries, cache, count, fresh):
    row_count = queries.shape[0]
    kv_heads = cache.shape[2]
    head_width = cache.shape[4] // 2
    half = cache.shape[3]
    group_size = queries.shape[1] // (kv_heads * head_width)
    score_scale = head_width ** (-0.5)
    head_rows = queries.reshape(row_count, kv_heads, group_size, head_width)
    blank = jnp.zeros_like(head_rows)
    wide_rows = jnp.stack(
        [
            jnp.concatenate([head_rows, blank], axis=-1),
            jnp.concatenate([blank, head_rows], axis=-1),
        ],
        axis=3,
    )
    key_rows = cache[:, 0]
    value_rows = cache[:, 1]
    scores = (
        jnp.einsum("nkgjc,nkpc->nkgjp", wide_rows, key_rows, preferred_element_type=jnp.float32)
        * score_scale
    )
    position = 2 * jnp.arange(half)[None, :] + jnp.arange(2)[:, None]
    inside = (position[None] < count[:, None, None])[:, None, None]
    top_score = jnp.max(jnp.where(inside, scores, -1e30), axis=(-2, -1))
    if fresh is not None:
        fresh_key = fresh[:, 0].reshape(row_count, kv_heads, head_width)
        fresh_score = (
            jnp.einsum("nkgd,nkd->nkg", head_rows, fresh_key, preferred_element_type=jnp.float32)
            * score_scale
        )
        top_score = jnp.maximum(top_score, fresh_score)
    weights = jnp.where(
        inside, jnp.exp(scores - top_score[..., None, None]), 0.0
    ).astype(jnp.bfloat16)
    weight_sum = jnp.sum(weights.astype(jnp.float32), axis=(-2, -1))
    both = jnp.einsum(
        "nkgjp,nkpc->nkgjc", weights, value_rows, preferred_element_type=jnp.float32
    )
    mixed_sum = both[..., 0, :head_width] + both[..., 1, head_width:]
    if fresh is not None:
        fresh_weight = lax.optimization_barrier(
            jnp.exp(fresh_score - top_score).astype(jnp.bfloat16)
        ).astype(jnp.float32)
        weight_sum = weight_sum + fresh_weight
        fresh_value = fresh[:, 1].reshape(row_count, kv_heads, 1, head_width).astype(jnp.float32)
        mixed_sum = mixed_sum + fresh_weight[..., None] * fresh_value
    return (
        top_score.reshape(row_count, -1),
        weight_sum.reshape(row_count, -1),
        mixed_sum.reshape(row_count, -1, head_width),
    )


def gather_kernel(n, x_ref, out_ref, held, send_sem, recv_sem):
    me = lax.axis_index("grp")
    col = lax.axis_index("tp")

    barrier = pltpu.get_barrier_semaphore()

    def greet(k, carry):
        peer = lax.rem(me + k, n)
        pl.semaphore_signal(barrier, inc=1, device_id=(peer, col), device_id_type=MESH)
        return carry

    lax.fori_loop(1, n, greet, 0)
    pl.semaphore_wait(barrier, n - 1)

    def copy_to(k):
        peer = lax.rem(me + k, n)
        return pltpu.make_async_remote_copy(
            src_ref=x_ref,
            dst_ref=held.at[me],
            send_sem=send_sem.at[k],
            recv_sem=recv_sem.at[k],
            device_id=(peer, col),
            device_id_type=MESH,
        )

    def copy_from(k):
        source = lax.rem(me + n - k, n)
        return pltpu.make_async_remote_copy(
            src_ref=x_ref,
            dst_ref=held.at[source],
            send_sem=send_sem.at[k],
            recv_sem=recv_sem.at[k],
            device_id=(source, col),
            device_id_type=MESH,
        )

    def start(k, carry):
        copy_to(k).start()
        return carry

    lax.fori_loop(1, n, start, 0)

    def finish(k, carry):
        copy_to(k).wait_send()
        copy_from(k).wait_recv()
        return carry

    lax.fori_loop(1, n, finish, 0)
    held[me] = x_ref[...]
    out_ref[...] = held[...]


def gather_grp(x, n, cid):
    return pl.pallas_call(
        functools.partial(gather_kernel, n),
        out_shape=jax.ShapeDtypeStruct((n,) + x.shape, x.dtype),
        in_specs=[pl.BlockSpec(memory_space=pltpu.VMEM)],
        out_specs=pl.BlockSpec(memory_space=pltpu.VMEM),
        scratch_shapes=[
            pltpu.VMEM((n,) + x.shape, x.dtype),
            pltpu.SemaphoreType.DMA((n,)),
            pltpu.SemaphoreType.DMA((n,)),
        ],
        compiler_params=pltpu.CompilerParams(collective_id=cid, has_side_effects=True),
    )(x)


def far_first(i, size):
    half = size // 2
    return jnp.where(i % 2 == 0, half + i // 2, half - (i + 1) // 2)


def fanout(ny, nz, me, col, src, dst, send, recv):
    my_y = me // nz
    my_z = me % nz

    def copy(k, peer, slot):
        return pltpu.make_async_remote_copy(
            src_ref=src,
            dst_ref=dst.at[slot],
            send_sem=send.at[k],
            recv_sem=recv.at[k],
            device_id=(peer, col),
            device_id_type=MESH,
        )

    def offsets(k):
        return far_first(k // nz, ny), far_first(k % nz, nz)

    def to(k):
        dy, dz = offsets(k)
        return lax.rem(my_y + dy, ny) * nz + lax.rem(my_z + dz, nz)

    def source(k):
        dy, dz = offsets(k)
        return lax.rem(my_y + ny - dy, ny) * nz + lax.rem(my_z + nz - dz, nz)

    last = ny * nz - 1

    def start(k, carry):
        copy(k, to(k), me).start()
        return carry

    lax.fori_loop(0, last, start, 0)

    def finish():
        def one(k, carry):
            copy(k, to(k), me).wait_send()
            s = source(k)
            copy(k, s, s).wait_recv()
            return carry

        lax.fori_loop(0, last, one, 0)

    return finish


def attend_tile(wide, keys, values, count, fresh_k=None, fresh_v=None):
    rows = wide.shape[0]
    scores = lax.dot_general(
        wide, keys, (((1,), (1,)), ((), ())), preferred_element_type=jnp.float32
    ) * 0.125
    half = rows // 2
    row = lax.broadcasted_iota(jnp.int32, scores.shape, 0)
    lane = lax.broadcasted_iota(jnp.int32, scores.shape, 1)
    position = 2 * lane + jnp.where(row >= half, 1, 0)
    inside = position.astype(jnp.float32) < count
    top = jnp.max(jnp.where(inside, scores, -1e30), axis=1, keepdims=True)
    top = jnp.maximum(top, pltpu.roll(top, half, 0))
    if fresh_k is not None:
        fresh_score = jnp.sum(
            wide.astype(jnp.float32) * fresh_k.astype(jnp.float32), axis=1, keepdims=True
        ) * 0.125
        top = jnp.maximum(top, fresh_score)
    weights = jnp.where(inside, jnp.exp(scores - top), 0.0).astype(jnp.bfloat16)
    total = jnp.sum(weights.astype(jnp.float32), axis=1, keepdims=True)
    total = total + pltpu.roll(total, half, 0)
    both = jnp.dot(weights, values, preferred_element_type=jnp.float32)
    mixed = both + pltpu.roll(pltpu.roll(both, half, 0), 64, 1)
    if fresh_k is not None:
        fresh_w = jnp.exp(fresh_score - top).astype(jnp.bfloat16).astype(jnp.float32)
        total = total + fresh_w
        mixed = mixed + fresh_w * fresh_v
    return top, total, mixed


def pair_rows(top, total, mixed, h):
    lane = lax.broadcasted_iota(jnp.int32, (1, mixed.shape[1]), 1)
    left = lane < 64
    g = 2 * h
    u = jnp.where(left, mixed[g : g + 1, :], mixed[g + 5 : g + 6, :])
    m = jnp.where(left, top[g : g + 1, :], top[g + 1 : g + 2, :])
    l = jnp.where(left, total[g : g + 1, :], total[g + 1 : g + 2, :])
    return u, m, l


def widen(q, heads):
    lane = lax.broadcasted_iota(jnp.int32, (2 * heads, 128), 1)
    row = lax.broadcasted_iota(jnp.int32, (2 * heads, 128), 0)
    low = lane < 64
    wide = jnp.zeros((2 * heads, 128), jnp.float32)
    for h in range(heads // 2):
        a = q[:, h * 128 : (h + 1) * 128]
        turned = pltpu.roll(a, 64, 1)
        g = 2 * h
        wide = jnp.where((row == g) & low, a, wide)
        wide = jnp.where((row == g + 1) & low, turned, wide)
        wide = jnp.where((row == heads + g) & ~low, turned, wide)
        wide = jnp.where((row == heads + g + 1) & ~low, a, wide)
    return wide.astype(jnp.bfloat16)


def whole_kernel(ny, nz, n_tp, slots, lengths_ref, splits_ref, helpers_ref, sent_ref, queries_ref,
                 kv_ref, home_hbm, help_hbm, w_hbm, out_ref, home_ref, help_ref, w_ref, local,
                 got1, got2, back, stat, part, held, send1, recv1, send2, recv2, send3, recv3):
    n = ny * nz
    me = lax.axis_index("grp")
    col = lax.axis_index("tp")
    rows = queries_ref.shape[0]
    heads = queries_ref.shape[1] // 64
    pairs = w_ref.shape[0] // 128
    width = out_ref.shape[1]

    barrier = pltpu.get_barrier_semaphore()

    def greet(k, carry):
        peer = lax.rem(me + k, n)
        pl.semaphore_signal(barrier, inc=1, device_id=(peer, col), device_id_type=MESH)
        return carry

    lax.fori_loop(1, n, greet, 0)
    for k in range(1, n_tp):
        peer = lax.rem(col + k, n_tp)
        pl.semaphore_signal(barrier, inc=1, device_id=(me, peer), device_id_type=MESH)
    loads = [
        pltpu.make_async_copy(hbm, vmem, local.at[i])
        for i, (hbm, vmem) in enumerate(
            [(home_hbm, home_ref), (help_hbm, help_ref), (w_hbm, w_ref)]
        )
    ]
    for load in loads:
        load.start()
    pl.semaphore_wait(barrier, (n - 1) + (n_tp - 1))

    wait1 = fanout(ny, nz, me, col, sent_ref, got1, send1, recv1)
    lane = lax.broadcasted_iota(jnp.int32, (1, 128), 1)
    low = lane < 64
    loads[0].wait()
    for r in range(rows):
        kv = kv_ref[r : r + 1, :].astype(jnp.float32)
        turned = pltpu.roll(kv, 64, 1)
        fresh_k = jnp.where(low, kv, turned).astype(jnp.bfloat16)
        fresh_v = jnp.where(low, turned, kv)
        count = splits_ref[r].astype(jnp.float32)
        top, total, mixed = attend_tile(
            widen(queries_ref[r : r + 1, :].astype(jnp.float32), heads),
            home_ref[r, 0, 0],
            home_ref[r, 1, 0],
            count,
            fresh_k,
            fresh_v,
        )
        for h in range(pairs):
            u, m, l = pair_rows(top, total, mixed, h)
            stat[0, h, r : r + 1, :] = u
            stat[1, h, r : r + 1, :] = m
            stat[2, h, r : r + 1, :] = l
    wait1()
    loads[1].wait()

    partner = helpers_ref[0] // rows
    block = got1[partner]
    pick_row = lax.broadcasted_iota(jnp.int32, (slots, rows), 0)
    pick_col = lax.broadcasted_iota(jnp.int32, (slots, rows), 1)
    pick = jnp.zeros((slots, rows), jnp.float32)
    for k in range(slots):
        pick = jnp.where((pick_row == k) & (pick_col == helpers_ref[k] % rows), 1.0, pick)
    chosen = jnp.dot(pick.astype(jnp.bfloat16), block, preferred_element_type=jnp.float32)
    qw = heads * 64
    for k in range(slots):
        count = chosen[k : k + 1, qw : qw + 1] * 32.0 + chosen[k : k + 1, qw + 1 : qw + 2]
        top, total, mixed = attend_tile(
            widen(chosen[k : k + 1, :qw], heads), help_ref[k, 0, 0], help_ref[k, 1, 0], count
        )
        for h in range(pairs):
            u, m, l = pair_rows(top, total, mixed, h)
            back[k * pairs + h : k * pairs + h + 1, :] = u
            back[(slots + k) * pairs + h : (slots + k) * pairs + h + 1, :] = m
            back[(2 * slots + k) * pairs + h : (2 * slots + k) * pairs + h + 1, :] = l

    wait2 = fanout(ny, nz, me, col, back, got2, send2, recv2)

    sel_row = lax.broadcasted_iota(jnp.int32, (rows, slots), 0)
    sel_col = lax.broadcasted_iota(jnp.int32, (rows, slots), 1)
    fsel = jnp.zeros((rows, slots), jnp.float32)
    rank = jnp.int32(0)
    for r in range(rows):
        is_long = lengths_ref[r] > LONG_AT
        fsel = jnp.where((sel_row == r) & (sel_col == rank) & is_long, 1.0, fsel)
        rank = rank + is_long.astype(jnp.int32)
    has = fsel[:, 0:1]
    for k in range(1, slots):
        has = has + fsel[:, k : k + 1]
    wait2()

    loads[2].wait()
    theirs = got2[partner]
    acc = jnp.zeros(part.shape, jnp.float32)
    for h in range(pairs):

        def pick_far(base):
            x = fsel[:, 0:1] * theirs[base + h : base + h + 1, :]
            for k in range(1, slots):
                r0 = base + k * pairs + h
                x = x + fsel[:, k : k + 1] * theirs[r0 : r0 + 1, :]
            return x

        far_u = pick_far(0)
        far_m = jnp.where(has > 0.0, pick_far(slots * pairs), -1e30)
        far_l = pick_far(2 * slots * pairs)
        home_u = stat[0, h]
        home_m = stat[1, h]
        home_l = stat[2, h]
        top = jnp.maximum(home_m, far_m)
        home_e = jnp.exp(home_m - top)
        far_e = jnp.exp(far_m - top)
        mix = (home_u * home_e + far_u * far_e) / (home_l * home_e + far_l * far_e)
        acc = acc + jnp.dot(
            mix.astype(jnp.bfloat16),
            w_ref[h * 128 : (h + 1) * 128, :],
            preferred_element_type=jnp.float32,
        )
    part[...] = acc

    sends = []
    for k in range(1, n_tp):
        peer = lax.rem(col + k, n_tp)
        cols = pl.ds(pl.multiple_of(peer * width, width), width)
        copy = pltpu.make_async_remote_copy(
            src_ref=part.at[:, cols],
            dst_ref=held.at[k],
            send_sem=send3.at[k],
            recv_sem=recv3.at[k],
            device_id=(me, peer),
            device_id_type=MESH,
        )
        copy.start()
        sends.append(copy)
    own = pl.ds(pl.multiple_of(col * width, width), width)
    total = part[:, own]
    for copy in sends:
        copy.wait_send()
        copy.wait_recv()
    for k in range(1, n_tp):
        total = total + held[k]
    out_ref[...] = total.astype(out_ref.dtype)


def per_device(ny, nz, queries, new_kv, home_cache, help_cache, lengths, split_at, helper_req, out_weight):
    n_grp = lax.axis_size("grp")
    n_tp = lax.axis_size("tp")
    row_count, width = queries.shape
    slots = help_cache.shape[0]
    pairs = width // 128
    lanes = 128

    count = lengths - split_at
    lane = jnp.arange(lanes)[None, :]
    code = jnp.where(
        lane == 0, (count // 32)[:, None], jnp.where(lane == 1, (count % 32)[:, None], 0)
    ).astype(jnp.bfloat16)
    sent = jnp.concatenate([queries, code], axis=1)
    kv = new_kv.reshape(row_count, 2 * new_kv.shape[2])

    out_cols = out_weight.shape[1] // n_tp
    vmem = pl.BlockSpec(memory_space=pltpu.VMEM)
    smem = pl.BlockSpec(memory_space=pltpu.SMEM)
    back_rows = 3 * slots * pairs
    return pl.pallas_call(
        functools.partial(whole_kernel, ny, nz, n_tp, slots),
        out_shape=jax.ShapeDtypeStruct((row_count, out_cols), jnp.bfloat16),
        in_specs=[smem] * 3 + [vmem] * 3 + [pl.BlockSpec(memory_space=pl.ANY)] * 3,
        out_specs=vmem,
        scratch_shapes=[
            pltpu.VMEM(home_cache.shape, home_cache.dtype),
            pltpu.VMEM(help_cache.shape, help_cache.dtype),
            pltpu.VMEM(out_weight.shape, out_weight.dtype),
            pltpu.SemaphoreType.DMA((3,)),
            pltpu.VMEM((n_grp,) + sent.shape, jnp.bfloat16),
            pltpu.VMEM((n_grp, back_rows, lanes), jnp.float32),
            pltpu.VMEM((back_rows, lanes), jnp.float32),
            pltpu.VMEM((3, pairs, row_count, lanes), jnp.float32),
            pltpu.VMEM((row_count, out_weight.shape[1]), jnp.float32),
            pltpu.VMEM((n_tp, row_count, out_cols), jnp.float32),
            pltpu.SemaphoreType.DMA((n_grp,)),
            pltpu.SemaphoreType.DMA((n_grp,)),
            pltpu.SemaphoreType.DMA((n_grp,)),
            pltpu.SemaphoreType.DMA((n_grp,)),
            pltpu.SemaphoreType.DMA((n_tp,)),
            pltpu.SemaphoreType.DMA((n_tp,)),
        ],
        compiler_params=pltpu.CompilerParams(collective_id=0, has_side_effects=True),
    )(lengths, split_at, helper_req, sent, queries, kv, home_cache, help_cache, out_weight)


def grp_rows(mesh):
    column = list(mesh.devices[:, 0])
    n = len(column)
    coords = [getattr(d, "coords", None) for d in column]
    if coords[0] is not None:
        nz = 1
        while nz < n and coords[nz][1] == coords[0][1]:
            nz += 1
    else:
        nz = 1
        while nz * nz < n:
            nz *= 2
    return n // nz, nz


def solution(mesh):
    ny, nz = grp_rows(mesh)
    return jax.shard_map(
        functools.partial(per_device, ny, nz),
        mesh=mesh,
        in_specs=(
            P("grp", "tp"),
            P("grp", None, "tp"),
            P("grp", None, "tp", None, None),
            P("grp", None, "tp", None, None),
            P("grp"),
            P("grp"),
            P("grp"),
            P("tp", None),
        ),
        out_specs=P("grp", "tp"),
        check_vma=False,
    )
```

```python
import functools

import jax
import jax.numpy as jnp
from jax import lax
from jax.experimental import pallas as pl
from jax.experimental.pallas import tpu as pltpu
from jax.sharding import PartitionSpec as P

MESH = pl.DeviceIdType.MESH
LONG_AT = 1024


def attend(queries, cache, count, fresh):
    row_count = queries.shape[0]
    kv_heads = cache.shape[2]
    head_width = cache.shape[4] // 2
    half = cache.shape[3]
    group_size = queries.shape[1] // (kv_heads * head_width)
    score_scale = head_width ** (-0.5)
    head_rows = queries.reshape(row_count, kv_heads, group_size, head_width)
    blank = jnp.zeros_like(head_rows)
    wide_rows = jnp.stack(
        [
            jnp.concatenate([head_rows, blank], axis=-1),
            jnp.concatenate([blank, head_rows], axis=-1),
        ],
        axis=3,
    )
    key_rows = cache[:, 0]
    value_rows = cache[:, 1]
    scores = (
        jnp.einsum("nkgjc,nkpc->nkgjp", wide_rows, key_rows, preferred_element_type=jnp.float32)
        * score_scale
    )
    position = 2 * jnp.arange(half)[None, :] + jnp.arange(2)[:, None]
    inside = (position[None] < count[:, None, None])[:, None, None]
    top_score = jnp.max(jnp.where(inside, scores, -1e30), axis=(-2, -1))
    if fresh is not None:
        fresh_key = fresh[:, 0].reshape(row_count, kv_heads, head_width)
        fresh_score = (
            jnp.einsum("nkgd,nkd->nkg", head_rows, fresh_key, preferred_element_type=jnp.float32)
            * score_scale
        )
        top_score = jnp.maximum(top_score, fresh_score)
    weights = jnp.where(
        inside, jnp.exp(scores - top_score[..., None, None]), 0.0
    ).astype(jnp.bfloat16)
    weight_sum = jnp.sum(weights.astype(jnp.float32), axis=(-2, -1))
    both = jnp.einsum(
        "nkgjp,nkpc->nkgjc", weights, value_rows, preferred_element_type=jnp.float32
    )
    mixed_sum = both[..., 0, :head_width] + both[..., 1, head_width:]
    if fresh is not None:
        fresh_weight = lax.optimization_barrier(
            jnp.exp(fresh_score - top_score).astype(jnp.bfloat16)
        ).astype(jnp.float32)
        weight_sum = weight_sum + fresh_weight
        fresh_value = fresh[:, 1].reshape(row_count, kv_heads, 1, head_width).astype(jnp.float32)
        mixed_sum = mixed_sum + fresh_weight[..., None] * fresh_value
    return (
        top_score.reshape(row_count, -1),
        weight_sum.reshape(row_count, -1),
        mixed_sum.reshape(row_count, -1, head_width),
    )


def gather_kernel(n, x_ref, out_ref, held, send_sem, recv_sem):
    me = lax.axis_index("grp")
    col = lax.axis_index("tp")

    barrier = pltpu.get_barrier_semaphore()

    def greet(k, carry):
        peer = lax.rem(me + k, n)
        pl.semaphore_signal(barrier, inc=1, device_id=(peer, col), device_id_type=MESH)
        return carry

    lax.fori_loop(1, n, greet, 0)
    pl.semaphore_wait(barrier, n - 1)

    def copy_to(k):
        peer = lax.rem(me + k, n)
        return pltpu.make_async_remote_copy(
            src_ref=x_ref,
            dst_ref=held.at[me],
            send_sem=send_sem.at[k],
            recv_sem=recv_sem.at[k],
            device_id=(peer, col),
            device_id_type=MESH,
        )

    def copy_from(k):
        source = lax.rem(me + n - k, n)
        return pltpu.make_async_remote_copy(
            src_ref=x_ref,
            dst_ref=held.at[source],
            send_sem=send_sem.at[k],
            recv_sem=recv_sem.at[k],
            device_id=(source, col),
            device_id_type=MESH,
        )

    def start(k, carry):
        copy_to(k).start()
        return carry

    lax.fori_loop(1, n, start, 0)

    def finish(k, carry):
        copy_to(k).wait_send()
        copy_from(k).wait_recv()
        return carry

    lax.fori_loop(1, n, finish, 0)
    held[me] = x_ref[...]
    out_ref[...] = held[...]


def gather_grp(x, n, cid):
    return pl.pallas_call(
        functools.partial(gather_kernel, n),
        out_shape=jax.ShapeDtypeStruct((n,) + x.shape, x.dtype),
        in_specs=[pl.BlockSpec(memory_space=pltpu.VMEM)],
        out_specs=pl.BlockSpec(memory_space=pltpu.VMEM),
        scratch_shapes=[
            pltpu.VMEM((n,) + x.shape, x.dtype),
            pltpu.SemaphoreType.DMA((n,)),
            pltpu.SemaphoreType.DMA((n,)),
        ],
        compiler_params=pltpu.CompilerParams(collective_id=cid, has_side_effects=True),
    )(x)


def far_first(i, size):
    half = size // 2
    return jnp.where(i % 2 == 0, half + i // 2, half - (i + 1) // 2)


def fanout(ny, nz, me, col, src, dst, send, recv):
    my_y = me // nz
    my_z = me % nz

    def copy(k, peer, slot):
        return pltpu.make_async_remote_copy(
            src_ref=src,
            dst_ref=dst.at[slot],
            send_sem=send.at[k],
            recv_sem=recv.at[k],
            device_id=(peer, col),
            device_id_type=MESH,
        )

    def offsets(k):
        return far_first(k // nz, ny), far_first(k % nz, nz)

    def to(k):
        dy, dz = offsets(k)
        return lax.rem(my_y + dy, ny) * nz + lax.rem(my_z + dz, nz)

    def source(k):
        dy, dz = offsets(k)
        return lax.rem(my_y + ny - dy, ny) * nz + lax.rem(my_z + nz - dz, nz)

    last = ny * nz - 1

    def start(k, carry):
        copy(k, to(k), me).start()
        return carry

    lax.fori_loop(0, last, start, 0)

    def finish():
        def one(k, carry):
            copy(k, to(k), me).wait_send()
            s = source(k)
            copy(k, s, s).wait_recv()
            return carry

        lax.fori_loop(0, last, one, 0)

    return finish


def attend_tile(wide, keys, values, count, fresh_k=None, fresh_v=None):
    rows = wide.shape[0]
    scores = lax.dot_general(
        wide, keys, (((1,), (1,)), ((), ())), preferred_element_type=jnp.float32
    ) * 0.125
    half = rows // 2
    row = lax.broadcasted_iota(jnp.int32, scores.shape, 0)
    lane = lax.broadcasted_iota(jnp.int32, scores.shape, 1)
    position = 2 * lane + jnp.where(row >= half, 1, 0)
    inside = position.astype(jnp.float32) < count
    top = jnp.max(jnp.where(inside, scores, -1e30), axis=1, keepdims=True)
    top = jnp.maximum(top, pltpu.roll(top, half, 0))
    if fresh_k is not None:
        fresh_score = jnp.sum(
            wide.astype(jnp.float32) * fresh_k.astype(jnp.float32), axis=1, keepdims=True
        ) * 0.125
        top = jnp.maximum(top, fresh_score)
    weights = jnp.where(inside, jnp.exp(scores - top), 0.0).astype(jnp.bfloat16)
    total = jnp.sum(weights.astype(jnp.float32), axis=1, keepdims=True)
    total = total + pltpu.roll(total, half, 0)
    both = jnp.dot(weights, values, preferred_element_type=jnp.float32)
    mixed = both + pltpu.roll(pltpu.roll(both, half, 0), 64, 1)
    if fresh_k is not None:
        fresh_w = jnp.exp(fresh_score - top).astype(jnp.bfloat16).astype(jnp.float32)
        total = total + fresh_w
        mixed = mixed + fresh_w * fresh_v
    return top, total, mixed


def pair_rows(top, total, mixed, h):
    lane = lax.broadcasted_iota(jnp.int32, (1, mixed.shape[1]), 1)
    left = lane < 64
    g = 2 * h
    u = jnp.where(left, mixed[g : g + 1, :], mixed[g + 5 : g + 6, :])
    m = jnp.where(left, top[g : g + 1, :], top[g + 1 : g + 2, :])
    l = jnp.where(left, total[g : g + 1, :], total[g + 1 : g + 2, :])
    return u, m, l


def widen(q, heads):
    lane = lax.broadcasted_iota(jnp.int32, (2 * heads, 128), 1)
    row = lax.broadcasted_iota(jnp.int32, (2 * heads, 128), 0)
    low = lane < 64
    wide = jnp.zeros((2 * heads, 128), jnp.float32)
    for h in range(heads // 2):
        a = q[:, h * 128 : (h + 1) * 128]
        turned = pltpu.roll(a, 64, 1)
        g = 2 * h
        wide = jnp.where((row == g) & low, a, wide)
        wide = jnp.where((row == g + 1) & low, turned, wide)
        wide = jnp.where((row == heads + g) & ~low, turned, wide)
        wide = jnp.where((row == heads + g + 1) & ~low, a, wide)
    return wide.astype(jnp.bfloat16)


def whole_kernel(ny, nz, n_tp, slots, lengths_ref, splits_ref, helpers_ref, sent_ref, kv_ref, home_hbm, help_hbm, w_hbm, out_ref, home_ref, help_ref, w_ref, local,
                 got1, got2, back, stat, part, held, send1, recv1, send2, recv2, send3, recv3):
    n = ny * nz
    me = lax.axis_index("grp")
    col = lax.axis_index("tp")
    rows = sent_ref.shape[0]
    heads = w_ref.shape[0] // 64
    qw = heads * 64
    pairs = w_ref.shape[0] // 128
    width = out_ref.shape[1]

    barrier = pltpu.get_barrier_semaphore()

    def greet(k, carry):
        peer = lax.rem(me + k, n)
        pl.semaphore_signal(barrier, inc=1, device_id=(peer, col), device_id_type=MESH)
        return carry

    lax.fori_loop(1, n, greet, 0)
    for k in range(1, n_tp):
        peer = lax.rem(col + k, n_tp)
        pl.semaphore_signal(barrier, inc=1, device_id=(me, peer), device_id_type=MESH)
    loads = [
        pltpu.make_async_copy(hbm, vmem, local.at[i])
        for i, (hbm, vmem) in enumerate(
            [(home_hbm, home_ref), (help_hbm, help_ref), (w_hbm, w_ref)]
        )
    ]
    for load in loads:
        load.start()
    pl.semaphore_wait(barrier, (n - 1) + (n_tp - 1))

    wait1 = fanout(ny, nz, me, col, sent_ref, got1, send1, recv1)
    lane = lax.broadcasted_iota(jnp.int32, (1, 128), 1)
    low = lane < 64
    loads[0].wait()
    for r in range(rows):
        key = kv_ref[r, 0:1, :].astype(jnp.float32)
        value = kv_ref[r, 1:2, :].astype(jnp.float32)
        fresh_k = jnp.concatenate([key, key], axis=1).astype(jnp.bfloat16)
        fresh_v = jnp.concatenate([value, value], axis=1)
        count = splits_ref[r].astype(jnp.float32)
        top, total, mixed = attend_tile(
            widen(sent_ref[r : r + 1, :qw].astype(jnp.float32), heads),
            home_ref[r, 0, 0],
            home_ref[r, 1, 0],
            count,
            fresh_k,
            fresh_v,
        )
        for h in range(pairs):
            u, m, l = pair_rows(top, total, mixed, h)
            stat[0, h, r : r + 1, :] = u
            stat[1, h, r : r + 1, :] = m
            stat[2, h, r : r + 1, :] = l
    wait1()
    loads[1].wait()

    partner = helpers_ref[0] // rows
    block = got1[partner]
    pick_row = lax.broadcasted_iota(jnp.int32, (slots, rows), 0)
    pick_col = lax.broadcasted_iota(jnp.int32, (slots, rows), 1)
    pick = jnp.zeros((slots, rows), jnp.float32)
    for k in range(slots):
        pick = jnp.where((pick_row == k) & (pick_col == helpers_ref[k] % rows), 1.0, pick)
    chosen = jnp.dot(pick.astype(jnp.bfloat16), block, preferred_element_type=jnp.float32)
    for k in range(slots):
        count = chosen[k : k + 1, qw : qw + 1] * 32.0 + chosen[k : k + 1, qw + 1 : qw + 2]
        top, total, mixed = attend_tile(
            widen(chosen[k : k + 1, :qw], heads), help_ref[k, 0, 0], help_ref[k, 1, 0], count
        )
        for h in range(pairs):
            u, m, l = pair_rows(top, total, mixed, h)
            back[k * pairs + h : k * pairs + h + 1, :] = u
            back[(slots + k) * pairs + h : (slots + k) * pairs + h + 1, :] = m
            back[(2 * slots + k) * pairs + h : (2 * slots + k) * pairs + h + 1, :] = l

    wait2 = fanout(ny, nz, me, col, back, got2, send2, recv2)

    sel_row = lax.broadcasted_iota(jnp.int32, (rows, slots), 0)
    sel_col = lax.broadcasted_iota(jnp.int32, (rows, slots), 1)
    fsel = jnp.zeros((rows, slots), jnp.float32)
    rank = jnp.int32(0)
    for r in range(rows):
        is_long = lengths_ref[r] > LONG_AT
        fsel = jnp.where((sel_row == r) & (sel_col == rank) & is_long, 1.0, fsel)
        rank = rank + is_long.astype(jnp.int32)
    has = fsel[:, 0:1]
    for k in range(1, slots):
        has = has + fsel[:, k : k + 1]
    wait2()

    loads[2].wait()
    theirs = got2[partner]
    acc = jnp.zeros(part.shape, jnp.float32)
    for h in range(pairs):

        def pick_far(base):
            x = fsel[:, 0:1] * theirs[base + h : base + h + 1, :]
            for k in range(1, slots):
                r0 = base + k * pairs + h
                x = x + fsel[:, k : k + 1] * theirs[r0 : r0 + 1, :]
            return x

        far_u = pick_far(0)
        far_m = jnp.where(has > 0.0, pick_far(slots * pairs), -1e30)
        far_l = pick_far(2 * slots * pairs)
        home_u = stat[0, h]
        home_m = stat[1, h]
        home_l = stat[2, h]
        top = jnp.maximum(home_m, far_m)
        home_e = jnp.exp(home_m - top)
        far_e = jnp.exp(far_m - top)
        mix = (home_u * home_e + far_u * far_e) / (home_l * home_e + far_l * far_e)
        acc = acc + jnp.dot(
            mix.astype(jnp.bfloat16),
            w_ref[h * 128 : (h + 1) * 128, :],
            preferred_element_type=jnp.float32,
        )
    part[...] = acc

    sends = []
    for k in range(1, n_tp):
        peer = lax.rem(col + k, n_tp)
        cols = pl.ds(pl.multiple_of(peer * width, width), width)
        copy = pltpu.make_async_remote_copy(
            src_ref=part.at[:, cols],
            dst_ref=held.at[k],
            send_sem=send3.at[k],
            recv_sem=recv3.at[k],
            device_id=(me, peer),
            device_id_type=MESH,
        )
        copy.start()
        sends.append(copy)
    own = pl.ds(pl.multiple_of(col * width, width), width)
    total = part[:, own]
    for copy in sends:
        copy.wait_send()
        copy.wait_recv()
    for k in range(1, n_tp):
        total = total + held[k]
    out_ref[...] = total.astype(out_ref.dtype)


def per_device(ny, nz, queries, new_kv, home_cache, help_cache, lengths, split_at, helper_req, out_weight):
    n_grp = lax.axis_size("grp")
    n_tp = lax.axis_size("tp")
    row_count, width = queries.shape
    slots = help_cache.shape[0]
    pairs = width // 128
    lanes = 128

    count = lengths - split_at
    lane = jnp.arange(lanes)[None, :]
    code = jnp.where(
        lane == 0, (count // 32)[:, None], jnp.where(lane == 1, (count % 32)[:, None], 0)
    ).astype(jnp.bfloat16)
    sent = jnp.concatenate([queries, code], axis=1)

    out_cols = out_weight.shape[1] // n_tp
    vmem = pl.BlockSpec(memory_space=pltpu.VMEM)
    smem = pl.BlockSpec(memory_space=pltpu.SMEM)
    back_rows = 3 * slots * pairs
    return pl.pallas_call(
        functools.partial(whole_kernel, ny, nz, n_tp, slots),
        out_shape=jax.ShapeDtypeStruct((row_count, out_cols), jnp.bfloat16),
        in_specs=[smem] * 3 + [vmem] * 2 + [pl.BlockSpec(memory_space=pl.ANY)] * 3,
        out_specs=vmem,
        scratch_shapes=[
            pltpu.VMEM(home_cache.shape, home_cache.dtype),
            pltpu.VMEM(help_cache.shape, help_cache.dtype),
            pltpu.VMEM(out_weight.shape, out_weight.dtype),
            pltpu.SemaphoreType.DMA((3,)),
            pltpu.VMEM((n_grp,) + sent.shape, jnp.bfloat16),
            pltpu.VMEM((n_grp, back_rows, lanes), jnp.float32),
            pltpu.VMEM((back_rows, lanes), jnp.float32),
            pltpu.VMEM((3, pairs, row_count, lanes), jnp.float32),
            pltpu.VMEM((row_count, out_weight.shape[1]), jnp.float32),
            pltpu.VMEM((n_tp, row_count, out_cols), jnp.float32),
            pltpu.SemaphoreType.DMA((n_grp,)),
            pltpu.SemaphoreType.DMA((n_grp,)),
            pltpu.SemaphoreType.DMA((n_grp,)),
            pltpu.SemaphoreType.DMA((n_grp,)),
            pltpu.SemaphoreType.DMA((n_tp,)),
            pltpu.SemaphoreType.DMA((n_tp,)),
        ],
        compiler_params=pltpu.CompilerParams(collective_id=0, has_side_effects=True),
    )(lengths, split_at, helper_req, sent, new_kv, home_cache, help_cache, out_weight)


def grp_rows(mesh):
    column = list(mesh.devices[:, 0])
    n = len(column)
    coords = [getattr(d, "coords", None) for d in column]
    if coords[0] is not None:
        nz = 1
        while nz < n and coords[nz][1] == coords[0][1]:
            nz += 1
    else:
        nz = 1
        while nz * nz < n:
            nz *= 2
    return n // nz, nz


def solution(mesh):
    ny, nz = grp_rows(mesh)
    return jax.shard_map(
        functools.partial(per_device, ny, nz),
        mesh=mesh,
        in_specs=(
            P("grp", "tp"),
            P("grp", None, "tp"),
            P("grp", None, "tp", None, None),
            P("grp", None, "tp", None, None),
            P("grp"),
            P("grp"),
            P("grp"),
            P("tp", None),
        ),
        out_specs=P("grp", "tp"),
        check_vma=False,
    )
```

```python
import functools

import jax
import jax.numpy as jnp
from jax import lax
from jax.experimental import pallas as pl
from jax.experimental.pallas import tpu as pltpu
from jax.sharding import PartitionSpec as P

MESH = pl.DeviceIdType.MESH
LONG_AT = 1024


def attend(queries, cache, count, fresh):
    row_count = queries.shape[0]
    kv_heads = cache.shape[2]
    head_width = cache.shape[4] // 2
    half = cache.shape[3]
    group_size = queries.shape[1] // (kv_heads * head_width)
    score_scale = head_width ** (-0.5)
    head_rows = queries.reshape(row_count, kv_heads, group_size, head_width)
    blank = jnp.zeros_like(head_rows)
    wide_rows = jnp.stack(
        [
            jnp.concatenate([head_rows, blank], axis=-1),
            jnp.concatenate([blank, head_rows], axis=-1),
        ],
        axis=3,
    )
    key_rows = cache[:, 0]
    value_rows = cache[:, 1]
    scores = (
        jnp.einsum("nkgjc,nkpc->nkgjp", wide_rows, key_rows, preferred_element_type=jnp.float32)
        * score_scale
    )
    position = 2 * jnp.arange(half)[None, :] + jnp.arange(2)[:, None]
    inside = (position[None] < count[:, None, None])[:, None, None]
    top_score = jnp.max(jnp.where(inside, scores, -1e30), axis=(-2, -1))
    if fresh is not None:
        fresh_key = fresh[:, 0].reshape(row_count, kv_heads, head_width)
        fresh_score = (
            jnp.einsum("nkgd,nkd->nkg", head_rows, fresh_key, preferred_element_type=jnp.float32)
            * score_scale
        )
        top_score = jnp.maximum(top_score, fresh_score)
    weights = jnp.where(
        inside, jnp.exp(scores - top_score[..., None, None]), 0.0
    ).astype(jnp.bfloat16)
    weight_sum = jnp.sum(weights.astype(jnp.float32), axis=(-2, -1))
    both = jnp.einsum(
        "nkgjp,nkpc->nkgjc", weights, value_rows, preferred_element_type=jnp.float32
    )
    mixed_sum = both[..., 0, :head_width] + both[..., 1, head_width:]
    if fresh is not None:
        fresh_weight = lax.optimization_barrier(
            jnp.exp(fresh_score - top_score).astype(jnp.bfloat16)
        ).astype(jnp.float32)
        weight_sum = weight_sum + fresh_weight
        fresh_value = fresh[:, 1].reshape(row_count, kv_heads, 1, head_width).astype(jnp.float32)
        mixed_sum = mixed_sum + fresh_weight[..., None] * fresh_value
    return (
        top_score.reshape(row_count, -1),
        weight_sum.reshape(row_count, -1),
        mixed_sum.reshape(row_count, -1, head_width),
    )


def gather_kernel(n, x_ref, out_ref, held, send_sem, recv_sem):
    me = lax.axis_index("grp")
    col = lax.axis_index("tp")

    barrier = pltpu.get_barrier_semaphore()

    def greet(k, carry):
        peer = lax.rem(me + k, n)
        pl.semaphore_signal(barrier, inc=1, device_id=(peer, col), device_id_type=MESH)
        return carry

    lax.fori_loop(1, n, greet, 0)
    pl.semaphore_wait(barrier, n - 1)

    def copy_to(k):
        peer = lax.rem(me + k, n)
        return pltpu.make_async_remote_copy(
            src_ref=x_ref,
            dst_ref=held.at[me],
            send_sem=send_sem.at[k],
            recv_sem=recv_sem.at[k],
            device_id=(peer, col),
            device_id_type=MESH,
        )

    def copy_from(k):
        source = lax.rem(me + n - k, n)
        return pltpu.make_async_remote_copy(
            src_ref=x_ref,
            dst_ref=held.at[source],
            send_sem=send_sem.at[k],
            recv_sem=recv_sem.at[k],
            device_id=(source, col),
            device_id_type=MESH,
        )

    def start(k, carry):
        copy_to(k).start()
        return carry

    lax.fori_loop(1, n, start, 0)

    def finish(k, carry):
        copy_to(k).wait_send()
        copy_from(k).wait_recv()
        return carry

    lax.fori_loop(1, n, finish, 0)
    held[me] = x_ref[...]
    out_ref[...] = held[...]


def gather_grp(x, n, cid):
    return pl.pallas_call(
        functools.partial(gather_kernel, n),
        out_shape=jax.ShapeDtypeStruct((n,) + x.shape, x.dtype),
        in_specs=[pl.BlockSpec(memory_space=pltpu.VMEM)],
        out_specs=pl.BlockSpec(memory_space=pltpu.VMEM),
        scratch_shapes=[
            pltpu.VMEM((n,) + x.shape, x.dtype),
            pltpu.SemaphoreType.DMA((n,)),
            pltpu.SemaphoreType.DMA((n,)),
        ],
        compiler_params=pltpu.CompilerParams(collective_id=cid, has_side_effects=True),
    )(x)


def far_first(i, size):
    half = size // 2
    return half + i // 2 if i % 2 == 0 else half - (i + 1) // 2


def fanout(ny, nz, me, col, src, dst, send, recv):
    my_y = me // nz
    my_z = me % nz
    order = [(far_first(a, ny), far_first(b, nz)) for a in range(ny) for b in range(nz)][:-1]

    def copy(k, peer, slot):
        return pltpu.make_async_remote_copy(
            src_ref=src,
            dst_ref=dst.at[slot],
            send_sem=send.at[k],
            recv_sem=recv.at[k],
            device_id=(peer, col),
            device_id_type=MESH,
        )

    targets = []
    for k, (dy, dz) in enumerate(order):
        peer = lax.rem(my_y + dy, ny) * nz + lax.rem(my_z + dz, nz)
        out = copy(k, peer, me)
        out.start()
        targets.append(out)

    def finish():
        for k, (dy, dz) in enumerate(order):
            targets[k].wait_send()
            source = lax.rem(my_y + (ny - dy), ny) * nz + lax.rem(my_z + (nz - dz), nz)
            copy(k, source, source).wait_recv()

    return finish


def attend_tile(wide, keys, values, count, fresh_k=None, fresh_v=None):
    rows = wide.shape[0]
    scores = lax.dot_general(
        wide, keys, (((1,), (1,)), ((), ())), preferred_element_type=jnp.float32
    ) * 0.125
    half = rows // 2
    row = lax.broadcasted_iota(jnp.int32, scores.shape, 0)
    lane = lax.broadcasted_iota(jnp.int32, scores.shape, 1)
    position = 2 * lane + jnp.where(row >= half, 1, 0)
    inside = position.astype(jnp.float32) < count
    top = jnp.max(jnp.where(inside, scores, -1e30), axis=1, keepdims=True)
    top = jnp.maximum(top, pltpu.roll(top, half, 0))
    if fresh_k is not None:
        fresh_score = jnp.sum(
            wide.astype(jnp.float32) * fresh_k.astype(jnp.float32), axis=1, keepdims=True
        ) * 0.125
        top = jnp.maximum(top, fresh_score)
    weights = jnp.where(inside, jnp.exp(scores - top), 0.0).astype(jnp.bfloat16)
    total = jnp.sum(weights.astype(jnp.float32), axis=1, keepdims=True)
    total = total + pltpu.roll(total, half, 0)
    both = jnp.dot(weights, values, preferred_element_type=jnp.float32)
    mixed = both + pltpu.roll(pltpu.roll(both, half, 0), 64, 1)
    if fresh_k is not None:
        fresh_w = jnp.exp(fresh_score - top).astype(jnp.bfloat16).astype(jnp.float32)
        total = total + fresh_w
        mixed = mixed + fresh_w * fresh_v
    return top, total, mixed


def pair_rows(top, total, mixed, h):
    lane = lax.broadcasted_iota(jnp.int32, (1, mixed.shape[1]), 1)
    left = lane < 64
    g = 2 * h
    u = jnp.where(left, mixed[g : g + 1, :], mixed[g + 5 : g + 6, :])
    m = jnp.where(left, top[g : g + 1, :], top[g + 1 : g + 2, :])
    l = jnp.where(left, total[g : g + 1, :], total[g + 1 : g + 2, :])
    return u, m, l


def widen(q, heads):
    lane = lax.broadcasted_iota(jnp.int32, (2 * heads, 128), 1)
    row = lax.broadcasted_iota(jnp.int32, (2 * heads, 128), 0)
    low = lane < 64
    wide = jnp.zeros((2 * heads, 128), jnp.float32)
    for h in range(heads // 2):
        a = q[:, h * 128 : (h + 1) * 128]
        turned = pltpu.roll(a, 64, 1)
        g = 2 * h
        wide = jnp.where((row == g) & low, a, wide)
        wide = jnp.where((row == g + 1) & low, turned, wide)
        wide = jnp.where((row == heads + g) & ~low, turned, wide)
        wide = jnp.where((row == heads + g + 1) & ~low, a, wide)
    return wide.astype(jnp.bfloat16)


def whole_kernel(ny, nz, n_tp, slots, lengths_ref, splits_ref, helpers_ref, sent_ref, kv_ref, home_hbm, help_hbm, w_hbm, out_ref, home_ref, help_ref, w_ref, local,
                 got1, got2, back, stat, part, held, send1, recv1, send2, recv2, send3, recv3):
    n = ny * nz
    me = lax.axis_index("grp")
    col = lax.axis_index("tp")
    rows = sent_ref.shape[0]
    heads = w_ref.shape[0] // 64
    qw = heads * 64
    pairs = w_ref.shape[0] // 128
    width = out_ref.shape[1]

    barrier = pltpu.get_barrier_semaphore()

    def greet(k, carry):
        peer = lax.rem(me + k, n)
        pl.semaphore_signal(barrier, inc=1, device_id=(peer, col), device_id_type=MESH)
        return carry

    lax.fori_loop(1, n, greet, 0)
    for k in range(1, n_tp):
        peer = lax.rem(col + k, n_tp)
        pl.semaphore_signal(barrier, inc=1, device_id=(me, peer), device_id_type=MESH)
    loads = [
        pltpu.make_async_copy(hbm, vmem, local.at[i])
        for i, (hbm, vmem) in enumerate(
            [(home_hbm, home_ref), (help_hbm, help_ref), (w_hbm, w_ref)]
        )
    ]
    for load in loads:
        load.start()
    pl.semaphore_wait(barrier, (n - 1) + (n_tp - 1))

    wait1 = fanout(ny, nz, me, col, sent_ref, got1, send1, recv1)
    lane = lax.broadcasted_iota(jnp.int32, (1, 128), 1)
    low = lane < 64
    loads[0].wait()
    for r in range(rows):
        key = kv_ref[r, 0:1, :].astype(jnp.float32)
        value = kv_ref[r, 1:2, :].astype(jnp.float32)
        fresh_k = jnp.concatenate([key, key], axis=1).astype(jnp.bfloat16)
        fresh_v = jnp.concatenate([value, value], axis=1)
        count = splits_ref[r].astype(jnp.float32)
        top, total, mixed = attend_tile(
            widen(sent_ref[r : r + 1, :qw].astype(jnp.float32), heads),
            home_ref[r, 0, 0],
            home_ref[r, 1, 0],
            count,
            fresh_k,
            fresh_v,
        )
        for h in range(pairs):
            u, m, l = pair_rows(top, total, mixed, h)
            stat[0, h, r : r + 1, :] = u
            stat[1, h, r : r + 1, :] = m
            stat[2, h, r : r + 1, :] = l
    wait1()
    loads[1].wait()

    partner = helpers_ref[0] // rows
    block = got1[partner]
    pick_row = lax.broadcasted_iota(jnp.int32, (slots, rows), 0)
    pick_col = lax.broadcasted_iota(jnp.int32, (slots, rows), 1)
    pick = jnp.zeros((slots, rows), jnp.float32)
    for k in range(slots):
        pick = jnp.where((pick_row == k) & (pick_col == helpers_ref[k] % rows), 1.0, pick)
    chosen = jnp.dot(pick.astype(jnp.bfloat16), block, preferred_element_type=jnp.float32)
    for k in range(slots):
        count = chosen[k : k + 1, qw : qw + 1] * 32.0 + chosen[k : k + 1, qw + 1 : qw + 2]
        top, total, mixed = attend_tile(
            widen(chosen[k : k + 1, :qw], heads), help_ref[k, 0, 0], help_ref[k, 1, 0], count
        )
        for h in range(pairs):
            u, m, l = pair_rows(top, total, mixed, h)
            back[k * pairs + h : k * pairs + h + 1, :] = u
            back[(slots + k) * pairs + h : (slots + k) * pairs + h + 1, :] = m
            back[(2 * slots + k) * pairs + h : (2 * slots + k) * pairs + h + 1, :] = l

    wait2 = fanout(ny, nz, me, col, back, got2, send2, recv2)

    sel_row = lax.broadcasted_iota(jnp.int32, (rows, slots), 0)
    sel_col = lax.broadcasted_iota(jnp.int32, (rows, slots), 1)
    fsel = jnp.zeros((rows, slots), jnp.float32)
    rank = jnp.int32(0)
    for r in range(rows):
        is_long = lengths_ref[r] > LONG_AT
        fsel = jnp.where((sel_row == r) & (sel_col == rank) & is_long, 1.0, fsel)
        rank = rank + is_long.astype(jnp.int32)
    has = fsel[:, 0:1]
    for k in range(1, slots):
        has = has + fsel[:, k : k + 1]
    wait2()

    loads[2].wait()
    theirs = got2[partner]
    acc = jnp.zeros(part.shape, jnp.float32)
    for h in range(pairs):

        def pick_far(base):
            x = fsel[:, 0:1] * theirs[base + h : base + h + 1, :]
            for k in range(1, slots):
                r0 = base + k * pairs + h
                x = x + fsel[:, k : k + 1] * theirs[r0 : r0 + 1, :]
            return x

        far_u = pick_far(0)
        far_m = jnp.where(has > 0.0, pick_far(slots * pairs), -1e30)
        far_l = pick_far(2 * slots * pairs)
        home_u = stat[0, h]
        home_m = stat[1, h]
        home_l = stat[2, h]
        top = jnp.maximum(home_m, far_m)
        home_e = jnp.exp(home_m - top)
        far_e = jnp.exp(far_m - top)
        mix = (home_u * home_e + far_u * far_e) / (home_l * home_e + far_l * far_e)
        acc = acc + jnp.dot(
            mix.astype(jnp.bfloat16),
            w_ref[h * 128 : (h + 1) * 128, :],
            preferred_element_type=jnp.float32,
        )
    part[...] = acc

    sends = []
    for k in range(1, n_tp):
        peer = lax.rem(col + k, n_tp)
        cols = pl.ds(pl.multiple_of(peer * width, width), width)
        copy = pltpu.make_async_remote_copy(
            src_ref=part.at[:, cols],
            dst_ref=held.at[k],
            send_sem=send3.at[k],
            recv_sem=recv3.at[k],
            device_id=(me, peer),
            device_id_type=MESH,
        )
        copy.start()
        sends.append(copy)
    own = pl.ds(pl.multiple_of(col * width, width), width)
    total = part[:, own]
    for copy in sends:
        copy.wait_send()
        copy.wait_recv()
    for k in range(1, n_tp):
        total = total + held[k]
    out_ref[...] = total.astype(out_ref.dtype)


def per_device(ny, nz, queries, new_kv, home_cache, help_cache, lengths, split_at, helper_req, out_weight):
    n_grp = lax.axis_size("grp")
    n_tp = lax.axis_size("tp")
    row_count, width = queries.shape
    slots = help_cache.shape[0]
    pairs = width // 128
    lanes = 128

    count = lengths - split_at
    lane = jnp.arange(lanes)[None, :]
    code = jnp.where(
        lane == 0, (count // 32)[:, None], jnp.where(lane == 1, (count % 32)[:, None], 0)
    ).astype(jnp.bfloat16)
    sent = jnp.concatenate([queries, code], axis=1)

    out_cols = out_weight.shape[1] // n_tp
    vmem = pl.BlockSpec(memory_space=pltpu.VMEM)
    smem = pl.BlockSpec(memory_space=pltpu.SMEM)
    back_rows = 3 * slots * pairs
    return pl.pallas_call(
        functools.partial(whole_kernel, ny, nz, n_tp, slots),
        out_shape=jax.ShapeDtypeStruct((row_count, out_cols), jnp.bfloat16),
        in_specs=[smem] * 3 + [vmem] * 2 + [pl.BlockSpec(memory_space=pl.ANY)] * 3,
        out_specs=vmem,
        scratch_shapes=[
            pltpu.VMEM(home_cache.shape, home_cache.dtype),
            pltpu.VMEM(help_cache.shape, help_cache.dtype),
            pltpu.VMEM(out_weight.shape, out_weight.dtype),
            pltpu.SemaphoreType.DMA((3,)),
            pltpu.VMEM((n_grp,) + sent.shape, jnp.bfloat16),
            pltpu.VMEM((n_grp, back_rows, lanes), jnp.float32),
            pltpu.VMEM((back_rows, lanes), jnp.float32),
            pltpu.VMEM((3, pairs, row_count, lanes), jnp.float32),
            pltpu.VMEM((row_count, out_weight.shape[1]), jnp.float32),
            pltpu.VMEM((n_tp, row_count, out_cols), jnp.float32),
            pltpu.SemaphoreType.DMA((n_grp,)),
            pltpu.SemaphoreType.DMA((n_grp,)),
            pltpu.SemaphoreType.DMA((n_grp,)),
            pltpu.SemaphoreType.DMA((n_grp,)),
            pltpu.SemaphoreType.DMA((n_tp,)),
            pltpu.SemaphoreType.DMA((n_tp,)),
        ],
        compiler_params=pltpu.CompilerParams(collective_id=0, has_side_effects=True),
    )(lengths, split_at, helper_req, sent, new_kv, home_cache, help_cache, out_weight)


def grp_rows(mesh):
    column = list(mesh.devices[:, 0])
    n = len(column)
    coords = [getattr(d, "coords", None) for d in column]
    if coords[0] is not None:
        nz = 1
        while nz < n and coords[nz][1] == coords[0][1]:
            nz += 1
    else:
        nz = 1
        while nz * nz < n:
            nz *= 2
    return n // nz, nz


def solution(mesh):
    ny, nz = grp_rows(mesh)
    return jax.shard_map(
        functools.partial(per_device, ny, nz),
        mesh=mesh,
        in_specs=(
            P("grp", "tp"),
            P("grp", None, "tp"),
            P("grp", None, "tp", None, None),
            P("grp", None, "tp", None, None),
            P("grp"),
            P("grp"),
            P("grp"),
            P("tp", None),
        ),
        out_specs=P("grp", "tp"),
        check_vma=False,
    )
```

```python
import functools

import jax
import jax.numpy as jnp
from jax import lax
from jax.experimental import pallas as pl
from jax.experimental.pallas import tpu as pltpu
from jax.sharding import PartitionSpec as P

MESH = pl.DeviceIdType.MESH
LONG_AT = 1024


def attend(queries, cache, count, fresh):
    row_count = queries.shape[0]
    kv_heads = cache.shape[2]
    head_width = cache.shape[4] // 2
    half = cache.shape[3]
    group_size = queries.shape[1] // (kv_heads * head_width)
    score_scale = head_width ** (-0.5)
    head_rows = queries.reshape(row_count, kv_heads, group_size, head_width)
    blank = jnp.zeros_like(head_rows)
    wide_rows = jnp.stack(
        [
            jnp.concatenate([head_rows, blank], axis=-1),
            jnp.concatenate([blank, head_rows], axis=-1),
        ],
        axis=3,
    )
    key_rows = cache[:, 0]
    value_rows = cache[:, 1]
    scores = (
        jnp.einsum("nkgjc,nkpc->nkgjp", wide_rows, key_rows, preferred_element_type=jnp.float32)
        * score_scale
    )
    position = 2 * jnp.arange(half)[None, :] + jnp.arange(2)[:, None]
    inside = (position[None] < count[:, None, None])[:, None, None]
    top_score = jnp.max(jnp.where(inside, scores, -1e30), axis=(-2, -1))
    if fresh is not None:
        fresh_key = fresh[:, 0].reshape(row_count, kv_heads, head_width)
        fresh_score = (
            jnp.einsum("nkgd,nkd->nkg", head_rows, fresh_key, preferred_element_type=jnp.float32)
            * score_scale
        )
        top_score = jnp.maximum(top_score, fresh_score)
    weights = jnp.where(
        inside, jnp.exp(scores - top_score[..., None, None]), 0.0
    ).astype(jnp.bfloat16)
    weight_sum = jnp.sum(weights.astype(jnp.float32), axis=(-2, -1))
    both = jnp.einsum(
        "nkgjp,nkpc->nkgjc", weights, value_rows, preferred_element_type=jnp.float32
    )
    mixed_sum = both[..., 0, :head_width] + both[..., 1, head_width:]
    if fresh is not None:
        fresh_weight = lax.optimization_barrier(
            jnp.exp(fresh_score - top_score).astype(jnp.bfloat16)
        ).astype(jnp.float32)
        weight_sum = weight_sum + fresh_weight
        fresh_value = fresh[:, 1].reshape(row_count, kv_heads, 1, head_width).astype(jnp.float32)
        mixed_sum = mixed_sum + fresh_weight[..., None] * fresh_value
    return (
        top_score.reshape(row_count, -1),
        weight_sum.reshape(row_count, -1),
        mixed_sum.reshape(row_count, -1, head_width),
    )


def gather_kernel(n, x_ref, out_ref, held, send_sem, recv_sem):
    me = lax.axis_index("grp")
    col = lax.axis_index("tp")

    barrier = pltpu.get_barrier_semaphore()

    def greet(k, carry):
        peer = lax.rem(me + k, n)
        pl.semaphore_signal(barrier, inc=1, device_id=(peer, col), device_id_type=MESH)
        return carry

    lax.fori_loop(1, n, greet, 0)
    pl.semaphore_wait(barrier, n - 1)

    def copy_to(k):
        peer = lax.rem(me + k, n)
        return pltpu.make_async_remote_copy(
            src_ref=x_ref,
            dst_ref=held.at[me],
            send_sem=send_sem.at[k],
            recv_sem=recv_sem.at[k],
            device_id=(peer, col),
            device_id_type=MESH,
        )

    def copy_from(k):
        source = lax.rem(me + n - k, n)
        return pltpu.make_async_remote_copy(
            src_ref=x_ref,
            dst_ref=held.at[source],
            send_sem=send_sem.at[k],
            recv_sem=recv_sem.at[k],
            device_id=(source, col),
            device_id_type=MESH,
        )

    def start(k, carry):
        copy_to(k).start()
        return carry

    lax.fori_loop(1, n, start, 0)

    def finish(k, carry):
        copy_to(k).wait_send()
        copy_from(k).wait_recv()
        return carry

    lax.fori_loop(1, n, finish, 0)
    held[me] = x_ref[...]
    out_ref[...] = held[...]


def gather_grp(x, n, cid):
    return pl.pallas_call(
        functools.partial(gather_kernel, n),
        out_shape=jax.ShapeDtypeStruct((n,) + x.shape, x.dtype),
        in_specs=[pl.BlockSpec(memory_space=pltpu.VMEM)],
        out_specs=pl.BlockSpec(memory_space=pltpu.VMEM),
        scratch_shapes=[
            pltpu.VMEM((n,) + x.shape, x.dtype),
            pltpu.SemaphoreType.DMA((n,)),
            pltpu.SemaphoreType.DMA((n,)),
        ],
        compiler_params=pltpu.CompilerParams(collective_id=cid, has_side_effects=True),
    )(x)


def far_first(i, size):
    half = size // 2
    return half + i // 2 if i % 2 == 0 else half - (i + 1) // 2


def fanout(ny, nz, me, col, src, dst, send, recv):
    my_y = me // nz
    my_z = me % nz
    order = [(far_first(a, ny), far_first(b, nz)) for a in range(ny) for b in range(nz)][:-1]

    def copy(k, peer, slot):
        return pltpu.make_async_remote_copy(
            src_ref=src,
            dst_ref=dst.at[slot],
            send_sem=send.at[k],
            recv_sem=recv.at[k],
            device_id=(peer, col),
            device_id_type=MESH,
        )

    targets = []
    for k, (dy, dz) in enumerate(order):
        peer = lax.rem(my_y + dy, ny) * nz + lax.rem(my_z + dz, nz)
        out = copy(k, peer, me)
        out.start()
        targets.append(out)

    def finish():
        for k, (dy, dz) in enumerate(order):
            targets[k].wait_send()
            source = lax.rem(my_y + (ny - dy), ny) * nz + lax.rem(my_z + (nz - dz), nz)
            copy(k, source, source).wait_recv()

    return finish


def attend_tile(wide, keys, values, count, fresh_k=None, fresh_v=None):
    rows = wide.shape[0]
    scores = lax.dot_general(
        wide, keys, (((1,), (1,)), ((), ())), preferred_element_type=jnp.float32
    ) * 0.125
    half = rows // 2
    row = lax.broadcasted_iota(jnp.int32, scores.shape, 0)
    lane = lax.broadcasted_iota(jnp.int32, scores.shape, 1)
    position = 2 * lane + jnp.where(row >= half, 1, 0)
    inside = position.astype(jnp.float32) < count
    top = jnp.max(jnp.where(inside, scores, -1e30), axis=1, keepdims=True)
    top = jnp.maximum(top, pltpu.roll(top, half, 0))
    if fresh_k is not None:
        fresh_score = jnp.sum(
            wide.astype(jnp.float32) * fresh_k.astype(jnp.float32), axis=1, keepdims=True
        ) * 0.125
        top = jnp.maximum(top, fresh_score)
    weights = jnp.where(inside, jnp.exp(scores - top), 0.0).astype(jnp.bfloat16)
    total = jnp.sum(weights.astype(jnp.float32), axis=1, keepdims=True)
    total = total + pltpu.roll(total, half, 0)
    both = jnp.dot(weights, values, preferred_element_type=jnp.float32)
    mixed = both + pltpu.roll(pltpu.roll(both, half, 0), 64, 1)
    if fresh_k is not None:
        fresh_w = jnp.exp(fresh_score - top).astype(jnp.bfloat16).astype(jnp.float32)
        total = total + fresh_w
        mixed = mixed + fresh_w * fresh_v
    return top, total, mixed


def pair_rows(top, total, mixed, h):
    lane = lax.broadcasted_iota(jnp.int32, (1, mixed.shape[1]), 1)
    left = lane < 64
    g = 2 * h
    u = jnp.where(left, mixed[g : g + 1, :], mixed[g + 5 : g + 6, :])
    m = jnp.where(left, top[g : g + 1, :], top[g + 1 : g + 2, :])
    l = jnp.where(left, total[g : g + 1, :], total[g + 1 : g + 2, :])
    return u, m, l


def widen(q, heads):
    lane = lax.broadcasted_iota(jnp.int32, (2 * heads, 128), 1)
    row = lax.broadcasted_iota(jnp.int32, (2 * heads, 128), 0)
    low = lane < 64
    wide = jnp.zeros((2 * heads, 128), jnp.float32)
    for h in range(heads // 2):
        a = q[:, h * 128 : (h + 1) * 128]
        turned = pltpu.roll(a, 64, 1)
        g = 2 * h
        wide = jnp.where((row == g) & low, a, wide)
        wide = jnp.where((row == g + 1) & low, turned, wide)
        wide = jnp.where((row == heads + g) & ~low, turned, wide)
        wide = jnp.where((row == heads + g + 1) & ~low, a, wide)
    return wide.astype(jnp.bfloat16)


def whole_kernel(ny, nz, n_tp, slots, lengths_ref, splits_ref, helpers_ref, sent_ref, kv_ref, home_hbm, help_hbm, w_hbm, out_ref, home_ref, help_ref, w_ref, local,
                 got1, got2, back, stat, part, held, send1, recv1, send2, recv2, send3, recv3):
    n = ny * nz
    me = lax.axis_index("grp")
    col = lax.axis_index("tp")
    rows = sent_ref.shape[0]
    heads = w_ref.shape[0] // 64
    qw = heads * 64
    pairs = w_ref.shape[0] // 128
    width = out_ref.shape[1]

    barrier = pltpu.get_barrier_semaphore()

    my_y = me // nz
    my_z = me % nz
    for a in range(ny):
        for b in range(nz):
            dy, dz = far_first(a, ny), far_first(b, nz)
            if dy == 0 and dz == 0:
                continue
            peer = lax.rem(my_y + dy, ny) * nz + lax.rem(my_z + dz, nz)
            pl.semaphore_signal(barrier, inc=1, device_id=(peer, col), device_id_type=MESH)
    for k in range(1, n_tp):
        peer = lax.rem(col + k, n_tp)
        pl.semaphore_signal(barrier, inc=1, device_id=(me, peer), device_id_type=MESH)
    loads = [
        pltpu.make_async_copy(hbm, vmem, local.at[i])
        for i, (hbm, vmem) in enumerate(
            [(home_hbm, home_ref), (help_hbm, help_ref), (w_hbm, w_ref)]
        )
    ]
    for load in loads:
        load.start()
    pl.semaphore_wait(barrier, (n - 1) + (n_tp - 1))

    wait1 = fanout(ny, nz, me, col, sent_ref, got1, send1, recv1)
    lane = lax.broadcasted_iota(jnp.int32, (1, 128), 1)
    low = lane < 64
    loads[0].wait()
    for r in range(rows):
        key = kv_ref[r, 0:1, :].astype(jnp.float32)
        value = kv_ref[r, 1:2, :].astype(jnp.float32)
        fresh_k = jnp.concatenate([key, key], axis=1).astype(jnp.bfloat16)
        fresh_v = jnp.concatenate([value, value], axis=1)
        count = splits_ref[r].astype(jnp.float32)
        top, total, mixed = attend_tile(
            widen(sent_ref[r : r + 1, :qw].astype(jnp.float32), heads),
            home_ref[r, 0, 0],
            home_ref[r, 1, 0],
            count,
            fresh_k,
            fresh_v,
        )
        for h in range(pairs):
            u, m, l = pair_rows(top, total, mixed, h)
            stat[0, h, r : r + 1, :] = u
            stat[1, h, r : r + 1, :] = m
            stat[2, h, r : r + 1, :] = l
    wait1()
    loads[1].wait()

    partner = helpers_ref[0] // rows
    block = got1[partner]
    pick_row = lax.broadcasted_iota(jnp.int32, (slots, rows), 0)
    pick_col = lax.broadcasted_iota(jnp.int32, (slots, rows), 1)
    pick = jnp.zeros((slots, rows), jnp.float32)
    for k in range(slots):
        pick = jnp.where((pick_row == k) & (pick_col == helpers_ref[k] % rows), 1.0, pick)
    chosen = jnp.dot(pick.astype(jnp.bfloat16), block, preferred_element_type=jnp.float32)
    for k in range(slots):
        count = chosen[k : k + 1, qw : qw + 1] * 32.0 + chosen[k : k + 1, qw + 1 : qw + 2]
        top, total, mixed = attend_tile(
            widen(chosen[k : k + 1, :qw], heads), help_ref[k, 0, 0], help_ref[k, 1, 0], count
        )
        for h in range(pairs):
            u, m, l = pair_rows(top, total, mixed, h)
            back[k * pairs + h : k * pairs + h + 1, :] = u
            back[(slots + k) * pairs + h : (slots + k) * pairs + h + 1, :] = m
            back[(2 * slots + k) * pairs + h : (2 * slots + k) * pairs + h + 1, :] = l

    wait2 = fanout(ny, nz, me, col, back, got2, send2, recv2)

    sel_row = lax.broadcasted_iota(jnp.int32, (rows, slots), 0)
    sel_col = lax.broadcasted_iota(jnp.int32, (rows, slots), 1)
    fsel = jnp.zeros((rows, slots), jnp.float32)
    rank = jnp.int32(0)
    for r in range(rows):
        is_long = lengths_ref[r] > LONG_AT
        fsel = jnp.where((sel_row == r) & (sel_col == rank) & is_long, 1.0, fsel)
        rank = rank + is_long.astype(jnp.int32)
    has = fsel[:, 0:1]
    for k in range(1, slots):
        has = has + fsel[:, k : k + 1]
    wait2()

    loads[2].wait()
    theirs = got2[partner]
    acc = jnp.zeros(part.shape, jnp.float32)
    for h in range(pairs):

        def pick_far(base):
            x = fsel[:, 0:1] * theirs[base + h : base + h + 1, :]
            for k in range(1, slots):
                r0 = base + k * pairs + h
                x = x + fsel[:, k : k + 1] * theirs[r0 : r0 + 1, :]
            return x

        far_u = pick_far(0)
        far_m = jnp.where(has > 0.0, pick_far(slots * pairs), -1e30)
        far_l = pick_far(2 * slots * pairs)
        home_u = stat[0, h]
        home_m = stat[1, h]
        home_l = stat[2, h]
        top = jnp.maximum(home_m, far_m)
        home_e = jnp.exp(home_m - top)
        far_e = jnp.exp(far_m - top)
        mix = (home_u * home_e + far_u * far_e) / (home_l * home_e + far_l * far_e)
        acc = acc + jnp.dot(
            mix.astype(jnp.bfloat16),
            w_ref[h * 128 : (h + 1) * 128, :],
            preferred_element_type=jnp.float32,
        )
    part[...] = acc

    sends = []
    for k in range(1, n_tp):
        peer = lax.rem(col + k, n_tp)
        cols = pl.ds(pl.multiple_of(peer * width, width), width)
        copy = pltpu.make_async_remote_copy(
            src_ref=part.at[:, cols],
            dst_ref=held.at[k],
            send_sem=send3.at[k],
            recv_sem=recv3.at[k],
            device_id=(me, peer),
            device_id_type=MESH,
        )
        copy.start()
        sends.append(copy)
    own = pl.ds(pl.multiple_of(col * width, width), width)
    total = part[:, own]
    for copy in sends:
        copy.wait_send()
        copy.wait_recv()
    for k in range(1, n_tp):
        total = total + held[k]
    out_ref[...] = total.astype(out_ref.dtype)


def per_device(ny, nz, queries, new_kv, home_cache, help_cache, lengths, split_at, helper_req, out_weight):
    n_grp = lax.axis_size("grp")
    n_tp = lax.axis_size("tp")
    row_count, width = queries.shape
    slots = help_cache.shape[0]
    pairs = width // 128
    lanes = 128

    count = lengths - split_at
    lane = jnp.arange(lanes)[None, :]
    code = jnp.where(
        lane == 0, (count // 32)[:, None], jnp.where(lane == 1, (count % 32)[:, None], 0)
    ).astype(jnp.bfloat16)
    sent = jnp.concatenate([queries, code], axis=1)

    out_cols = out_weight.shape[1] // n_tp
    vmem = pl.BlockSpec(memory_space=pltpu.VMEM)
    smem = pl.BlockSpec(memory_space=pltpu.SMEM)
    back_rows = 3 * slots * pairs
    return pl.pallas_call(
        functools.partial(whole_kernel, ny, nz, n_tp, slots),
        out_shape=jax.ShapeDtypeStruct((row_count, out_cols), jnp.bfloat16),
        in_specs=[smem] * 3 + [vmem] * 2 + [pl.BlockSpec(memory_space=pl.ANY)] * 3,
        out_specs=vmem,
        scratch_shapes=[
            pltpu.VMEM(home_cache.shape, home_cache.dtype),
            pltpu.VMEM(help_cache.shape, help_cache.dtype),
            pltpu.VMEM(out_weight.shape, out_weight.dtype),
            pltpu.SemaphoreType.DMA((3,)),
            pltpu.VMEM((n_grp,) + sent.shape, jnp.bfloat16),
            pltpu.VMEM((n_grp, back_rows, lanes), jnp.float32),
            pltpu.VMEM((back_rows, lanes), jnp.float32),
            pltpu.VMEM((3, pairs, row_count, lanes), jnp.float32),
            pltpu.VMEM((row_count, out_weight.shape[1]), jnp.float32),
            pltpu.VMEM((n_tp, row_count, out_cols), jnp.float32),
            pltpu.SemaphoreType.DMA((n_grp,)),
            pltpu.SemaphoreType.DMA((n_grp,)),
            pltpu.SemaphoreType.DMA((n_grp,)),
            pltpu.SemaphoreType.DMA((n_grp,)),
            pltpu.SemaphoreType.DMA((n_tp,)),
            pltpu.SemaphoreType.DMA((n_tp,)),
        ],
        compiler_params=pltpu.CompilerParams(collective_id=0, has_side_effects=True),
    )(lengths, split_at, helper_req, sent, new_kv, home_cache, help_cache, out_weight)


def grp_rows(mesh):
    column = list(mesh.devices[:, 0])
    n = len(column)
    coords = [getattr(d, "coords", None) for d in column]
    if coords[0] is not None:
        nz = 1
        while nz < n and coords[nz][1] == coords[0][1]:
            nz += 1
    else:
        nz = 1
        while nz * nz < n:
            nz *= 2
    return n // nz, nz


def solution(mesh):
    ny, nz = grp_rows(mesh)
    return jax.shard_map(
        functools.partial(per_device, ny, nz),
        mesh=mesh,
        in_specs=(
            P("grp", "tp"),
            P("grp", None, "tp"),
            P("grp", None, "tp", None, None),
            P("grp", None, "tp", None, None),
            P("grp"),
            P("grp"),
            P("grp"),
            P("tp", None),
        ),
        out_specs=P("grp", "tp"),
        check_vma=False,
    )
```

```python
import functools

import jax
import jax.numpy as jnp
from jax import lax
from jax.experimental import pallas as pl
from jax.experimental.pallas import tpu as pltpu
from jax.sharding import PartitionSpec as P

MESH = pl.DeviceIdType.MESH
LONG_AT = 1024


def attend(queries, cache, count, fresh):
    row_count = queries.shape[0]
    kv_heads = cache.shape[2]
    head_width = cache.shape[4] // 2
    half = cache.shape[3]
    group_size = queries.shape[1] // (kv_heads * head_width)
    score_scale = head_width ** (-0.5)
    head_rows = queries.reshape(row_count, kv_heads, group_size, head_width)
    blank = jnp.zeros_like(head_rows)
    wide_rows = jnp.stack(
        [
            jnp.concatenate([head_rows, blank], axis=-1),
            jnp.concatenate([blank, head_rows], axis=-1),
        ],
        axis=3,
    )
    key_rows = cache[:, 0]
    value_rows = cache[:, 1]
    scores = (
        jnp.einsum("nkgjc,nkpc->nkgjp", wide_rows, key_rows, preferred_element_type=jnp.float32)
        * score_scale
    )
    position = 2 * jnp.arange(half)[None, :] + jnp.arange(2)[:, None]
    inside = (position[None] < count[:, None, None])[:, None, None]
    top_score = jnp.max(jnp.where(inside, scores, -1e30), axis=(-2, -1))
    if fresh is not None:
        fresh_key = fresh[:, 0].reshape(row_count, kv_heads, head_width)
        fresh_score = (
            jnp.einsum("nkgd,nkd->nkg", head_rows, fresh_key, preferred_element_type=jnp.float32)
            * score_scale
        )
        top_score = jnp.maximum(top_score, fresh_score)
    weights = jnp.where(
        inside, jnp.exp(scores - top_score[..., None, None]), 0.0
    ).astype(jnp.bfloat16)
    weight_sum = jnp.sum(weights.astype(jnp.float32), axis=(-2, -1))
    both = jnp.einsum(
        "nkgjp,nkpc->nkgjc", weights, value_rows, preferred_element_type=jnp.float32
    )
    mixed_sum = both[..., 0, :head_width] + both[..., 1, head_width:]
    if fresh is not None:
        fresh_weight = lax.optimization_barrier(
            jnp.exp(fresh_score - top_score).astype(jnp.bfloat16)
        ).astype(jnp.float32)
        weight_sum = weight_sum + fresh_weight
        fresh_value = fresh[:, 1].reshape(row_count, kv_heads, 1, head_width).astype(jnp.float32)
        mixed_sum = mixed_sum + fresh_weight[..., None] * fresh_value
    return (
        top_score.reshape(row_count, -1),
        weight_sum.reshape(row_count, -1),
        mixed_sum.reshape(row_count, -1, head_width),
    )


def gather_kernel(n, x_ref, out_ref, held, send_sem, recv_sem):
    me = lax.axis_index("grp")
    col = lax.axis_index("tp")

    barrier = pltpu.get_barrier_semaphore()

    def greet(k, carry):
        peer = lax.rem(me + k, n)
        pl.semaphore_signal(barrier, inc=1, device_id=(peer, col), device_id_type=MESH)
        return carry

    lax.fori_loop(1, n, greet, 0)
    pl.semaphore_wait(barrier, n - 1)

    def copy_to(k):
        peer = lax.rem(me + k, n)
        return pltpu.make_async_remote_copy(
            src_ref=x_ref,
            dst_ref=held.at[me],
            send_sem=send_sem.at[k],
            recv_sem=recv_sem.at[k],
            device_id=(peer, col),
            device_id_type=MESH,
        )

    def copy_from(k):
        source = lax.rem(me + n - k, n)
        return pltpu.make_async_remote_copy(
            src_ref=x_ref,
            dst_ref=held.at[source],
            send_sem=send_sem.at[k],
            recv_sem=recv_sem.at[k],
            device_id=(source, col),
            device_id_type=MESH,
        )

    def start(k, carry):
        copy_to(k).start()
        return carry

    lax.fori_loop(1, n, start, 0)

    def finish(k, carry):
        copy_to(k).wait_send()
        copy_from(k).wait_recv()
        return carry

    lax.fori_loop(1, n, finish, 0)
    held[me] = x_ref[...]
    out_ref[...] = held[...]


def gather_grp(x, n, cid):
    return pl.pallas_call(
        functools.partial(gather_kernel, n),
        out_shape=jax.ShapeDtypeStruct((n,) + x.shape, x.dtype),
        in_specs=[pl.BlockSpec(memory_space=pltpu.VMEM)],
        out_specs=pl.BlockSpec(memory_space=pltpu.VMEM),
        scratch_shapes=[
            pltpu.VMEM((n,) + x.shape, x.dtype),
            pltpu.SemaphoreType.DMA((n,)),
            pltpu.SemaphoreType.DMA((n,)),
        ],
        compiler_params=pltpu.CompilerParams(collective_id=cid, has_side_effects=True),
    )(x)


def far_first(i, size):
    half = size // 2
    return half + i // 2 if i % 2 == 0 else half - (i + 1) // 2


def fanout(ny, nz, me, col, src, dst, send, recv):
    my_y = me // nz
    my_z = me % nz
    order = [(far_first(a, ny), far_first(b, nz)) for a in range(ny) for b in range(nz)][:-1]

    def copy(k, peer, slot):
        return pltpu.make_async_remote_copy(
            src_ref=src,
            dst_ref=dst.at[slot],
            send_sem=send.at[k],
            recv_sem=recv.at[k],
            device_id=(peer, col),
            device_id_type=MESH,
        )

    targets = []
    for k, (dy, dz) in enumerate(order):
        peer = lax.rem(my_y + dy, ny) * nz + lax.rem(my_z + dz, nz)
        out = copy(k, peer, me)
        out.start()
        targets.append(out)

    def finish():
        for k, (dy, dz) in enumerate(order):
            targets[k].wait_send()
            source = lax.rem(my_y + (ny - dy), ny) * nz + lax.rem(my_z + (nz - dz), nz)
            copy(k, source, source).wait_recv()

    return finish


def attend_tile(wide, keys, values, count, fresh_k=None, fresh_v=None):
    rows = wide.shape[0]
    scores = lax.dot_general(
        wide, keys, (((1,), (1,)), ((), ())), preferred_element_type=jnp.float32
    ) * 0.125
    half = rows // 2
    row = lax.broadcasted_iota(jnp.int32, scores.shape, 0)
    lane = lax.broadcasted_iota(jnp.int32, scores.shape, 1)
    position = 2 * lane + jnp.where(row >= half, 1, 0)
    inside = position.astype(jnp.float32) < count
    top = jnp.max(jnp.where(inside, scores, -1e30), axis=1, keepdims=True)
    top = jnp.maximum(top, pltpu.roll(top, half, 0))
    if fresh_k is not None:
        fresh_score = jnp.sum(
            wide.astype(jnp.float32) * fresh_k.astype(jnp.float32), axis=1, keepdims=True
        ) * 0.125
        top = jnp.maximum(top, fresh_score)
    weights = jnp.where(inside, jnp.exp(scores - top), 0.0).astype(jnp.bfloat16)
    total = jnp.sum(weights.astype(jnp.float32), axis=1, keepdims=True)
    total = total + pltpu.roll(total, half, 0)
    both = jnp.dot(weights, values, preferred_element_type=jnp.float32)
    mixed = both + pltpu.roll(pltpu.roll(both, half, 0), 64, 1)
    if fresh_k is not None:
        fresh_w = jnp.exp(fresh_score - top).astype(jnp.bfloat16).astype(jnp.float32)
        total = total + fresh_w
        mixed = mixed + fresh_w * fresh_v
    return top, total, mixed


def pair_rows(top, total, mixed, h):
    lane = lax.broadcasted_iota(jnp.int32, (1, mixed.shape[1]), 1)
    left = lane < 64
    g = 2 * h
    u = jnp.where(left, mixed[g : g + 1, :], mixed[g + 5 : g + 6, :])
    m = jnp.where(left, top[g : g + 1, :], top[g + 1 : g + 2, :])
    l = jnp.where(left, total[g : g + 1, :], total[g + 1 : g + 2, :])
    return u, m, l


def widen(q, heads):
    lane = lax.broadcasted_iota(jnp.int32, (2 * heads, 128), 1)
    row = lax.broadcasted_iota(jnp.int32, (2 * heads, 128), 0)
    low = lane < 64
    wide = jnp.zeros((2 * heads, 128), jnp.float32)
    for h in range(heads // 2):
        a = q[:, h * 128 : (h + 1) * 128]
        turned = pltpu.roll(a, 64, 1)
        g = 2 * h
        wide = jnp.where((row == g) & low, a, wide)
        wide = jnp.where((row == g + 1) & low, turned, wide)
        wide = jnp.where((row == heads + g) & ~low, turned, wide)
        wide = jnp.where((row == heads + g + 1) & ~low, a, wide)
    return wide.astype(jnp.bfloat16)


def whole_kernel(ny, nz, n_tp, slots, lengths_ref, splits_ref, helpers_ref, queries_ref, kv_ref,
                 home_hbm, help_hbm, w_hbm, out_ref, sent_ref, home_ref, help_ref, w_ref, local,
                 got1, got2, back, stat, part, held, send1, recv1, send2, recv2, send3, recv3):
    n = ny * nz
    me = lax.axis_index("grp")
    col = lax.axis_index("tp")
    rows = queries_ref.shape[0]
    heads = w_ref.shape[0] // 64
    qw = heads * 64

    code_row = lax.broadcasted_iota(jnp.int32, (rows, 128), 0)
    code_lane = lax.broadcasted_iota(jnp.int32, (rows, 128), 1)
    code = jnp.zeros((rows, 128), jnp.float32)
    for r in range(rows):
        count = lengths_ref[r] - splits_ref[r]
        code = jnp.where((code_row == r) & (code_lane == 0), (count // 32).astype(jnp.float32), code)
        code = jnp.where((code_row == r) & (code_lane == 1), (count % 32).astype(jnp.float32), code)
    sent_ref[:, :qw] = queries_ref[...]
    sent_ref[:, qw:] = code.astype(sent_ref.dtype)
    pairs = w_ref.shape[0] // 128
    width = out_ref.shape[1]

    barrier = pltpu.get_barrier_semaphore()

    my_y = me // nz
    my_z = me % nz
    for a in range(ny):
        for b in range(nz):
            dy, dz = far_first(a, ny), far_first(b, nz)
            if dy == 0 and dz == 0:
                continue
            peer = lax.rem(my_y + dy, ny) * nz + lax.rem(my_z + dz, nz)
            pl.semaphore_signal(barrier, inc=1, device_id=(peer, col), device_id_type=MESH)
    for k in range(1, n_tp):
        peer = lax.rem(col + k, n_tp)
        pl.semaphore_signal(barrier, inc=1, device_id=(me, peer), device_id_type=MESH)
    loads = [
        pltpu.make_async_copy(hbm, vmem, local.at[i])
        for i, (hbm, vmem) in enumerate(
            [(home_hbm, home_ref), (help_hbm, help_ref), (w_hbm, w_ref)]
        )
    ]
    for load in loads:
        load.start()
    pl.semaphore_wait(barrier, (n - 1) + (n_tp - 1))

    wait1 = fanout(ny, nz, me, col, sent_ref, got1, send1, recv1)
    lane = lax.broadcasted_iota(jnp.int32, (1, 128), 1)
    low = lane < 64
    loads[0].wait()
    for r in range(rows):
        key = kv_ref[r, 0:1, :].astype(jnp.float32)
        value = kv_ref[r, 1:2, :].astype(jnp.float32)
        fresh_k = jnp.concatenate([key, key], axis=1).astype(jnp.bfloat16)
        fresh_v = jnp.concatenate([value, value], axis=1)
        count = splits_ref[r].astype(jnp.float32)
        top, total, mixed = attend_tile(
            widen(queries_ref[r : r + 1, :].astype(jnp.float32), heads),
            home_ref[r, 0, 0],
            home_ref[r, 1, 0],
            count,
            fresh_k,
            fresh_v,
        )
        for h in range(pairs):
            u, m, l = pair_rows(top, total, mixed, h)
            stat[0, h, r : r + 1, :] = u
            stat[1, h, r : r + 1, :] = m
            stat[2, h, r : r + 1, :] = l
    wait1()
    loads[1].wait()

    partner = helpers_ref[0] // rows
    block = got1[partner]
    pick_row = lax.broadcasted_iota(jnp.int32, (slots, rows), 0)
    pick_col = lax.broadcasted_iota(jnp.int32, (slots, rows), 1)
    pick = jnp.zeros((slots, rows), jnp.float32)
    for k in range(slots):
        pick = jnp.where((pick_row == k) & (pick_col == helpers_ref[k] % rows), 1.0, pick)
    chosen = jnp.dot(pick.astype(jnp.bfloat16), block, preferred_element_type=jnp.float32)
    for k in range(slots):
        count = chosen[k : k + 1, qw : qw + 1] * 32.0 + chosen[k : k + 1, qw + 1 : qw + 2]
        top, total, mixed = attend_tile(
            widen(chosen[k : k + 1, :qw], heads), help_ref[k, 0, 0], help_ref[k, 1, 0], count
        )
        for h in range(pairs):
            u, m, l = pair_rows(top, total, mixed, h)
            back[k * pairs + h : k * pairs + h + 1, :] = u
            back[(slots + k) * pairs + h : (slots + k) * pairs + h + 1, :] = m
            back[(2 * slots + k) * pairs + h : (2 * slots + k) * pairs + h + 1, :] = l

    wait2 = fanout(ny, nz, me, col, back, got2, send2, recv2)

    sel_row = lax.broadcasted_iota(jnp.int32, (rows, slots), 0)
    sel_col = lax.broadcasted_iota(jnp.int32, (rows, slots), 1)
    fsel = jnp.zeros((rows, slots), jnp.float32)
    rank = jnp.int32(0)
    for r in range(rows):
        is_long = lengths_ref[r] > LONG_AT
        fsel = jnp.where((sel_row == r) & (sel_col == rank) & is_long, 1.0, fsel)
        rank = rank + is_long.astype(jnp.int32)
    has = fsel[:, 0:1]
    for k in range(1, slots):
        has = has + fsel[:, k : k + 1]
    wait2()

    loads[2].wait()
    theirs = got2[partner]
    acc = jnp.zeros(part.shape, jnp.float32)
    for h in range(pairs):

        def pick_far(base):
            x = fsel[:, 0:1] * theirs[base + h : base + h + 1, :]
            for k in range(1, slots):
                r0 = base + k * pairs + h
                x = x + fsel[:, k : k + 1] * theirs[r0 : r0 + 1, :]
            return x

        far_u = pick_far(0)
        far_m = jnp.where(has > 0.0, pick_far(slots * pairs), -1e30)
        far_l = pick_far(2 * slots * pairs)
        home_u = stat[0, h]
        home_m = stat[1, h]
        home_l = stat[2, h]
        top = jnp.maximum(home_m, far_m)
        home_e = jnp.exp(home_m - top)
        far_e = jnp.exp(far_m - top)
        mix = (home_u * home_e + far_u * far_e) / (home_l * home_e + far_l * far_e)
        acc = acc + jnp.dot(
            mix.astype(jnp.bfloat16),
            w_ref[h * 128 : (h + 1) * 128, :],
            preferred_element_type=jnp.float32,
        )
    part[...] = acc

    sends = []
    for k in range(1, n_tp):
        peer = lax.rem(col + k, n_tp)
        cols = pl.ds(pl.multiple_of(peer * width, width), width)
        copy = pltpu.make_async_remote_copy(
            src_ref=part.at[:, cols],
            dst_ref=held.at[k],
            send_sem=send3.at[k],
            recv_sem=recv3.at[k],
            device_id=(me, peer),
            device_id_type=MESH,
        )
        copy.start()
        sends.append(copy)
    own = pl.ds(pl.multiple_of(col * width, width), width)
    total = part[:, own]
    for copy in sends:
        copy.wait_send()
        copy.wait_recv()
    for k in range(1, n_tp):
        total = total + held[k]
    out_ref[...] = total.astype(out_ref.dtype)


def per_device(ny, nz, queries, new_kv, home_cache, help_cache, lengths, split_at, helper_req, out_weight):
    n_grp = lax.axis_size("grp")
    n_tp = lax.axis_size("tp")
    row_count, width = queries.shape
    slots = help_cache.shape[0]
    pairs = width // 128
    lanes = 128

    sent_shape = (row_count, width + lanes)

    out_cols = out_weight.shape[1] // n_tp
    vmem = pl.BlockSpec(memory_space=pltpu.VMEM)
    smem = pl.BlockSpec(memory_space=pltpu.SMEM)
    back_rows = 3 * slots * pairs
    return pl.pallas_call(
        functools.partial(whole_kernel, ny, nz, n_tp, slots),
        out_shape=jax.ShapeDtypeStruct((row_count, out_cols), jnp.bfloat16),
        in_specs=[smem] * 3 + [vmem] * 2 + [pl.BlockSpec(memory_space=pl.ANY)] * 3,
        out_specs=vmem,
        scratch_shapes=[
            pltpu.VMEM(sent_shape, jnp.bfloat16),
            pltpu.VMEM(home_cache.shape, home_cache.dtype),
            pltpu.VMEM(help_cache.shape, help_cache.dtype),
            pltpu.VMEM(out_weight.shape, out_weight.dtype),
            pltpu.SemaphoreType.DMA((3,)),
            pltpu.VMEM((n_grp,) + sent_shape, jnp.bfloat16),
            pltpu.VMEM((n_grp, back_rows, lanes), jnp.float32),
            pltpu.VMEM((back_rows, lanes), jnp.float32),
            pltpu.VMEM((3, pairs, row_count, lanes), jnp.float32),
            pltpu.VMEM((row_count, out_weight.shape[1]), jnp.float32),
            pltpu.VMEM((n_tp, row_count, out_cols), jnp.float32),
            pltpu.SemaphoreType.DMA((n_grp,)),
            pltpu.SemaphoreType.DMA((n_grp,)),
            pltpu.SemaphoreType.DMA((n_grp,)),
            pltpu.SemaphoreType.DMA((n_grp,)),
            pltpu.SemaphoreType.DMA((n_tp,)),
            pltpu.SemaphoreType.DMA((n_tp,)),
        ],
        compiler_params=pltpu.CompilerParams(collective_id=0, has_side_effects=True),
    )(lengths, split_at, helper_req, queries, new_kv, home_cache, help_cache, out_weight)


def grp_rows(mesh):
    column = list(mesh.devices[:, 0])
    n = len(column)
    coords = [getattr(d, "coords", None) for d in column]
    if coords[0] is not None:
        nz = 1
        while nz < n and coords[nz][1] == coords[0][1]:
            nz += 1
    else:
        nz = 1
        while nz * nz < n:
            nz *= 2
    return n // nz, nz


def solution(mesh):
    ny, nz = grp_rows(mesh)
    return jax.shard_map(
        functools.partial(per_device, ny, nz),
        mesh=mesh,
        in_specs=(
            P("grp", "tp"),
            P("grp", None, "tp"),
            P("grp", None, "tp", None, None),
            P("grp", None, "tp", None, None),
            P("grp"),
            P("grp"),
            P("grp"),
            P("tp", None),
        ),
        out_specs=P("grp", "tp"),
        check_vma=False,
    )
```

```python
import functools

import jax
import jax.numpy as jnp
from jax import lax
from jax.experimental import pallas as pl
from jax.experimental.pallas import tpu as pltpu
from jax.sharding import PartitionSpec as P

MESH = pl.DeviceIdType.MESH
LONG_AT = 1024


def attend(queries, cache, count, fresh):
    row_count = queries.shape[0]
    kv_heads = cache.shape[2]
    head_width = cache.shape[4] // 2
    half = cache.shape[3]
    group_size = queries.shape[1] // (kv_heads * head_width)
    score_scale = head_width ** (-0.5)
    head_rows = queries.reshape(row_count, kv_heads, group_size, head_width)
    blank = jnp.zeros_like(head_rows)
    wide_rows = jnp.stack(
        [
            jnp.concatenate([head_rows, blank], axis=-1),
            jnp.concatenate([blank, head_rows], axis=-1),
        ],
        axis=3,
    )
    key_rows = cache[:, 0]
    value_rows = cache[:, 1]
    scores = (
        jnp.einsum("nkgjc,nkpc->nkgjp", wide_rows, key_rows, preferred_element_type=jnp.float32)
        * score_scale
    )
    position = 2 * jnp.arange(half)[None, :] + jnp.arange(2)[:, None]
    inside = (position[None] < count[:, None, None])[:, None, None]
    top_score = jnp.max(jnp.where(inside, scores, -1e30), axis=(-2, -1))
    if fresh is not None:
        fresh_key = fresh[:, 0].reshape(row_count, kv_heads, head_width)
        fresh_score = (
            jnp.einsum("nkgd,nkd->nkg", head_rows, fresh_key, preferred_element_type=jnp.float32)
            * score_scale
        )
        top_score = jnp.maximum(top_score, fresh_score)
    weights = jnp.where(
        inside, jnp.exp(scores - top_score[..., None, None]), 0.0
    ).astype(jnp.bfloat16)
    weight_sum = jnp.sum(weights.astype(jnp.float32), axis=(-2, -1))
    both = jnp.einsum(
        "nkgjp,nkpc->nkgjc", weights, value_rows, preferred_element_type=jnp.float32
    )
    mixed_sum = both[..., 0, :head_width] + both[..., 1, head_width:]
    if fresh is not None:
        fresh_weight = lax.optimization_barrier(
            jnp.exp(fresh_score - top_score).astype(jnp.bfloat16)
        ).astype(jnp.float32)
        weight_sum = weight_sum + fresh_weight
        fresh_value = fresh[:, 1].reshape(row_count, kv_heads, 1, head_width).astype(jnp.float32)
        mixed_sum = mixed_sum + fresh_weight[..., None] * fresh_value
    return (
        top_score.reshape(row_count, -1),
        weight_sum.reshape(row_count, -1),
        mixed_sum.reshape(row_count, -1, head_width),
    )


def gather_kernel(n, x_ref, out_ref, held, send_sem, recv_sem):
    me = lax.axis_index("grp")
    col = lax.axis_index("tp")

    barrier = pltpu.get_barrier_semaphore()

    def greet(k, carry):
        peer = lax.rem(me + k, n)
        pl.semaphore_signal(barrier, inc=1, device_id=(peer, col), device_id_type=MESH)
        return carry

    lax.fori_loop(1, n, greet, 0)
    pl.semaphore_wait(barrier, n - 1)

    def copy_to(k):
        peer = lax.rem(me + k, n)
        return pltpu.make_async_remote_copy(
            src_ref=x_ref,
            dst_ref=held.at[me],
            send_sem=send_sem.at[k],
            recv_sem=recv_sem.at[k],
            device_id=(peer, col),
            device_id_type=MESH,
        )

    def copy_from(k):
        source = lax.rem(me + n - k, n)
        return pltpu.make_async_remote_copy(
            src_ref=x_ref,
            dst_ref=held.at[source],
            send_sem=send_sem.at[k],
            recv_sem=recv_sem.at[k],
            device_id=(source, col),
            device_id_type=MESH,
        )

    def start(k, carry):
        copy_to(k).start()
        return carry

    lax.fori_loop(1, n, start, 0)

    def finish(k, carry):
        copy_to(k).wait_send()
        copy_from(k).wait_recv()
        return carry

    lax.fori_loop(1, n, finish, 0)
    held[me] = x_ref[...]
    out_ref[...] = held[...]


def gather_grp(x, n, cid):
    return pl.pallas_call(
        functools.partial(gather_kernel, n),
        out_shape=jax.ShapeDtypeStruct((n,) + x.shape, x.dtype),
        in_specs=[pl.BlockSpec(memory_space=pltpu.VMEM)],
        out_specs=pl.BlockSpec(memory_space=pltpu.VMEM),
        scratch_shapes=[
            pltpu.VMEM((n,) + x.shape, x.dtype),
            pltpu.SemaphoreType.DMA((n,)),
            pltpu.SemaphoreType.DMA((n,)),
        ],
        compiler_params=pltpu.CompilerParams(collective_id=cid, has_side_effects=True),
    )(x)


def far_first(i, size):
    half = size // 2
    return half + i // 2 if i % 2 == 0 else half - (i + 1) // 2


def fanout(ny, nz, me, col, src, dst, send, recv):
    my_y = me // nz
    my_z = me % nz
    order = [(far_first(a, ny), far_first(b, nz)) for a in range(ny) for b in range(nz)][:-1]

    def copy(k, peer, slot):
        return pltpu.make_async_remote_copy(
            src_ref=src,
            dst_ref=dst.at[slot],
            send_sem=send.at[k],
            recv_sem=recv.at[k],
            device_id=(peer, col),
            device_id_type=MESH,
        )

    targets = []
    for k, (dy, dz) in enumerate(order):
        peer = lax.rem(my_y + dy, ny) * nz + lax.rem(my_z + dz, nz)
        out = copy(k, peer, me)
        out.start()
        targets.append(out)

    def finish():
        for k, (dy, dz) in enumerate(order):
            targets[k].wait_send()
            source = lax.rem(my_y + (ny - dy), ny) * nz + lax.rem(my_z + (nz - dz), nz)
            copy(k, source, source).wait_recv()

    return finish


def attend_tile(wide, keys, values, count, fresh_k=None, fresh_v=None):
    rows = wide.shape[0]
    scores = lax.dot_general(
        wide, keys, (((1,), (1,)), ((), ())), preferred_element_type=jnp.float32
    ) * 0.125
    half = rows // 2
    row = lax.broadcasted_iota(jnp.int32, scores.shape, 0)
    lane = lax.broadcasted_iota(jnp.int32, scores.shape, 1)
    position = 2 * lane + jnp.where(row >= half, 1, 0)
    inside = position.astype(jnp.float32) < count
    top = jnp.max(jnp.where(inside, scores, -1e30), axis=1, keepdims=True)
    top = jnp.maximum(top, pltpu.roll(top, half, 0))
    if fresh_k is not None:
        fresh_score = jnp.sum(
            wide.astype(jnp.float32) * fresh_k.astype(jnp.float32), axis=1, keepdims=True
        ) * 0.125
        top = jnp.maximum(top, fresh_score)
    weights = jnp.where(inside, jnp.exp(scores - top), 0.0).astype(jnp.bfloat16)
    total = jnp.sum(weights.astype(jnp.float32), axis=1, keepdims=True)
    total = total + pltpu.roll(total, half, 0)
    both = jnp.dot(weights, values, preferred_element_type=jnp.float32)
    mixed = both + pltpu.roll(pltpu.roll(both, half, 0), 64, 1)
    if fresh_k is not None:
        fresh_w = jnp.exp(fresh_score - top).astype(jnp.bfloat16).astype(jnp.float32)
        total = total + fresh_w
        mixed = mixed + fresh_w * fresh_v
    return top, total, mixed


def pair_rows(top, total, mixed, h):
    lane = lax.broadcasted_iota(jnp.int32, (1, mixed.shape[1]), 1)
    left = lane < 64
    g = 2 * h
    u = jnp.where(left, mixed[g : g + 1, :], mixed[g + 5 : g + 6, :])
    m = jnp.where(left, top[g : g + 1, :], top[g + 1 : g + 2, :])
    l = jnp.where(left, total[g : g + 1, :], total[g + 1 : g + 2, :])
    return u, m, l


def widen(q, heads):
    lane = lax.broadcasted_iota(jnp.int32, (2 * heads, 128), 1)
    row = lax.broadcasted_iota(jnp.int32, (2 * heads, 128), 0)
    low = lane < 64
    wide = jnp.zeros((2 * heads, 128), jnp.float32)
    for h in range(heads // 2):
        a = q[:, h * 128 : (h + 1) * 128]
        turned = pltpu.roll(a, 64, 1)
        g = 2 * h
        wide = jnp.where((row == g) & low, a, wide)
        wide = jnp.where((row == g + 1) & low, turned, wide)
        wide = jnp.where((row == heads + g) & ~low, turned, wide)
        wide = jnp.where((row == heads + g + 1) & ~low, a, wide)
    return wide.astype(jnp.bfloat16)


def whole_kernel(ny, nz, n_tp, slots, lengths_ref, splits_ref, helpers_ref, queries_ref, kv_ref,
                 home_hbm, help_hbm, w_hbm, out_ref, sent_ref, home_ref, help_ref, w_ref, local,
                 got1, got2, back, stat, part, held, send1, recv1, send2, recv2, send3, recv3):
    n = ny * nz
    me = lax.axis_index("grp")
    col = lax.axis_index("tp")
    rows = queries_ref.shape[0]
    heads = w_ref.shape[0] // 64
    qw = heads * 64

    code_row = lax.broadcasted_iota(jnp.int32, (rows, 128), 0)
    code_lane = lax.broadcasted_iota(jnp.int32, (rows, 128), 1)
    code = jnp.zeros((rows, 128), jnp.float32)
    for r in range(rows):
        count = lengths_ref[r] - splits_ref[r]
        code = jnp.where((code_row == r) & (code_lane == 0), (count // 32).astype(jnp.float32), code)
        code = jnp.where((code_row == r) & (code_lane == 1), (count % 32).astype(jnp.float32), code)
    sent_ref[:, :qw] = queries_ref[...]
    sent_ref[:, qw:] = code.astype(sent_ref.dtype)
    pairs = w_ref.shape[0] // 128
    width = out_ref.shape[1]

    barrier = pltpu.get_barrier_semaphore()

    my_y = me // nz
    my_z = me % nz
    for a in range(ny):
        for b in range(nz):
            dy, dz = far_first(a, ny), far_first(b, nz)
            if dy == 0 and dz == 0:
                continue
            peer = lax.rem(my_y + dy, ny) * nz + lax.rem(my_z + dz, nz)
            pl.semaphore_signal(barrier, inc=1, device_id=(peer, col), device_id_type=MESH)
    for k in range(1, n_tp):
        peer = lax.rem(col + k, n_tp)
        pl.semaphore_signal(barrier, inc=1, device_id=(me, peer), device_id_type=MESH)
    loads = [
        pltpu.make_async_copy(hbm, vmem, local.at[i])
        for i, (hbm, vmem) in enumerate(
            [(home_hbm, home_ref), (help_hbm, help_ref), (w_hbm, w_ref)]
        )
    ]
    for load in loads:
        load.start()
    pl.semaphore_wait(barrier, (n - 1) + (n_tp - 1))

    wait1 = fanout(ny, nz, me, col, sent_ref, got1, send1, recv1)
    lane = lax.broadcasted_iota(jnp.int32, (1, 128), 1)
    low = lane < 64
    loads[0].wait()
    for r in range(rows):
        key = kv_ref[r, 0:1, :].astype(jnp.float32)
        value = kv_ref[r, 1:2, :].astype(jnp.float32)
        fresh_k = jnp.concatenate([key, key], axis=1).astype(jnp.bfloat16)
        fresh_v = jnp.concatenate([value, value], axis=1)
        count = splits_ref[r].astype(jnp.float32)
        top, total, mixed = attend_tile(
            widen(queries_ref[r : r + 1, :].astype(jnp.float32), heads),
            home_ref[r, 0, 0],
            home_ref[r, 1, 0],
            count,
            fresh_k,
            fresh_v,
        )
        for h in range(pairs):
            u, m, l = pair_rows(top, total, mixed, h)
            stat[0, h, r : r + 1, :] = u
            stat[1, h, r : r + 1, :] = m
            stat[2, h, r : r + 1, :] = l
    wait1()
    loads[1].wait()

    partner = helpers_ref[0] // rows
    block = got1[partner]
    pick_row = lax.broadcasted_iota(jnp.int32, (slots, rows), 0)
    pick_col = lax.broadcasted_iota(jnp.int32, (slots, rows), 1)
    pick = jnp.zeros((slots, rows), jnp.float32)
    for k in range(slots):
        pick = jnp.where((pick_row == k) & (pick_col == helpers_ref[k] % rows), 1.0, pick)
    chosen = jnp.dot(pick.astype(jnp.bfloat16), block, preferred_element_type=jnp.float32)
    for k in range(slots):
        count = chosen[k : k + 1, qw : qw + 1] * 32.0 + chosen[k : k + 1, qw + 1 : qw + 2]
        top, total, mixed = attend_tile(
            widen(chosen[k : k + 1, :qw], heads), help_ref[k, 0, 0], help_ref[k, 1, 0], count
        )
        for h in range(pairs):
            u, m, l = pair_rows(top, total, mixed, h)
            back[k * pairs + h : k * pairs + h + 1, :] = u
            back[(slots + k) * pairs + h : (slots + k) * pairs + h + 1, :] = m
            back[(2 * slots + k) * pairs + h : (2 * slots + k) * pairs + h + 1, :] = l

    wait2 = fanout(ny, nz, me, col, back, got2, send2, recv2)

    sel_row = lax.broadcasted_iota(jnp.int32, (rows, slots), 0)
    sel_col = lax.broadcasted_iota(jnp.int32, (rows, slots), 1)
    fsel = jnp.zeros((rows, slots), jnp.float32)
    rank = jnp.int32(0)
    for r in range(rows):
        is_long = lengths_ref[r] > LONG_AT
        fsel = jnp.where((sel_row == r) & (sel_col == rank) & is_long, 1.0, fsel)
        rank = rank + is_long.astype(jnp.int32)
    has = fsel[:, 0:1]
    for k in range(1, slots):
        has = has + fsel[:, k : k + 1]
    wait2()

    loads[2].wait()
    theirs = got2[partner]
    acc = jnp.zeros(part.shape, jnp.float32)
    for h in range(pairs):

        def pick_far(base):
            x = fsel[:, 0:1] * theirs[base + h : base + h + 1, :]
            for k in range(1, slots):
                r0 = base + k * pairs + h
                x = x + fsel[:, k : k + 1] * theirs[r0 : r0 + 1, :]
            return x

        far_u = pick_far(0)
        far_m = jnp.where(has > 0.0, pick_far(slots * pairs), -1e30)
        far_l = pick_far(2 * slots * pairs)
        home_u = stat[0, h]
        home_m = stat[1, h]
        home_l = stat[2, h]
        top = jnp.maximum(home_m, far_m)
        home_e = jnp.exp(home_m - top)
        far_e = jnp.exp(far_m - top)
        mix = (home_u * home_e + far_u * far_e) / (home_l * home_e + far_l * far_e)
        acc = acc + jnp.dot(
            mix.astype(jnp.bfloat16),
            w_ref[h * 128 : (h + 1) * 128, :],
            preferred_element_type=jnp.float32,
        )
    part[...] = acc

    sends = []
    for k in range(1, n_tp):
        peer = lax.rem(col + k, n_tp)
        cols = pl.ds(pl.multiple_of(peer * width, width), width)
        copy = pltpu.make_async_remote_copy(
            src_ref=part.at[:, cols],
            dst_ref=held.at[k],
            send_sem=send3.at[k],
            recv_sem=recv3.at[k],
            device_id=(me, peer),
            device_id_type=MESH,
        )
        copy.start()
        sends.append(copy)
    own = pl.ds(pl.multiple_of(col * width, width), width)
    total = part[:, own]
    for copy in sends:
        copy.wait_send()
        copy.wait_recv()
    for k in range(1, n_tp):
        total = total + held[k]
    out_ref[...] = total.astype(out_ref.dtype)


def per_device(ny, nz, queries, new_kv, home_cache, help_cache, lengths, split_at, helper_req, out_weight):
    n_grp = lax.axis_size("grp")
    n_tp = lax.axis_size("tp")
    row_count, width = queries.shape
    slots = help_cache.shape[0]
    pairs = width // 128
    lanes = 128

    sent_shape = (row_count, width + lanes)

    out_cols = out_weight.shape[1] // n_tp
    vmem = pl.BlockSpec(memory_space=pltpu.VMEM)
    smem = pl.BlockSpec(memory_space=pltpu.SMEM)
    back_rows = 3 * slots * pairs
    return pl.pallas_call(
        functools.partial(whole_kernel, ny, nz, n_tp, slots),
        out_shape=jax.ShapeDtypeStruct((row_count, out_cols), jnp.float32),
        in_specs=[smem] * 3 + [vmem] * 2 + [pl.BlockSpec(memory_space=pl.ANY)] * 3,
        out_specs=vmem,
        scratch_shapes=[
            pltpu.VMEM(sent_shape, jnp.bfloat16),
            pltpu.VMEM(home_cache.shape, home_cache.dtype),
            pltpu.VMEM(help_cache.shape, help_cache.dtype),
            pltpu.VMEM(out_weight.shape, out_weight.dtype),
            pltpu.SemaphoreType.DMA((3,)),
            pltpu.VMEM((n_grp,) + sent_shape, jnp.bfloat16),
            pltpu.VMEM((n_grp, back_rows, lanes), jnp.float32),
            pltpu.VMEM((back_rows, lanes), jnp.float32),
            pltpu.VMEM((3, pairs, row_count, lanes), jnp.float32),
            pltpu.VMEM((row_count, out_weight.shape[1]), jnp.float32),
            pltpu.VMEM((n_tp, row_count, out_cols), jnp.float32),
            pltpu.SemaphoreType.DMA((n_grp,)),
            pltpu.SemaphoreType.DMA((n_grp,)),
            pltpu.SemaphoreType.DMA((n_grp,)),
            pltpu.SemaphoreType.DMA((n_grp,)),
            pltpu.SemaphoreType.DMA((n_tp,)),
            pltpu.SemaphoreType.DMA((n_tp,)),
        ],
        compiler_params=pltpu.CompilerParams(collective_id=0, has_side_effects=True),
    )(lengths, split_at, helper_req, queries, new_kv, home_cache, help_cache, out_weight).astype(jnp.bfloat16)


def grp_rows(mesh):
    column = list(mesh.devices[:, 0])
    n = len(column)
    coords = [getattr(d, "coords", None) for d in column]
    if coords[0] is not None:
        nz = 1
        while nz < n and coords[nz][1] == coords[0][1]:
            nz += 1
    else:
        nz = 1
        while nz * nz < n:
            nz *= 2
    return n // nz, nz


def solution(mesh):
    ny, nz = grp_rows(mesh)
    return jax.shard_map(
        functools.partial(per_device, ny, nz),
        mesh=mesh,
        in_specs=(
            P("grp", "tp"),
            P("grp", None, "tp"),
            P("grp", None, "tp", None, None),
            P("grp", None, "tp", None, None),
            P("grp"),
            P("grp"),
            P("grp"),
            P("tp", None),
        ),
        out_specs=P("grp", "tp"),
        check_vma=False,
    )
```

```python
import functools

import jax
import jax.numpy as jnp
from jax import lax
from jax.experimental import pallas as pl
from jax.experimental.pallas import tpu as pltpu
from jax.sharding import PartitionSpec as P

MESH = pl.DeviceIdType.MESH
LONG_AT = 1024


def attend(queries, cache, count, fresh):
    row_count = queries.shape[0]
    kv_heads = cache.shape[2]
    head_width = cache.shape[4] // 2
    half = cache.shape[3]
    group_size = queries.shape[1] // (kv_heads * head_width)
    score_scale = head_width ** (-0.5)
    head_rows = queries.reshape(row_count, kv_heads, group_size, head_width)
    blank = jnp.zeros_like(head_rows)
    wide_rows = jnp.stack(
        [
            jnp.concatenate([head_rows, blank], axis=-1),
            jnp.concatenate([blank, head_rows], axis=-1),
        ],
        axis=3,
    )
    key_rows = cache[:, 0]
    value_rows = cache[:, 1]
    scores = (
        jnp.einsum("nkgjc,nkpc->nkgjp", wide_rows, key_rows, preferred_element_type=jnp.float32)
        * score_scale
    )
    position = 2 * jnp.arange(half)[None, :] + jnp.arange(2)[:, None]
    inside = (position[None] < count[:, None, None])[:, None, None]
    top_score = jnp.max(jnp.where(inside, scores, -1e30), axis=(-2, -1))
    if fresh is not None:
        fresh_key = fresh[:, 0].reshape(row_count, kv_heads, head_width)
        fresh_score = (
            jnp.einsum("nkgd,nkd->nkg", head_rows, fresh_key, preferred_element_type=jnp.float32)
            * score_scale
        )
        top_score = jnp.maximum(top_score, fresh_score)
    weights = jnp.where(
        inside, jnp.exp(scores - top_score[..., None, None]), 0.0
    ).astype(jnp.bfloat16)
    weight_sum = jnp.sum(weights.astype(jnp.float32), axis=(-2, -1))
    both = jnp.einsum(
        "nkgjp,nkpc->nkgjc", weights, value_rows, preferred_element_type=jnp.float32
    )
    mixed_sum = both[..., 0, :head_width] + both[..., 1, head_width:]
    if fresh is not None:
        fresh_weight = lax.optimization_barrier(
            jnp.exp(fresh_score - top_score).astype(jnp.bfloat16)
        ).astype(jnp.float32)
        weight_sum = weight_sum + fresh_weight
        fresh_value = fresh[:, 1].reshape(row_count, kv_heads, 1, head_width).astype(jnp.float32)
        mixed_sum = mixed_sum + fresh_weight[..., None] * fresh_value
    return (
        top_score.reshape(row_count, -1),
        weight_sum.reshape(row_count, -1),
        mixed_sum.reshape(row_count, -1, head_width),
    )


def gather_kernel(n, x_ref, out_ref, held, send_sem, recv_sem):
    me = lax.axis_index("grp")
    col = lax.axis_index("tp")

    barrier = pltpu.get_barrier_semaphore()

    def greet(k, carry):
        peer = lax.rem(me + k, n)
        pl.semaphore_signal(barrier, inc=1, device_id=(peer, col), device_id_type=MESH)
        return carry

    lax.fori_loop(1, n, greet, 0)
    pl.semaphore_wait(barrier, n - 1)

    def copy_to(k):
        peer = lax.rem(me + k, n)
        return pltpu.make_async_remote_copy(
            src_ref=x_ref,
            dst_ref=held.at[me],
            send_sem=send_sem.at[k],
            recv_sem=recv_sem.at[k],
            device_id=(peer, col),
            device_id_type=MESH,
        )

    def copy_from(k):
        source = lax.rem(me + n - k, n)
        return pltpu.make_async_remote_copy(
            src_ref=x_ref,
            dst_ref=held.at[source],
            send_sem=send_sem.at[k],
            recv_sem=recv_sem.at[k],
            device_id=(source, col),
            device_id_type=MESH,
        )

    def start(k, carry):
        copy_to(k).start()
        return carry

    lax.fori_loop(1, n, start, 0)

    def finish(k, carry):
        copy_to(k).wait_send()
        copy_from(k).wait_recv()
        return carry

    lax.fori_loop(1, n, finish, 0)
    held[me] = x_ref[...]
    out_ref[...] = held[...]


def gather_grp(x, n, cid):
    return pl.pallas_call(
        functools.partial(gather_kernel, n),
        out_shape=jax.ShapeDtypeStruct((n,) + x.shape, x.dtype),
        in_specs=[pl.BlockSpec(memory_space=pltpu.VMEM)],
        out_specs=pl.BlockSpec(memory_space=pltpu.VMEM),
        scratch_shapes=[
            pltpu.VMEM((n,) + x.shape, x.dtype),
            pltpu.SemaphoreType.DMA((n,)),
            pltpu.SemaphoreType.DMA((n,)),
        ],
        compiler_params=pltpu.CompilerParams(collective_id=cid, has_side_effects=True),
    )(x)


def far_first(i, size):
    half = size // 2
    return half + i // 2 if i % 2 == 0 else half - (i + 1) // 2


def fanout(ny, nz, me, col, src, dst, send, recv):
    my_y = me // nz
    my_z = me % nz
    order = [(far_first(a, ny), far_first(b, nz)) for a in range(ny) for b in range(nz)][:-1]

    def copy(k, peer, slot):
        return pltpu.make_async_remote_copy(
            src_ref=src,
            dst_ref=dst.at[slot],
            send_sem=send.at[k],
            recv_sem=recv.at[k],
            device_id=(peer, col),
            device_id_type=MESH,
        )

    targets = []
    for k, (dy, dz) in enumerate(order):
        peer = lax.rem(my_y + dy, ny) * nz + lax.rem(my_z + dz, nz)
        out = copy(k, peer, me)
        out.start()
        targets.append(out)

    def finish():
        for k, (dy, dz) in enumerate(order):
            targets[k].wait_send()
            source = lax.rem(my_y + (ny - dy), ny) * nz + lax.rem(my_z + (nz - dz), nz)
            copy(k, source, source).wait_recv()

    return finish


def attend_tile(wide, keys, values, count, fresh_k=None, fresh_v=None):
    rows = wide.shape[0]
    scores = lax.dot_general(
        wide, keys, (((1,), (1,)), ((), ())), preferred_element_type=jnp.float32
    ) * 0.125
    half = rows // 2
    row = lax.broadcasted_iota(jnp.int32, scores.shape, 0)
    lane = lax.broadcasted_iota(jnp.int32, scores.shape, 1)
    position = 2 * lane + jnp.where(row >= half, 1, 0)
    inside = position.astype(jnp.float32) < count
    top = jnp.max(jnp.where(inside, scores, -1e30), axis=1, keepdims=True)
    top = jnp.maximum(top, pltpu.roll(top, half, 0))
    if fresh_k is not None:
        fresh_score = jnp.sum(
            wide.astype(jnp.float32) * fresh_k.astype(jnp.float32), axis=1, keepdims=True
        ) * 0.125
        top = jnp.maximum(top, fresh_score)
    weights = jnp.where(inside, jnp.exp(scores - top), 0.0).astype(jnp.bfloat16)
    total = jnp.sum(weights.astype(jnp.float32), axis=1, keepdims=True)
    total = total + pltpu.roll(total, half, 0)
    both = jnp.dot(weights, values, preferred_element_type=jnp.float32)
    mixed = both + pltpu.roll(pltpu.roll(both, half, 0), 64, 1)
    if fresh_k is not None:
        fresh_w = jnp.exp(fresh_score - top).astype(jnp.bfloat16).astype(jnp.float32)
        total = total + fresh_w
        mixed = mixed + fresh_w * fresh_v
    return top, total, mixed


def pair_rows(top, total, mixed, h):
    lane = lax.broadcasted_iota(jnp.int32, (1, mixed.shape[1]), 1)
    left = lane < 64
    g = 2 * h
    u = jnp.where(left, mixed[g : g + 1, :], mixed[g + 5 : g + 6, :])
    m = jnp.where(left, top[g : g + 1, :], top[g + 1 : g + 2, :])
    l = jnp.where(left, total[g : g + 1, :], total[g + 1 : g + 2, :])
    return u, m, l


def widen(q, heads):
    lane = lax.broadcasted_iota(jnp.int32, (2 * heads, 128), 1)
    row = lax.broadcasted_iota(jnp.int32, (2 * heads, 128), 0)
    low = lane < 64
    wide = jnp.zeros((2 * heads, 128), jnp.float32)
    for h in range(heads // 2):
        a = q[:, h * 128 : (h + 1) * 128]
        turned = pltpu.roll(a, 64, 1)
        g = 2 * h
        wide = jnp.where((row == g) & low, a, wide)
        wide = jnp.where((row == g + 1) & low, turned, wide)
        wide = jnp.where((row == heads + g) & ~low, turned, wide)
        wide = jnp.where((row == heads + g + 1) & ~low, a, wide)
    return wide.astype(jnp.bfloat16)


def whole_kernel(ny, nz, n_tp, slots, lengths_ref, splits_ref, helpers_ref, queries_ref, kv_ref,
                 home_hbm, help_hbm, w_hbm, out_ref, sent_ref, home_ref, help_ref, w_ref, local,
                 got1, got2, back, stat, part, held, send1, recv1, send2, recv2, send3, recv3):
    n = ny * nz
    me = lax.axis_index("grp")
    col = lax.axis_index("tp")
    rows = queries_ref.shape[0]
    heads = w_ref.shape[0] // 64
    qw = heads * 64

    code_row = lax.broadcasted_iota(jnp.int32, (rows, 128), 0)
    code_lane = lax.broadcasted_iota(jnp.int32, (rows, 128), 1)
    code = jnp.zeros((rows, 128), jnp.float32)
    for r in range(rows):
        count = lengths_ref[r] - splits_ref[r]
        code = jnp.where((code_row == r) & (code_lane == 0), (count // 32).astype(jnp.float32), code)
        code = jnp.where((code_row == r) & (code_lane == 1), (count % 32).astype(jnp.float32), code)
    sent_ref[:, :qw] = queries_ref[...]
    sent_ref[:, qw:] = code.astype(sent_ref.dtype)
    pairs = w_ref.shape[0] // 128
    width = out_ref.shape[1]

    barrier = pltpu.get_barrier_semaphore()

    my_y = me // nz
    my_z = me % nz
    for a in range(ny):
        for b in range(nz):
            dy, dz = far_first(a, ny), far_first(b, nz)
            if dy == 0 and dz == 0:
                continue
            peer = lax.rem(my_y + dy, ny) * nz + lax.rem(my_z + dz, nz)
            pl.semaphore_signal(barrier, inc=1, device_id=(peer, col), device_id_type=MESH)
    for k in range(1, n_tp):
        peer = lax.rem(col + k, n_tp)
        pl.semaphore_signal(barrier, inc=1, device_id=(me, peer), device_id_type=MESH)
    loads = [
        pltpu.make_async_copy(hbm, vmem, local.at[i])
        for i, (hbm, vmem) in enumerate(
            [(home_hbm, home_ref), (help_hbm, help_ref), (w_hbm, w_ref)]
        )
    ]
    for load in loads:
        load.start()
    pl.semaphore_wait(barrier, (n - 1) + (n_tp - 1))

    wait1 = fanout(ny, nz, me, col, sent_ref, got1, send1, recv1)
    lane = lax.broadcasted_iota(jnp.int32, (1, 128), 1)
    low = lane < 64
    loads[0].wait()
    for r in range(rows):
        key = kv_ref[r, 0:1, :].astype(jnp.float32)
        value = kv_ref[r, 1:2, :].astype(jnp.float32)
        fresh_k = jnp.concatenate([key, key], axis=1).astype(jnp.bfloat16)
        fresh_v = jnp.concatenate([value, value], axis=1)
        count = splits_ref[r].astype(jnp.float32)
        top, total, mixed = attend_tile(
            widen(queries_ref[r : r + 1, :].astype(jnp.float32), heads),
            home_ref[r, 0, 0],
            home_ref[r, 1, 0],
            count,
            fresh_k,
            fresh_v,
        )
        for h in range(pairs):
            u, m, l = pair_rows(top, total, mixed, h)
            stat[0, h, r : r + 1, :] = u
            stat[1, h, r : r + 1, :] = m
            stat[2, h, r : r + 1, :] = l
    wait1()
    loads[1].wait()

    partner = helpers_ref[0] // rows
    block = got1[partner]
    pick_row = lax.broadcasted_iota(jnp.int32, (slots, rows), 0)
    pick_col = lax.broadcasted_iota(jnp.int32, (slots, rows), 1)
    pick = jnp.zeros((slots, rows), jnp.float32)
    for k in range(slots):
        pick = jnp.where((pick_row == k) & (pick_col == helpers_ref[k] % rows), 1.0, pick)
    chosen = jnp.dot(pick.astype(jnp.bfloat16), block, preferred_element_type=jnp.float32)
    stat_lane = lax.broadcasted_iota(jnp.int32, (1, 128), 1)
    stat_row = jnp.zeros((1, 128), jnp.float32)
    for k in range(slots):
        count = chosen[k : k + 1, qw : qw + 1] * 32.0 + chosen[k : k + 1, qw + 1 : qw + 2]
        top, total, mixed = attend_tile(
            widen(chosen[k : k + 1, :qw], heads), help_ref[k, 0, 0], help_ref[k, 1, 0], count
        )
        for h in range(pairs):
            u, m, l = pair_rows(top, total, mixed, h)
            back[k * pairs + h : k * pairs + h + 1, :] = u
        for g in range(heads):
            stat_row = jnp.where(stat_lane == k * heads + g, top[g : g + 1, :], stat_row)
            stat_row = jnp.where(
                stat_lane == (slots + k) * heads + g, total[g : g + 1, :], stat_row
            )
    back[slots * pairs : slots * pairs + 1, :] = stat_row

    wait2 = fanout(ny, nz, me, col, back, got2, send2, recv2)

    sel_row = lax.broadcasted_iota(jnp.int32, (rows, slots), 0)
    sel_col = lax.broadcasted_iota(jnp.int32, (rows, slots), 1)
    fsel = jnp.zeros((rows, slots), jnp.float32)
    rank = jnp.int32(0)
    for r in range(rows):
        is_long = lengths_ref[r] > LONG_AT
        fsel = jnp.where((sel_row == r) & (sel_col == rank) & is_long, 1.0, fsel)
        rank = rank + is_long.astype(jnp.int32)
    has = fsel[:, 0:1]
    for k in range(1, slots):
        has = has + fsel[:, k : k + 1]
    wait2()

    loads[2].wait()
    theirs = got2[partner]
    stats = theirs[slots * pairs : slots * pairs + 1, :]
    left = lax.broadcasted_iota(jnp.int32, (1, 128), 1) < 64
    acc = jnp.zeros(part.shape, jnp.float32)
    for h in range(pairs):
        far_u = fsel[:, 0:1] * theirs[h : h + 1, :]
        for k in range(1, slots):
            far_u = far_u + fsel[:, k : k + 1] * theirs[k * pairs + h : k * pairs + h + 1, :]

        def pick_stat(base):
            x = None
            for k in range(slots):
                j = base + k * heads + 2 * h
                val = jnp.where(left, stats[:, j : j + 1], stats[:, j + 1 : j + 2])
                x = fsel[:, k : k + 1] * val if x is None else x + fsel[:, k : k + 1] * val
            return x

        far_m = jnp.where(has > 0.0, pick_stat(0), -1e30)
        far_l = pick_stat(slots * heads)
        home_u = stat[0, h]
        home_m = stat[1, h]
        home_l = stat[2, h]
        top = jnp.maximum(home_m, far_m)
        home_e = jnp.exp(home_m - top)
        far_e = jnp.exp(far_m - top)
        mix = (home_u * home_e + far_u * far_e) / (home_l * home_e + far_l * far_e)
        acc = acc + jnp.dot(
            mix.astype(jnp.bfloat16),
            w_ref[h * 128 : (h + 1) * 128, :],
            preferred_element_type=jnp.float32,
        )
    part[...] = acc

    sends = []
    for k in range(1, n_tp):
        peer = lax.rem(col + k, n_tp)
        cols = pl.ds(pl.multiple_of(peer * width, width), width)
        copy = pltpu.make_async_remote_copy(
            src_ref=part.at[:, cols],
            dst_ref=held.at[k],
            send_sem=send3.at[k],
            recv_sem=recv3.at[k],
            device_id=(me, peer),
            device_id_type=MESH,
        )
        copy.start()
        sends.append(copy)
    own = pl.ds(pl.multiple_of(col * width, width), width)
    total = part[:, own]
    for copy in sends:
        copy.wait_send()
        copy.wait_recv()
    for k in range(1, n_tp):
        total = total + held[k]
    out_ref[...] = total.astype(out_ref.dtype)


def per_device(ny, nz, queries, new_kv, home_cache, help_cache, lengths, split_at, helper_req, out_weight):
    n_grp = lax.axis_size("grp")
    n_tp = lax.axis_size("tp")
    row_count, width = queries.shape
    slots = help_cache.shape[0]
    pairs = width // 128
    lanes = 128

    sent_shape = (row_count, width + lanes)

    out_cols = out_weight.shape[1] // n_tp
    vmem = pl.BlockSpec(memory_space=pltpu.VMEM)
    smem = pl.BlockSpec(memory_space=pltpu.SMEM)
    back_rows = slots * pairs + 1
    return pl.pallas_call(
        functools.partial(whole_kernel, ny, nz, n_tp, slots),
        out_shape=jax.ShapeDtypeStruct((row_count, out_cols), jnp.bfloat16),
        in_specs=[smem] * 3 + [vmem] * 2 + [pl.BlockSpec(memory_space=pl.ANY)] * 3,
        out_specs=vmem,
        scratch_shapes=[
            pltpu.VMEM(sent_shape, jnp.bfloat16),
            pltpu.VMEM(home_cache.shape, home_cache.dtype),
            pltpu.VMEM(help_cache.shape, help_cache.dtype),
            pltpu.VMEM(out_weight.shape, out_weight.dtype),
            pltpu.SemaphoreType.DMA((3,)),
            pltpu.VMEM((n_grp,) + sent_shape, jnp.bfloat16),
            pltpu.VMEM((n_grp, back_rows, lanes), jnp.float32),
            pltpu.VMEM((back_rows, lanes), jnp.float32),
            pltpu.VMEM((3, pairs, row_count, lanes), jnp.float32),
            pltpu.VMEM((row_count, out_weight.shape[1]), jnp.float32),
            pltpu.VMEM((n_tp, row_count, out_cols), jnp.float32),
            pltpu.SemaphoreType.DMA((n_grp,)),
            pltpu.SemaphoreType.DMA((n_grp,)),
            pltpu.SemaphoreType.DMA((n_grp,)),
            pltpu.SemaphoreType.DMA((n_grp,)),
            pltpu.SemaphoreType.DMA((n_tp,)),
            pltpu.SemaphoreType.DMA((n_tp,)),
        ],
        compiler_params=pltpu.CompilerParams(collective_id=0, has_side_effects=True),
    )(lengths, split_at, helper_req, queries, new_kv, home_cache, help_cache, out_weight)


def grp_rows(mesh):
    column = list(mesh.devices[:, 0])
    n = len(column)
    coords = [getattr(d, "coords", None) for d in column]
    if coords[0] is not None:
        nz = 1
        while nz < n and coords[nz][1] == coords[0][1]:
            nz += 1
    else:
        nz = 1
        while nz * nz < n:
            nz *= 2
    return n // nz, nz


def solution(mesh):
    ny, nz = grp_rows(mesh)
    return jax.shard_map(
        functools.partial(per_device, ny, nz),
        mesh=mesh,
        in_specs=(
            P("grp", "tp"),
            P("grp", None, "tp"),
            P("grp", None, "tp", None, None),
            P("grp", None, "tp", None, None),
            P("grp"),
            P("grp"),
            P("grp"),
            P("tp", None),
        ),
        out_specs=P("grp", "tp"),
        check_vma=False,
    )
```

```python
import functools

import jax
import jax.numpy as jnp
from jax import lax
from jax.experimental import pallas as pl
from jax.experimental.pallas import tpu as pltpu
from jax.sharding import PartitionSpec as P

MESH = pl.DeviceIdType.MESH
LONG_AT = 1024


def attend(queries, cache, count, fresh):
    row_count = queries.shape[0]
    kv_heads = cache.shape[2]
    head_width = cache.shape[4] // 2
    half = cache.shape[3]
    group_size = queries.shape[1] // (kv_heads * head_width)
    score_scale = head_width ** (-0.5)
    head_rows = queries.reshape(row_count, kv_heads, group_size, head_width)
    blank = jnp.zeros_like(head_rows)
    wide_rows = jnp.stack(
        [
            jnp.concatenate([head_rows, blank], axis=-1),
            jnp.concatenate([blank, head_rows], axis=-1),
        ],
        axis=3,
    )
    key_rows = cache[:, 0]
    value_rows = cache[:, 1]
    scores = (
        jnp.einsum("nkgjc,nkpc->nkgjp", wide_rows, key_rows, preferred_element_type=jnp.float32)
        * score_scale
    )
    position = 2 * jnp.arange(half)[None, :] + jnp.arange(2)[:, None]
    inside = (position[None] < count[:, None, None])[:, None, None]
    top_score = jnp.max(jnp.where(inside, scores, -1e30), axis=(-2, -1))
    if fresh is not None:
        fresh_key = fresh[:, 0].reshape(row_count, kv_heads, head_width)
        fresh_score = (
            jnp.einsum("nkgd,nkd->nkg", head_rows, fresh_key, preferred_element_type=jnp.float32)
            * score_scale
        )
        top_score = jnp.maximum(top_score, fresh_score)
    weights = jnp.where(
        inside, jnp.exp(scores - top_score[..., None, None]), 0.0
    ).astype(jnp.bfloat16)
    weight_sum = jnp.sum(weights.astype(jnp.float32), axis=(-2, -1))
    both = jnp.einsum(
        "nkgjp,nkpc->nkgjc", weights, value_rows, preferred_element_type=jnp.float32
    )
    mixed_sum = both[..., 0, :head_width] + both[..., 1, head_width:]
    if fresh is not None:
        fresh_weight = lax.optimization_barrier(
            jnp.exp(fresh_score - top_score).astype(jnp.bfloat16)
        ).astype(jnp.float32)
        weight_sum = weight_sum + fresh_weight
        fresh_value = fresh[:, 1].reshape(row_count, kv_heads, 1, head_width).astype(jnp.float32)
        mixed_sum = mixed_sum + fresh_weight[..., None] * fresh_value
    return (
        top_score.reshape(row_count, -1),
        weight_sum.reshape(row_count, -1),
        mixed_sum.reshape(row_count, -1, head_width),
    )


def gather_kernel(n, x_ref, out_ref, held, send_sem, recv_sem):
    me = lax.axis_index("grp")
    col = lax.axis_index("tp")

    barrier = pltpu.get_barrier_semaphore()

    def greet(k, carry):
        peer = lax.rem(me + k, n)
        pl.semaphore_signal(barrier, inc=1, device_id=(peer, col), device_id_type=MESH)
        return carry

    lax.fori_loop(1, n, greet, 0)
    pl.semaphore_wait(barrier, n - 1)

    def copy_to(k):
        peer = lax.rem(me + k, n)
        return pltpu.make_async_remote_copy(
            src_ref=x_ref,
            dst_ref=held.at[me],
            send_sem=send_sem.at[k],
            recv_sem=recv_sem.at[k],
            device_id=(peer, col),
            device_id_type=MESH,
        )

    def copy_from(k):
        source = lax.rem(me + n - k, n)
        return pltpu.make_async_remote_copy(
            src_ref=x_ref,
            dst_ref=held.at[source],
            send_sem=send_sem.at[k],
            recv_sem=recv_sem.at[k],
            device_id=(source, col),
            device_id_type=MESH,
        )

    def start(k, carry):
        copy_to(k).start()
        return carry

    lax.fori_loop(1, n, start, 0)

    def finish(k, carry):
        copy_to(k).wait_send()
        copy_from(k).wait_recv()
        return carry

    lax.fori_loop(1, n, finish, 0)
    held[me] = x_ref[...]
    out_ref[...] = held[...]


def gather_grp(x, n, cid):
    return pl.pallas_call(
        functools.partial(gather_kernel, n),
        out_shape=jax.ShapeDtypeStruct((n,) + x.shape, x.dtype),
        in_specs=[pl.BlockSpec(memory_space=pltpu.VMEM)],
        out_specs=pl.BlockSpec(memory_space=pltpu.VMEM),
        scratch_shapes=[
            pltpu.VMEM((n,) + x.shape, x.dtype),
            pltpu.SemaphoreType.DMA((n,)),
            pltpu.SemaphoreType.DMA((n,)),
        ],
        compiler_params=pltpu.CompilerParams(collective_id=cid, has_side_effects=True),
    )(x)


def far_first(i, size):
    half = size // 2
    return half + i // 2 if i % 2 == 0 else half - (i + 1) // 2


def fanout(ny, nz, me, col, src, dst, send, recv):
    my_y = me // nz
    my_z = me % nz
    order = [(far_first(a, ny), far_first(b, nz)) for a in range(ny) for b in range(nz)][:-1]

    def copy(k, peer, slot):
        return pltpu.make_async_remote_copy(
            src_ref=src,
            dst_ref=dst.at[slot],
            send_sem=send.at[k],
            recv_sem=recv.at[k],
            device_id=(peer, col),
            device_id_type=MESH,
        )

    targets = []
    for k, (dy, dz) in enumerate(order):
        peer = lax.rem(my_y + dy, ny) * nz + lax.rem(my_z + dz, nz)
        out = copy(k, peer, me)
        out.start()
        targets.append(out)

    def finish():
        for k, (dy, dz) in enumerate(order):
            targets[k].wait_send()
            source = lax.rem(my_y + (ny - dy), ny) * nz + lax.rem(my_z + (nz - dz), nz)
            copy(k, source, source).wait_recv()

    return finish


def attend_tile(wide, keys, values, count, fresh_k=None, fresh_v=None):
    rows = wide.shape[0]
    scores = lax.dot_general(
        wide, keys, (((1,), (1,)), ((), ())), preferred_element_type=jnp.float32
    ) * 0.125
    half = rows // 2
    row = lax.broadcasted_iota(jnp.int32, scores.shape, 0)
    lane = lax.broadcasted_iota(jnp.int32, scores.shape, 1)
    position = 2 * lane + jnp.where(row >= half, 1, 0)
    inside = position.astype(jnp.float32) < count
    top = jnp.max(jnp.where(inside, scores, -1e30), axis=1, keepdims=True)
    top = jnp.maximum(top, pltpu.roll(top, half, 0))
    if fresh_k is not None:
        fresh_score = jnp.sum(
            wide.astype(jnp.float32) * fresh_k.astype(jnp.float32), axis=1, keepdims=True
        ) * 0.125
        top = jnp.maximum(top, fresh_score)
    weights = jnp.where(inside, jnp.exp(scores - top), 0.0).astype(jnp.bfloat16)
    total = jnp.sum(weights.astype(jnp.float32), axis=1, keepdims=True)
    total = total + pltpu.roll(total, half, 0)
    both = jnp.dot(weights, values, preferred_element_type=jnp.float32)
    mixed = both + pltpu.roll(pltpu.roll(both, half, 0), 64, 1)
    if fresh_k is not None:
        fresh_w = jnp.exp(fresh_score - top).astype(jnp.bfloat16).astype(jnp.float32)
        total = total + fresh_w
        mixed = mixed + fresh_w * fresh_v
    return top, total, mixed


def pair_rows(top, total, mixed, h):
    lane = lax.broadcasted_iota(jnp.int32, (1, mixed.shape[1]), 1)
    left = lane < 64
    g = 2 * h
    u = jnp.where(left, mixed[g : g + 1, :], mixed[g + 5 : g + 6, :])
    m = jnp.where(left, top[g : g + 1, :], top[g + 1 : g + 2, :])
    l = jnp.where(left, total[g : g + 1, :], total[g + 1 : g + 2, :])
    return u, m, l


def widen(pieces, heads):
    lane = lax.broadcasted_iota(jnp.int32, (2 * heads, 128), 1)
    row = lax.broadcasted_iota(jnp.int32, (2 * heads, 128), 0)
    low = lane < 64
    wide = jnp.zeros((2 * heads, 128), jnp.float32)
    for h in range(heads // 2):
        a = pieces[h]
        turned = pltpu.roll(a, 64, 1)
        g = 2 * h
        wide = jnp.where((row == g) & low, a, wide)
        wide = jnp.where((row == g + 1) & low, turned, wide)
        wide = jnp.where((row == heads + g) & ~low, turned, wide)
        wide = jnp.where((row == heads + g + 1) & ~low, a, wide)
    return wide.astype(jnp.bfloat16)


def whole_kernel(ny, nz, n_tp, slots, lengths_ref, splits_ref, helpers_ref, queries_ref, kv_ref,
                 home_hbm, help_hbm, w_hbm, out_ref, sent_ref, home_ref, help_ref, w_ref, local,
                 got1, got2, back, stat, part, held, send1, recv1, send2, recv2, send3, recv3):
    n = ny * nz
    me = lax.axis_index("grp")
    col = lax.axis_index("tp")
    rows = queries_ref.shape[0]
    heads = w_ref.shape[0] // 64
    qw = heads * 64

    pairs = heads // 2
    pick_row = lax.broadcasted_iota(jnp.int32, (slots, rows), 0)
    pick_col = lax.broadcasted_iota(jnp.int32, (slots, rows), 1)
    code_lane = lax.broadcasted_iota(jnp.int32, (1, 128), 1)
    pick = jnp.zeros((slots, rows), jnp.float32)
    code = jnp.zeros((1, 128), jnp.float32)
    rank = jnp.int32(0)
    for r in range(rows):
        is_long = lengths_ref[r] > LONG_AT
        count = lengths_ref[r] - splits_ref[r]
        pick = jnp.where((pick_row == rank) & (pick_col == r) & is_long, 1.0, pick)
        code = jnp.where((code_lane == rank) & is_long, (count // 32).astype(jnp.float32), code)
        code = jnp.where(
            (code_lane == slots + rank) & is_long, (count % 32).astype(jnp.float32), code
        )
        rank = rank + is_long.astype(jnp.int32)
    long_q = jnp.dot(pick.astype(jnp.bfloat16), queries_ref[...], preferred_element_type=jnp.float32)
    pay_row = lax.broadcasted_iota(jnp.int32, sent_ref.shape, 0)
    pay = jnp.where(pay_row == slots * pairs, code, 0.0)
    for k in range(slots):
        for h in range(pairs):
            pay = jnp.where(pay_row == k * pairs + h, long_q[k : k + 1, h * 128 : (h + 1) * 128], pay)
    sent_ref[...] = pay.astype(sent_ref.dtype)
    width = out_ref.shape[1]

    barrier = pltpu.get_barrier_semaphore()

    my_y = me // nz
    my_z = me % nz
    for a in range(ny):
        for b in range(nz):
            dy, dz = far_first(a, ny), far_first(b, nz)
            if dy == 0 and dz == 0:
                continue
            peer = lax.rem(my_y + dy, ny) * nz + lax.rem(my_z + dz, nz)
            pl.semaphore_signal(barrier, inc=1, device_id=(peer, col), device_id_type=MESH)
    for k in range(1, n_tp):
        peer = lax.rem(col + k, n_tp)
        pl.semaphore_signal(barrier, inc=1, device_id=(me, peer), device_id_type=MESH)
    loads = [
        pltpu.make_async_copy(hbm, vmem, local.at[i])
        for i, (hbm, vmem) in enumerate(
            [(home_hbm, home_ref), (help_hbm, help_ref), (w_hbm, w_ref)]
        )
    ]
    for load in loads:
        load.start()
    pl.semaphore_wait(barrier, (n - 1) + (n_tp - 1))

    wait1 = fanout(ny, nz, me, col, sent_ref, got1, send1, recv1)
    lane = lax.broadcasted_iota(jnp.int32, (1, 128), 1)
    low = lane < 64
    loads[0].wait()
    for r in range(rows):
        key = kv_ref[r, 0:1, :].astype(jnp.float32)
        value = kv_ref[r, 1:2, :].astype(jnp.float32)
        fresh_k = jnp.concatenate([key, key], axis=1).astype(jnp.bfloat16)
        fresh_v = jnp.concatenate([value, value], axis=1)
        count = splits_ref[r].astype(jnp.float32)
        top, total, mixed = attend_tile(
            widen([queries_ref[r : r + 1, h * 128 : (h + 1) * 128].astype(jnp.float32) for h in range(pairs)], heads),
            home_ref[r, 0, 0],
            home_ref[r, 1, 0],
            count,
            fresh_k,
            fresh_v,
        )
        for h in range(pairs):
            u, m, l = pair_rows(top, total, mixed, h)
            stat[0, h, r : r + 1, :] = u
            stat[1, h, r : r + 1, :] = m
            stat[2, h, r : r + 1, :] = l
    wait1()
    loads[1].wait()

    partner = helpers_ref[0] // rows
    block = got1[partner].astype(jnp.float32)
    codes = block[slots * pairs : slots * pairs + 1, :]
    stat_lane = lax.broadcasted_iota(jnp.int32, (1, 128), 1)
    stat_row = jnp.zeros((1, 128), jnp.float32)
    for k in range(slots):
        count = codes[:, k : k + 1] * 32.0 + codes[:, slots + k : slots + k + 1]
        pieces = [block[k * pairs + h : k * pairs + h + 1, :] for h in range(pairs)]
        top, total, mixed = attend_tile(
            widen(pieces, heads), help_ref[k, 0, 0], help_ref[k, 1, 0], count
        )
        for h in range(pairs):
            u, m, l = pair_rows(top, total, mixed, h)
            back[k * pairs + h : k * pairs + h + 1, :] = u
        for g in range(heads):
            stat_row = jnp.where(stat_lane == k * heads + g, top[g : g + 1, :], stat_row)
            stat_row = jnp.where(
                stat_lane == (slots + k) * heads + g, total[g : g + 1, :], stat_row
            )
    back[slots * pairs : slots * pairs + 1, :] = stat_row

    wait2 = fanout(ny, nz, me, col, back, got2, send2, recv2)

    sel_row = lax.broadcasted_iota(jnp.int32, (rows, slots), 0)
    sel_col = lax.broadcasted_iota(jnp.int32, (rows, slots), 1)
    fsel = jnp.zeros((rows, slots), jnp.float32)
    rank = jnp.int32(0)
    for r in range(rows):
        is_long = lengths_ref[r] > LONG_AT
        fsel = jnp.where((sel_row == r) & (sel_col == rank) & is_long, 1.0, fsel)
        rank = rank + is_long.astype(jnp.int32)
    has = fsel[:, 0:1]
    for k in range(1, slots):
        has = has + fsel[:, k : k + 1]
    wait2()

    loads[2].wait()
    theirs = got2[partner]
    stats = theirs[slots * pairs : slots * pairs + 1, :]
    left = lax.broadcasted_iota(jnp.int32, (1, 128), 1) < 64
    acc = jnp.zeros(part.shape, jnp.float32)
    for h in range(pairs):
        far_u = fsel[:, 0:1] * theirs[h : h + 1, :]
        for k in range(1, slots):
            far_u = far_u + fsel[:, k : k + 1] * theirs[k * pairs + h : k * pairs + h + 1, :]

        def pick_stat(base):
            x = None
            for k in range(slots):
                j = base + k * heads + 2 * h
                val = jnp.where(left, stats[:, j : j + 1], stats[:, j + 1 : j + 2])
                x = fsel[:, k : k + 1] * val if x is None else x + fsel[:, k : k + 1] * val
            return x

        far_m = jnp.where(has > 0.0, pick_stat(0), -1e30)
        far_l = pick_stat(slots * heads)
        home_u = stat[0, h]
        home_m = stat[1, h]
        home_l = stat[2, h]
        top = jnp.maximum(home_m, far_m)
        home_e = jnp.exp(home_m - top)
        far_e = jnp.exp(far_m - top)
        mix = (home_u * home_e + far_u * far_e) / (home_l * home_e + far_l * far_e)
        acc = acc + jnp.dot(
            mix.astype(jnp.bfloat16),
            w_ref[h * 128 : (h + 1) * 128, :],
            preferred_element_type=jnp.float32,
        )
    part[...] = acc

    sends = []
    for k in range(1, n_tp):
        peer = lax.rem(col + k, n_tp)
        cols = pl.ds(pl.multiple_of(peer * width, width), width)
        copy = pltpu.make_async_remote_copy(
            src_ref=part.at[:, cols],
            dst_ref=held.at[k],
            send_sem=send3.at[k],
            recv_sem=recv3.at[k],
            device_id=(me, peer),
            device_id_type=MESH,
        )
        copy.start()
        sends.append(copy)
    own = pl.ds(pl.multiple_of(col * width, width), width)
    total = part[:, own]
    for copy in sends:
        copy.wait_send()
        copy.wait_recv()
    for k in range(1, n_tp):
        total = total + held[k]
    out_ref[...] = total.astype(out_ref.dtype)


def per_device(ny, nz, queries, new_kv, home_cache, help_cache, lengths, split_at, helper_req, out_weight):
    n_grp = lax.axis_size("grp")
    n_tp = lax.axis_size("tp")
    row_count, width = queries.shape
    slots = help_cache.shape[0]
    pairs = width // 128
    lanes = 128

    sent_shape = (slots * pairs + 1, lanes)

    out_cols = out_weight.shape[1] // n_tp
    vmem = pl.BlockSpec(memory_space=pltpu.VMEM)
    smem = pl.BlockSpec(memory_space=pltpu.SMEM)
    back_rows = slots * pairs + 1
    return pl.pallas_call(
        functools.partial(whole_kernel, ny, nz, n_tp, slots),
        out_shape=jax.ShapeDtypeStruct((row_count, out_cols), jnp.bfloat16),
        in_specs=[smem] * 3 + [vmem] * 2 + [pl.BlockSpec(memory_space=pl.ANY)] * 3,
        out_specs=vmem,
        scratch_shapes=[
            pltpu.VMEM(sent_shape, jnp.bfloat16),
            pltpu.VMEM(home_cache.shape, home_cache.dtype),
            pltpu.VMEM(help_cache.shape, help_cache.dtype),
            pltpu.VMEM(out_weight.shape, out_weight.dtype),
            pltpu.SemaphoreType.DMA((3,)),
            pltpu.VMEM((n_grp,) + sent_shape, jnp.bfloat16),
            pltpu.VMEM((n_grp, back_rows, lanes), jnp.float32),
            pltpu.VMEM((back_rows, lanes), jnp.float32),
            pltpu.VMEM((3, pairs, row_count, lanes), jnp.float32),
            pltpu.VMEM((row_count, out_weight.shape[1]), jnp.float32),
            pltpu.VMEM((n_tp, row_count, out_cols), jnp.float32),
            pltpu.SemaphoreType.DMA((n_grp,)),
            pltpu.SemaphoreType.DMA((n_grp,)),
            pltpu.SemaphoreType.DMA((n_grp,)),
            pltpu.SemaphoreType.DMA((n_grp,)),
            pltpu.SemaphoreType.DMA((n_tp,)),
            pltpu.SemaphoreType.DMA((n_tp,)),
        ],
        compiler_params=pltpu.CompilerParams(collective_id=0, has_side_effects=True),
    )(lengths, split_at, helper_req, queries, new_kv, home_cache, help_cache, out_weight)


def grp_rows(mesh):
    column = list(mesh.devices[:, 0])
    n = len(column)
    coords = [getattr(d, "coords", None) for d in column]
    if coords[0] is not None:
        nz = 1
        while nz < n and coords[nz][1] == coords[0][1]:
            nz += 1
    else:
        nz = 1
        while nz * nz < n:
            nz *= 2
    return n // nz, nz


def solution(mesh):
    ny, nz = grp_rows(mesh)
    return jax.shard_map(
        functools.partial(per_device, ny, nz),
        mesh=mesh,
        in_specs=(
            P("grp", "tp"),
            P("grp", None, "tp"),
            P("grp", None, "tp", None, None),
            P("grp", None, "tp", None, None),
            P("grp"),
            P("grp"),
            P("grp"),
            P("tp", None),
        ),
        out_specs=P("grp", "tp"),
        check_vma=False,
    )
```

```python
import functools

import jax
import jax.numpy as jnp
from jax import lax
from jax.experimental import pallas as pl
from jax.experimental.pallas import tpu as pltpu
from jax.sharding import PartitionSpec as P

MESH = pl.DeviceIdType.MESH
LONG_AT = 1024


def attend(queries, cache, count, fresh):
    row_count = queries.shape[0]
    kv_heads = cache.shape[2]
    head_width = cache.shape[4] // 2
    half = cache.shape[3]
    group_size = queries.shape[1] // (kv_heads * head_width)
    score_scale = head_width ** (-0.5)
    head_rows = queries.reshape(row_count, kv_heads, group_size, head_width)
    blank = jnp.zeros_like(head_rows)
    wide_rows = jnp.stack(
        [
            jnp.concatenate([head_rows, blank], axis=-1),
            jnp.concatenate([blank, head_rows], axis=-1),
        ],
        axis=3,
    )
    key_rows = cache[:, 0]
    value_rows = cache[:, 1]
    scores = (
        jnp.einsum("nkgjc,nkpc->nkgjp", wide_rows, key_rows, preferred_element_type=jnp.float32)
        * score_scale
    )
    position = 2 * jnp.arange(half)[None, :] + jnp.arange(2)[:, None]
    inside = (position[None] < count[:, None, None])[:, None, None]
    top_score = jnp.max(jnp.where(inside, scores, -1e30), axis=(-2, -1))
    if fresh is not None:
        fresh_key = fresh[:, 0].reshape(row_count, kv_heads, head_width)
        fresh_score = (
            jnp.einsum("nkgd,nkd->nkg", head_rows, fresh_key, preferred_element_type=jnp.float32)
            * score_scale
        )
        top_score = jnp.maximum(top_score, fresh_score)
    weights = jnp.where(
        inside, jnp.exp(scores - top_score[..., None, None]), 0.0
    ).astype(jnp.bfloat16)
    weight_sum = jnp.sum(weights.astype(jnp.float32), axis=(-2, -1))
    both = jnp.einsum(
        "nkgjp,nkpc->nkgjc", weights, value_rows, preferred_element_type=jnp.float32
    )
    mixed_sum = both[..., 0, :head_width] + both[..., 1, head_width:]
    if fresh is not None:
        fresh_weight = lax.optimization_barrier(
            jnp.exp(fresh_score - top_score).astype(jnp.bfloat16)
        ).astype(jnp.float32)
        weight_sum = weight_sum + fresh_weight
        fresh_value = fresh[:, 1].reshape(row_count, kv_heads, 1, head_width).astype(jnp.float32)
        mixed_sum = mixed_sum + fresh_weight[..., None] * fresh_value
    return (
        top_score.reshape(row_count, -1),
        weight_sum.reshape(row_count, -1),
        mixed_sum.reshape(row_count, -1, head_width),
    )


def gather_kernel(n, x_ref, out_ref, held, send_sem, recv_sem):
    me = lax.axis_index("grp")
    col = lax.axis_index("tp")

    barrier = pltpu.get_barrier_semaphore()

    def greet(k, carry):
        peer = lax.rem(me + k, n)
        pl.semaphore_signal(barrier, inc=1, device_id=(peer, col), device_id_type=MESH)
        return carry

    lax.fori_loop(1, n, greet, 0)
    pl.semaphore_wait(barrier, n - 1)

    def copy_to(k):
        peer = lax.rem(me + k, n)
        return pltpu.make_async_remote_copy(
            src_ref=x_ref,
            dst_ref=held.at[me],
            send_sem=send_sem.at[k],
            recv_sem=recv_sem.at[k],
            device_id=(peer, col),
            device_id_type=MESH,
        )

    def copy_from(k):
        source = lax.rem(me + n - k, n)
        return pltpu.make_async_remote_copy(
            src_ref=x_ref,
            dst_ref=held.at[source],
            send_sem=send_sem.at[k],
            recv_sem=recv_sem.at[k],
            device_id=(source, col),
            device_id_type=MESH,
        )

    def start(k, carry):
        copy_to(k).start()
        return carry

    lax.fori_loop(1, n, start, 0)

    def finish(k, carry):
        copy_to(k).wait_send()
        copy_from(k).wait_recv()
        return carry

    lax.fori_loop(1, n, finish, 0)
    held[me] = x_ref[...]
    out_ref[...] = held[...]


def gather_grp(x, n, cid):
    return pl.pallas_call(
        functools.partial(gather_kernel, n),
        out_shape=jax.ShapeDtypeStruct((n,) + x.shape, x.dtype),
        in_specs=[pl.BlockSpec(memory_space=pltpu.VMEM)],
        out_specs=pl.BlockSpec(memory_space=pltpu.VMEM),
        scratch_shapes=[
            pltpu.VMEM((n,) + x.shape, x.dtype),
            pltpu.SemaphoreType.DMA((n,)),
            pltpu.SemaphoreType.DMA((n,)),
        ],
        compiler_params=pltpu.CompilerParams(collective_id=cid, has_side_effects=True),
    )(x)


def far_first(i, size):
    half = size // 2
    return half + i // 2 if i % 2 == 0 else half - (i + 1) // 2


def fanout(ny, nz, me, col, src, dst, send, recv):
    my_y = me // nz
    my_z = me % nz
    order = [(far_first(a, ny), far_first(b, nz)) for a in range(ny) for b in range(nz)][:-1]

    def copy(k, peer, slot):
        return pltpu.make_async_remote_copy(
            src_ref=src,
            dst_ref=dst.at[slot],
            send_sem=send.at[k],
            recv_sem=recv.at[k],
            device_id=(peer, col),
            device_id_type=MESH,
        )

    targets = []
    for k, (dy, dz) in enumerate(order):
        peer = lax.rem(my_y + dy, ny) * nz + lax.rem(my_z + dz, nz)
        out = copy(k, peer, me)
        out.start()
        targets.append(out)

    def finish():
        for k, (dy, dz) in enumerate(order):
            targets[k].wait_send()
            source = lax.rem(my_y + (ny - dy), ny) * nz + lax.rem(my_z + (nz - dz), nz)
            copy(k, source, source).wait_recv()

    return finish


def attend_tile(wide, keys, values, count, fresh_k=None, fresh_v=None):
    rows = wide.shape[0]
    scores = lax.dot_general(
        wide, keys, (((1,), (1,)), ((), ())), preferred_element_type=jnp.float32
    ) * 0.125
    half = rows // 2
    row = lax.broadcasted_iota(jnp.int32, scores.shape, 0)
    lane = lax.broadcasted_iota(jnp.int32, scores.shape, 1)
    position = 2 * lane + jnp.where(row >= half, 1, 0)
    inside = position.astype(jnp.float32) < count
    top = jnp.max(jnp.where(inside, scores, -1e30), axis=1, keepdims=True)
    top = jnp.maximum(top, pltpu.roll(top, half, 0))
    if fresh_k is not None:
        fresh_score = jnp.sum(
            wide.astype(jnp.float32) * fresh_k.astype(jnp.float32), axis=1, keepdims=True
        ) * 0.125
        top = jnp.maximum(top, fresh_score)
    weights = jnp.where(inside, jnp.exp(scores - top), 0.0).astype(jnp.bfloat16)
    total = jnp.sum(weights.astype(jnp.float32), axis=1, keepdims=True)
    total = total + pltpu.roll(total, half, 0)
    both = jnp.dot(weights, values, preferred_element_type=jnp.float32)
    mixed = both + pltpu.roll(pltpu.roll(both, half, 0), 64, 1)
    if fresh_k is not None:
        fresh_w = jnp.exp(fresh_score - top).astype(jnp.bfloat16).astype(jnp.float32)
        total = total + fresh_w
        mixed = mixed + fresh_w * fresh_v
    return top, total, mixed


def pair_rows(top, total, mixed, h):
    lane = lax.broadcasted_iota(jnp.int32, (1, mixed.shape[1]), 1)
    left = lane < 64
    g = 2 * h
    u = jnp.where(left, mixed[g : g + 1, :], mixed[g + 5 : g + 6, :])
    m = jnp.where(left, top[g : g + 1, :], top[g + 1 : g + 2, :])
    l = jnp.where(left, total[g : g + 1, :], total[g + 1 : g + 2, :])
    return u, m, l


def widen(pieces, heads):
    lane = lax.broadcasted_iota(jnp.int32, (2 * heads, 128), 1)
    row = lax.broadcasted_iota(jnp.int32, (2 * heads, 128), 0)
    low = lane < 64
    wide = jnp.zeros((2 * heads, 128), jnp.float32)
    for h in range(heads // 2):
        a = pieces[h]
        turned = pltpu.roll(a, 64, 1)
        g = 2 * h
        wide = jnp.where((row == g) & low, a, wide)
        wide = jnp.where((row == g + 1) & low, turned, wide)
        wide = jnp.where((row == heads + g) & ~low, turned, wide)
        wide = jnp.where((row == heads + g + 1) & ~low, a, wide)
    return wide.astype(jnp.bfloat16)


def whole_kernel(ny, nz, n_tp, slots, lengths_ref, splits_ref, helpers_ref, queries_ref, kv_ref,
                 home_hbm, help_hbm, w_hbm, out_ref, sent_ref, home_ref, help_ref, w_ref, local,
                 got1, got2, back, stat, part, held, send1, recv1, send2, recv2, send3, recv3):
    n = ny * nz
    me = lax.axis_index("grp")
    col = lax.axis_index("tp")
    rows = queries_ref.shape[0]
    heads = w_ref.shape[0] // 64
    qw = heads * 64

    pairs = heads // 2
    pick_row = lax.broadcasted_iota(jnp.int32, (slots, rows), 0)
    pick_col = lax.broadcasted_iota(jnp.int32, (slots, rows), 1)
    code_lane = lax.broadcasted_iota(jnp.int32, (1, 128), 1)
    pick = jnp.zeros((slots, rows), jnp.float32)
    code = jnp.zeros((1, 128), jnp.float32)
    rank = jnp.int32(0)
    for r in range(rows):
        is_long = lengths_ref[r] > LONG_AT
        count = lengths_ref[r] - splits_ref[r]
        pick = jnp.where((pick_row == rank) & (pick_col == r) & is_long, 1.0, pick)
        code = jnp.where((code_lane == rank) & is_long, (count // 32).astype(jnp.float32), code)
        code = jnp.where(
            (code_lane == slots + rank) & is_long, (count % 32).astype(jnp.float32), code
        )
        rank = rank + is_long.astype(jnp.int32)
    long_q = jnp.dot(pick.astype(jnp.bfloat16), queries_ref[...], preferred_element_type=jnp.float32)
    pay_row = lax.broadcasted_iota(jnp.int32, sent_ref.shape, 0)
    pay = jnp.where(pay_row == slots * pairs, code, 0.0)
    for k in range(slots):
        for h in range(pairs):
            pay = jnp.where(pay_row == k * pairs + h, long_q[k : k + 1, h * 128 : (h + 1) * 128], pay)
    sent_ref[...] = pay.astype(sent_ref.dtype)
    width = out_ref.shape[1]

    barrier = pltpu.get_barrier_semaphore()

    my_y = me // nz
    my_z = me % nz
    for a in range(ny):
        for b in range(nz):
            dy, dz = far_first(a, ny), far_first(b, nz)
            if dy == 0 and dz == 0:
                continue
            peer = lax.rem(my_y + dy, ny) * nz + lax.rem(my_z + dz, nz)
            pl.semaphore_signal(barrier, inc=1, device_id=(peer, col), device_id_type=MESH)
    for k in range(1, n_tp):
        peer = lax.rem(col + k, n_tp)
        pl.semaphore_signal(barrier, inc=1, device_id=(me, peer), device_id_type=MESH)
    loads = [
        pltpu.make_async_copy(hbm, vmem, local.at[i])
        for i, (hbm, vmem) in enumerate(
            [(home_hbm, home_ref), (help_hbm, help_ref), (w_hbm, w_ref)]
        )
    ]
    for load in loads:
        load.start()
    pl.semaphore_wait(barrier, (n - 1) + (n_tp - 1))

    wait1 = fanout(ny, nz, me, col, sent_ref, got1, send1, recv1)
    lane = lax.broadcasted_iota(jnp.int32, (1, 128), 1)
    low = lane < 64
    loads[0].wait()
    for r in range(rows):
        key = kv_ref[r, 0:1, :].astype(jnp.float32)
        value = kv_ref[r, 1:2, :].astype(jnp.float32)
        fresh_k = jnp.concatenate([key, key], axis=1).astype(jnp.bfloat16)
        fresh_v = jnp.concatenate([value, value], axis=1)
        count = splits_ref[r].astype(jnp.float32)
        top, total, mixed = attend_tile(
            widen([queries_ref[r : r + 1, h * 128 : (h + 1) * 128].astype(jnp.float32) for h in range(pairs)], heads),
            home_ref[r, 0, 0],
            home_ref[r, 1, 0],
            count,
            fresh_k,
            fresh_v,
        )
        for h in range(pairs):
            u, m, l = pair_rows(top, total, mixed, h)
            stat[0, h, r : r + 1, :] = u
            stat[1, h, r : r + 1, :] = m
            stat[2, h, r : r + 1, :] = l
    wait1()
    loads[1].wait()

    partner = helpers_ref[0] // rows
    block = got1[partner].astype(jnp.float32)
    codes = block[slots * pairs : slots * pairs + 1, :]
    stat_lane = lax.broadcasted_iota(jnp.int32, (1, 128), 1)
    stat_row = jnp.zeros((1, 128), jnp.float32)
    for k in range(slots):
        count = codes[:, k : k + 1] * 32.0 + codes[:, slots + k : slots + k + 1]
        pieces = [block[k * pairs + h : k * pairs + h + 1, :] for h in range(pairs)]
        top, total, mixed = attend_tile(
            widen(pieces, heads), help_ref[k, 0, 0], help_ref[k, 1, 0], count
        )
        for h in range(pairs):
            u, m, l = pair_rows(top, total, mixed, h)
            back[k * pairs + h : k * pairs + h + 1, :] = u.astype(back.dtype)
        n_st = slots * heads
        for g in range(heads):
            for which, value in enumerate((top[g : g + 1, :], total[g : g + 1, :])):
                hi = value.astype(jnp.bfloat16).astype(jnp.float32)
                rest = value - hi
                mid = rest.astype(jnp.bfloat16).astype(jnp.float32)
                lo = (rest - mid).astype(jnp.bfloat16).astype(jnp.float32)
                for part_i, piece in enumerate((hi, mid, lo)):
                    at = (3 * which + part_i) * n_st + k * heads + g
                    stat_row = jnp.where(stat_lane == at, piece, stat_row)
    back[slots * pairs : slots * pairs + 1, :] = stat_row.astype(back.dtype)

    wait2 = fanout(ny, nz, me, col, back, got2, send2, recv2)

    sel_row = lax.broadcasted_iota(jnp.int32, (rows, slots), 0)
    sel_col = lax.broadcasted_iota(jnp.int32, (rows, slots), 1)
    fsel = jnp.zeros((rows, slots), jnp.float32)
    rank = jnp.int32(0)
    for r in range(rows):
        is_long = lengths_ref[r] > LONG_AT
        fsel = jnp.where((sel_row == r) & (sel_col == rank) & is_long, 1.0, fsel)
        rank = rank + is_long.astype(jnp.int32)
    has = fsel[:, 0:1]
    for k in range(1, slots):
        has = has + fsel[:, k : k + 1]
    wait2()

    loads[2].wait()
    theirs = got2[partner].astype(jnp.float32)
    packed = theirs[slots * pairs : slots * pairs + 1, :]
    n_st = slots * heads

    def joined(which):
        base = 3 * which * n_st
        return (
            packed[:, base : base + n_st]
            + packed[:, base + n_st : base + 2 * n_st]
            + packed[:, base + 2 * n_st : base + 3 * n_st]
        )

    stats = jnp.concatenate([joined(0), joined(1)], axis=1)
    left = lax.broadcasted_iota(jnp.int32, (1, 128), 1) < 64
    acc = jnp.zeros(part.shape, jnp.float32)
    for h in range(pairs):
        far_u = fsel[:, 0:1] * theirs[h : h + 1, :]
        for k in range(1, slots):
            far_u = far_u + fsel[:, k : k + 1] * theirs[k * pairs + h : k * pairs + h + 1, :]

        def pick_stat(base):
            x = None
            for k in range(slots):
                j = base + k * heads + 2 * h
                val = jnp.where(left, stats[:, j : j + 1], stats[:, j + 1 : j + 2])
                x = fsel[:, k : k + 1] * val if x is None else x + fsel[:, k : k + 1] * val
            return x

        far_m = jnp.where(has > 0.0, pick_stat(0), -1e30)
        far_l = pick_stat(slots * heads)
        home_u = stat[0, h]
        home_m = stat[1, h]
        home_l = stat[2, h]
        top = jnp.maximum(home_m, far_m)
        home_e = jnp.exp(home_m - top)
        far_e = jnp.exp(far_m - top)
        mix = (home_u * home_e + far_u * far_e) / (home_l * home_e + far_l * far_e)
        acc = acc + jnp.dot(
            mix.astype(jnp.bfloat16),
            w_ref[h * 128 : (h + 1) * 128, :],
            preferred_element_type=jnp.float32,
        )
    part[...] = acc

    sends = []
    for k in range(1, n_tp):
        peer = lax.rem(col + k, n_tp)
        cols = pl.ds(pl.multiple_of(peer * width, width), width)
        copy = pltpu.make_async_remote_copy(
            src_ref=part.at[:, cols],
            dst_ref=held.at[k],
            send_sem=send3.at[k],
            recv_sem=recv3.at[k],
            device_id=(me, peer),
            device_id_type=MESH,
        )
        copy.start()
        sends.append(copy)
    own = pl.ds(pl.multiple_of(col * width, width), width)
    total = part[:, own]
    for copy in sends:
        copy.wait_send()
        copy.wait_recv()
    for k in range(1, n_tp):
        total = total + held[k]
    out_ref[...] = total.astype(out_ref.dtype)


def per_device(ny, nz, queries, new_kv, home_cache, help_cache, lengths, split_at, helper_req, out_weight):
    n_grp = lax.axis_size("grp")
    n_tp = lax.axis_size("tp")
    row_count, width = queries.shape
    slots = help_cache.shape[0]
    pairs = width // 128
    lanes = 128

    sent_shape = (slots * pairs + 1, lanes)

    out_cols = out_weight.shape[1] // n_tp
    vmem = pl.BlockSpec(memory_space=pltpu.VMEM)
    smem = pl.BlockSpec(memory_space=pltpu.SMEM)
    back_rows = slots * pairs + 1
    return pl.pallas_call(
        functools.partial(whole_kernel, ny, nz, n_tp, slots),
        out_shape=jax.ShapeDtypeStruct((row_count, out_cols), jnp.bfloat16),
        in_specs=[smem] * 3 + [vmem] * 2 + [pl.BlockSpec(memory_space=pl.ANY)] * 3,
        out_specs=vmem,
        scratch_shapes=[
            pltpu.VMEM(sent_shape, jnp.bfloat16),
            pltpu.VMEM(home_cache.shape, home_cache.dtype),
            pltpu.VMEM(help_cache.shape, help_cache.dtype),
            pltpu.VMEM(out_weight.shape, out_weight.dtype),
            pltpu.SemaphoreType.DMA((3,)),
            pltpu.VMEM((n_grp,) + sent_shape, jnp.bfloat16),
            pltpu.VMEM((n_grp, back_rows, lanes), jnp.bfloat16),
            pltpu.VMEM((back_rows, lanes), jnp.bfloat16),
            pltpu.VMEM((3, pairs, row_count, lanes), jnp.float32),
            pltpu.VMEM((row_count, out_weight.shape[1]), jnp.float32),
            pltpu.VMEM((n_tp, row_count, out_cols), jnp.float32),
            pltpu.SemaphoreType.DMA((n_grp,)),
            pltpu.SemaphoreType.DMA((n_grp,)),
            pltpu.SemaphoreType.DMA((n_grp,)),
            pltpu.SemaphoreType.DMA((n_grp,)),
            pltpu.SemaphoreType.DMA((n_tp,)),
            pltpu.SemaphoreType.DMA((n_tp,)),
        ],
        compiler_params=pltpu.CompilerParams(collective_id=0, has_side_effects=True),
    )(lengths, split_at, helper_req, queries, new_kv, home_cache, help_cache, out_weight)


def grp_rows(mesh):
    column = list(mesh.devices[:, 0])
    n = len(column)
    coords = [getattr(d, "coords", None) for d in column]
    if coords[0] is not None:
        nz = 1
        while nz < n and coords[nz][1] == coords[0][1]:
            nz += 1
    else:
        nz = 1
        while nz * nz < n:
            nz *= 2
    return n // nz, nz


def solution(mesh):
    ny, nz = grp_rows(mesh)
    return jax.shard_map(
        functools.partial(per_device, ny, nz),
        mesh=mesh,
        in_specs=(
            P("grp", "tp"),
            P("grp", None, "tp"),
            P("grp", None, "tp", None, None),
            P("grp", None, "tp", None, None),
            P("grp"),
            P("grp"),
            P("grp"),
            P("tp", None),
        ),
        out_specs=P("grp", "tp"),
        check_vma=False,
    )
```

```python
import functools

import jax
import jax.numpy as jnp
from jax import lax
from jax.experimental import pallas as pl
from jax.experimental.pallas import tpu as pltpu
from jax.sharding import PartitionSpec as P

MESH = pl.DeviceIdType.MESH
LONG_AT = 1024


def attend(queries, cache, count, fresh):
    row_count = queries.shape[0]
    kv_heads = cache.shape[2]
    head_width = cache.shape[4] // 2
    half = cache.shape[3]
    group_size = queries.shape[1] // (kv_heads * head_width)
    score_scale = head_width ** (-0.5)
    head_rows = queries.reshape(row_count, kv_heads, group_size, head_width)
    blank = jnp.zeros_like(head_rows)
    wide_rows = jnp.stack(
        [
            jnp.concatenate([head_rows, blank], axis=-1),
            jnp.concatenate([blank, head_rows], axis=-1),
        ],
        axis=3,
    )
    key_rows = cache[:, 0]
    value_rows = cache[:, 1]
    scores = (
        jnp.einsum("nkgjc,nkpc->nkgjp", wide_rows, key_rows, preferred_element_type=jnp.float32)
        * score_scale
    )
    position = 2 * jnp.arange(half)[None, :] + jnp.arange(2)[:, None]
    inside = (position[None] < count[:, None, None])[:, None, None]
    top_score = jnp.max(jnp.where(inside, scores, -1e30), axis=(-2, -1))
    if fresh is not None:
        fresh_key = fresh[:, 0].reshape(row_count, kv_heads, head_width)
        fresh_score = (
            jnp.einsum("nkgd,nkd->nkg", head_rows, fresh_key, preferred_element_type=jnp.float32)
            * score_scale
        )
        top_score = jnp.maximum(top_score, fresh_score)
    weights = jnp.where(
        inside, jnp.exp(scores - top_score[..., None, None]), 0.0
    ).astype(jnp.bfloat16)
    weight_sum = jnp.sum(weights.astype(jnp.float32), axis=(-2, -1))
    both = jnp.einsum(
        "nkgjp,nkpc->nkgjc", weights, value_rows, preferred_element_type=jnp.float32
    )
    mixed_sum = both[..., 0, :head_width] + both[..., 1, head_width:]
    if fresh is not None:
        fresh_weight = lax.optimization_barrier(
            jnp.exp(fresh_score - top_score).astype(jnp.bfloat16)
        ).astype(jnp.float32)
        weight_sum = weight_sum + fresh_weight
        fresh_value = fresh[:, 1].reshape(row_count, kv_heads, 1, head_width).astype(jnp.float32)
        mixed_sum = mixed_sum + fresh_weight[..., None] * fresh_value
    return (
        top_score.reshape(row_count, -1),
        weight_sum.reshape(row_count, -1),
        mixed_sum.reshape(row_count, -1, head_width),
    )


def gather_kernel(n, x_ref, out_ref, held, send_sem, recv_sem):
    me = lax.axis_index("grp")
    col = lax.axis_index("tp")

    barrier = pltpu.get_barrier_semaphore()

    def greet(k, carry):
        peer = lax.rem(me + k, n)
        pl.semaphore_signal(barrier, inc=1, device_id=(peer, col), device_id_type=MESH)
        return carry

    lax.fori_loop(1, n, greet, 0)
    pl.semaphore_wait(barrier, n - 1)

    def copy_to(k):
        peer = lax.rem(me + k, n)
        return pltpu.make_async_remote_copy(
            src_ref=x_ref,
            dst_ref=held.at[me],
            send_sem=send_sem.at[k],
            recv_sem=recv_sem.at[k],
            device_id=(peer, col),
            device_id_type=MESH,
        )

    def copy_from(k):
        source = lax.rem(me + n - k, n)
        return pltpu.make_async_remote_copy(
            src_ref=x_ref,
            dst_ref=held.at[source],
            send_sem=send_sem.at[k],
            recv_sem=recv_sem.at[k],
            device_id=(source, col),
            device_id_type=MESH,
        )

    def start(k, carry):
        copy_to(k).start()
        return carry

    lax.fori_loop(1, n, start, 0)

    def finish(k, carry):
        copy_to(k).wait_send()
        copy_from(k).wait_recv()
        return carry

    lax.fori_loop(1, n, finish, 0)
    held[me] = x_ref[...]
    out_ref[...] = held[...]


def gather_grp(x, n, cid):
    return pl.pallas_call(
        functools.partial(gather_kernel, n),
        out_shape=jax.ShapeDtypeStruct((n,) + x.shape, x.dtype),
        in_specs=[pl.BlockSpec(memory_space=pltpu.VMEM)],
        out_specs=pl.BlockSpec(memory_space=pltpu.VMEM),
        scratch_shapes=[
            pltpu.VMEM((n,) + x.shape, x.dtype),
            pltpu.SemaphoreType.DMA((n,)),
            pltpu.SemaphoreType.DMA((n,)),
        ],
        compiler_params=pltpu.CompilerParams(collective_id=cid, has_side_effects=True),
    )(x)


def far_first(i, size):
    half = size // 2
    return half + i // 2 if i % 2 == 0 else half - (i + 1) // 2


def fanout(ny, nz, me, col, src, dst, send, recv):
    my_y = me // nz
    my_z = me % nz
    order = [(far_first(a, ny), far_first(b, nz)) for a in range(ny) for b in range(nz)][:-1]

    def copy(k, peer, slot):
        return pltpu.make_async_remote_copy(
            src_ref=src,
            dst_ref=dst.at[slot],
            send_sem=send.at[k],
            recv_sem=recv.at[k],
            device_id=(peer, col),
            device_id_type=MESH,
        )

    targets = []
    for k, (dy, dz) in enumerate(order):
        peer = lax.rem(my_y + dy, ny) * nz + lax.rem(my_z + dz, nz)
        out = copy(k, peer, me)
        out.start()
        targets.append(out)

    def finish():
        for k, (dy, dz) in enumerate(order):
            targets[k].wait_send()
            source = lax.rem(my_y + (ny - dy), ny) * nz + lax.rem(my_z + (nz - dz), nz)
            copy(k, source, source).wait_recv()

    return finish


def attend_tile(wide, keys, values, count, fresh_k=None, fresh_v=None):
    rows = wide.shape[0]
    scores = lax.dot_general(
        wide, keys, (((1,), (1,)), ((), ())), preferred_element_type=jnp.float32
    ) * 0.125
    half = rows // 2
    row = lax.broadcasted_iota(jnp.int32, scores.shape, 0)
    lane = lax.broadcasted_iota(jnp.int32, scores.shape, 1)
    position = 2 * lane + jnp.where(row >= half, 1, 0)
    inside = position.astype(jnp.float32) < count
    top = jnp.max(jnp.where(inside, scores, -1e30), axis=1, keepdims=True)
    top = jnp.maximum(top, pltpu.roll(top, half, 0))
    if fresh_k is not None:
        fresh_score = jnp.sum(
            wide.astype(jnp.float32) * fresh_k.astype(jnp.float32), axis=1, keepdims=True
        ) * 0.125
        top = jnp.maximum(top, fresh_score)
    weights = jnp.where(inside, jnp.exp(scores - top), 0.0).astype(jnp.bfloat16)
    total = jnp.sum(weights.astype(jnp.float32), axis=1, keepdims=True)
    total = total + pltpu.roll(total, half, 0)
    both = jnp.dot(weights, values, preferred_element_type=jnp.float32)
    mixed = both + pltpu.roll(pltpu.roll(both, half, 0), 64, 1)
    if fresh_k is not None:
        fresh_w = jnp.exp(fresh_score - top).astype(jnp.bfloat16).astype(jnp.float32)
        total = total + fresh_w
        mixed = mixed + fresh_w * fresh_v
    return top, total, mixed


def pair_rows(top, total, mixed, h):
    lane = lax.broadcasted_iota(jnp.int32, (1, mixed.shape[1]), 1)
    left = lane < 64
    g = 2 * h
    u = jnp.where(left, mixed[g : g + 1, :], mixed[g + 5 : g + 6, :])
    m = jnp.where(left, top[g : g + 1, :], top[g + 1 : g + 2, :])
    l = jnp.where(left, total[g : g + 1, :], total[g + 1 : g + 2, :])
    return u, m, l


def widen(pieces, heads):
    lane = lax.broadcasted_iota(jnp.int32, (2 * heads, 128), 1)
    row = lax.broadcasted_iota(jnp.int32, (2 * heads, 128), 0)
    low = lane < 64
    wide = jnp.zeros((2 * heads, 128), jnp.float32)
    for h in range(heads // 2):
        a = pieces[h]
        turned = pltpu.roll(a, 64, 1)
        g = 2 * h
        wide = jnp.where((row == g) & low, a, wide)
        wide = jnp.where((row == g + 1) & low, turned, wide)
        wide = jnp.where((row == heads + g) & ~low, turned, wide)
        wide = jnp.where((row == heads + g + 1) & ~low, a, wide)
    return wide.astype(jnp.bfloat16)


def whole_kernel(ny, nz, n_tp, slots, lengths_ref, splits_ref, helpers_ref, queries_ref, kv_ref,
                 home_hbm, help_hbm, w_hbm, out_ref, sent_ref, home_ref, help_ref, w_ref, local,
                 got1, got2, back, stat, part, held, send1, recv1, send2, recv2, send3, recv3):
    n = ny * nz
    me = lax.axis_index("grp")
    col = lax.axis_index("tp")
    rows = queries_ref.shape[0]
    heads = w_ref.shape[0] // 64
    qw = heads * 64

    pairs = heads // 2
    pick_row = lax.broadcasted_iota(jnp.int32, (slots, rows), 0)
    pick_col = lax.broadcasted_iota(jnp.int32, (slots, rows), 1)
    code_lane = lax.broadcasted_iota(jnp.int32, (1, 128), 1)
    pick = jnp.zeros((slots, rows), jnp.float32)
    code = jnp.zeros((1, 128), jnp.float32)
    rank = jnp.int32(0)
    for r in range(rows):
        is_long = lengths_ref[r] > LONG_AT
        count = lengths_ref[r] - splits_ref[r]
        pick = jnp.where((pick_row == rank) & (pick_col == r) & is_long, 1.0, pick)
        code = jnp.where((code_lane == rank) & is_long, (count // 32).astype(jnp.float32), code)
        code = jnp.where(
            (code_lane == slots + rank) & is_long, (count % 32).astype(jnp.float32), code
        )
        rank = rank + is_long.astype(jnp.int32)
    long_q = jnp.dot(pick.astype(jnp.bfloat16), queries_ref[...], preferred_element_type=jnp.float32)
    pay_row = lax.broadcasted_iota(jnp.int32, sent_ref.shape, 0)
    pay = jnp.where(pay_row == slots * pairs, code, 0.0)
    for k in range(slots):
        for h in range(pairs):
            pay = jnp.where(pay_row == k * pairs + h, long_q[k : k + 1, h * 128 : (h + 1) * 128], pay)
    sent_ref[...] = pay.astype(sent_ref.dtype)
    width = out_ref.shape[1]

    barrier = pltpu.get_barrier_semaphore()

    my_y = me // nz
    my_z = me % nz
    for a in range(ny):
        for b in range(nz):
            dy, dz = far_first(a, ny), far_first(b, nz)
            if dy == 0 and dz == 0:
                continue
            peer = lax.rem(my_y + dy, ny) * nz + lax.rem(my_z + dz, nz)
            pl.semaphore_signal(barrier, inc=1, device_id=(peer, col), device_id_type=MESH)
    for k in range(1, n_tp):
        peer = lax.rem(col + k, n_tp)
        pl.semaphore_signal(barrier, inc=1, device_id=(me, peer), device_id_type=MESH)
    loads = [
        pltpu.make_async_copy(hbm, vmem, local.at[i])
        for i, (hbm, vmem) in enumerate(
            [(home_hbm, home_ref), (help_hbm, help_ref), (w_hbm, w_ref)]
        )
    ]
    for load in loads:
        load.start()
    pl.semaphore_wait(barrier, (n - 1) + (n_tp - 1))

    wait1 = fanout(ny, nz, me, col, sent_ref, got1, send1, recv1)
    lane = lax.broadcasted_iota(jnp.int32, (1, 128), 1)
    low = lane < 64
    loads[0].wait()
    for r in range(rows):
        key = kv_ref[r, 0:1, :].astype(jnp.float32)
        value = kv_ref[r, 1:2, :].astype(jnp.float32)
        fresh_k = jnp.concatenate([key, key], axis=1).astype(jnp.bfloat16)
        fresh_v = jnp.concatenate([value, value], axis=1)
        count = splits_ref[r].astype(jnp.float32)
        top, total, mixed = attend_tile(
            widen([queries_ref[r : r + 1, h * 128 : (h + 1) * 128].astype(jnp.float32) for h in range(pairs)], heads),
            home_ref[r, 0, 0],
            home_ref[r, 1, 0],
            count,
            fresh_k,
            fresh_v,
        )
        for h in range(pairs):
            u, m, l = pair_rows(top, total, mixed, h)
            stat[0, h, r : r + 1, :] = u
            stat[1, h, r : r + 1, :] = m
            stat[2, h, r : r + 1, :] = l
    wait1()
    loads[1].wait()

    partner = helpers_ref[0] // rows
    block = got1[partner].astype(jnp.float32)
    codes = block[slots * pairs : slots * pairs + 1, :]
    stat_lane = lax.broadcasted_iota(jnp.int32, (1, 128), 1)
    stat_row = jnp.zeros((1, 128), jnp.float32)
    for k in range(slots):
        count = codes[:, k : k + 1] * 32.0 + codes[:, slots + k : slots + k + 1]
        pieces = [block[k * pairs + h : k * pairs + h + 1, :] for h in range(pairs)]
        top, total, mixed = attend_tile(
            widen(pieces, heads), help_ref[k, 0, 0], help_ref[k, 1, 0], count
        )
        for h in range(pairs):
            u, m, l = pair_rows(top, total, mixed, h)
            back[k * pairs + h : k * pairs + h + 1, :] = u
        for g in range(heads):
            stat_row = jnp.where(stat_lane == k * heads + g, top[g : g + 1, :], stat_row)
            stat_row = jnp.where(
                stat_lane == (slots + k) * heads + g, total[g : g + 1, :], stat_row
            )
    back[slots * pairs : slots * pairs + 1, :] = stat_row

    wait2 = fanout(ny, nz, me, col, back, got2, send2, recv2)

    sel_row = lax.broadcasted_iota(jnp.int32, (rows, slots), 0)
    sel_col = lax.broadcasted_iota(jnp.int32, (rows, slots), 1)
    fsel = jnp.zeros((rows, slots), jnp.float32)
    rank = jnp.int32(0)
    for r in range(rows):
        is_long = lengths_ref[r] > LONG_AT
        fsel = jnp.where((sel_row == r) & (sel_col == rank) & is_long, 1.0, fsel)
        rank = rank + is_long.astype(jnp.int32)
    has = fsel[:, 0:1]
    for k in range(1, slots):
        has = has + fsel[:, k : k + 1]
    wait2()

    loads[2].wait()
    theirs = got2[partner]
    stats = theirs[slots * pairs : slots * pairs + 1, :]
    left = lax.broadcasted_iota(jnp.int32, (1, 128), 1) < 64
    mixes = []
    for h in range(pairs):
        far_u = fsel[:, 0:1] * theirs[h : h + 1, :]
        for k in range(1, slots):
            far_u = far_u + fsel[:, k : k + 1] * theirs[k * pairs + h : k * pairs + h + 1, :]

        def pick_stat(base):
            x = None
            for k in range(slots):
                j = base + k * heads + 2 * h
                val = jnp.where(left, stats[:, j : j + 1], stats[:, j + 1 : j + 2])
                x = fsel[:, k : k + 1] * val if x is None else x + fsel[:, k : k + 1] * val
            return x

        far_m = jnp.where(has > 0.0, pick_stat(0), -1e30)
        far_l = pick_stat(slots * heads)
        home_u = stat[0, h]
        home_m = stat[1, h]
        home_l = stat[2, h]
        top = jnp.maximum(home_m, far_m)
        home_e = jnp.exp(home_m - top)
        far_e = jnp.exp(far_m - top)
        mix = (home_u * home_e + far_u * far_e) / (home_l * home_e + far_l * far_e)
        mixes.append(mix.astype(jnp.bfloat16))
    part[...] = jnp.dot(
        jnp.concatenate(mixes, axis=1), w_ref[...], preferred_element_type=jnp.float32
    )

    sends = []
    for k in range(1, n_tp):
        peer = lax.rem(col + k, n_tp)
        cols = pl.ds(pl.multiple_of(peer * width, width), width)
        copy = pltpu.make_async_remote_copy(
            src_ref=part.at[:, cols],
            dst_ref=held.at[k],
            send_sem=send3.at[k],
            recv_sem=recv3.at[k],
            device_id=(me, peer),
            device_id_type=MESH,
        )
        copy.start()
        sends.append(copy)
    own = pl.ds(pl.multiple_of(col * width, width), width)
    total = part[:, own]
    for copy in sends:
        copy.wait_send()
        copy.wait_recv()
    for k in range(1, n_tp):
        total = total + held[k]
    out_ref[...] = total.astype(out_ref.dtype)


def per_device(ny, nz, queries, new_kv, home_cache, help_cache, lengths, split_at, helper_req, out_weight):
    n_grp = lax.axis_size("grp")
    n_tp = lax.axis_size("tp")
    row_count, width = queries.shape
    slots = help_cache.shape[0]
    pairs = width // 128
    lanes = 128

    sent_shape = (slots * pairs + 1, lanes)

    out_cols = out_weight.shape[1] // n_tp
    vmem = pl.BlockSpec(memory_space=pltpu.VMEM)
    smem = pl.BlockSpec(memory_space=pltpu.SMEM)
    back_rows = slots * pairs + 1
    return pl.pallas_call(
        functools.partial(whole_kernel, ny, nz, n_tp, slots),
        out_shape=jax.ShapeDtypeStruct((row_count, out_cols), jnp.bfloat16),
        in_specs=[smem] * 3 + [vmem] * 2 + [pl.BlockSpec(memory_space=pl.ANY)] * 3,
        out_specs=vmem,
        scratch_shapes=[
            pltpu.VMEM(sent_shape, jnp.bfloat16),
            pltpu.VMEM(home_cache.shape, home_cache.dtype),
            pltpu.VMEM(help_cache.shape, help_cache.dtype),
            pltpu.VMEM(out_weight.shape, out_weight.dtype),
            pltpu.SemaphoreType.DMA((3,)),
            pltpu.VMEM((n_grp,) + sent_shape, jnp.bfloat16),
            pltpu.VMEM((n_grp, back_rows, lanes), jnp.float32),
            pltpu.VMEM((back_rows, lanes), jnp.float32),
            pltpu.VMEM((3, pairs, row_count, lanes), jnp.float32),
            pltpu.VMEM((row_count, out_weight.shape[1]), jnp.float32),
            pltpu.VMEM((n_tp, row_count, out_cols), jnp.float32),
            pltpu.SemaphoreType.DMA((n_grp,)),
            pltpu.SemaphoreType.DMA((n_grp,)),
            pltpu.SemaphoreType.DMA((n_grp,)),
            pltpu.SemaphoreType.DMA((n_grp,)),
            pltpu.SemaphoreType.DMA((n_tp,)),
            pltpu.SemaphoreType.DMA((n_tp,)),
        ],
        compiler_params=pltpu.CompilerParams(collective_id=0, has_side_effects=True),
    )(lengths, split_at, helper_req, queries, new_kv, home_cache, help_cache, out_weight)


def grp_rows(mesh):
    column = list(mesh.devices[:, 0])
    n = len(column)
    coords = [getattr(d, "coords", None) for d in column]
    if coords[0] is not None:
        nz = 1
        while nz < n and coords[nz][1] == coords[0][1]:
            nz += 1
    else:
        nz = 1
        while nz * nz < n:
            nz *= 2
    return n // nz, nz


def solution(mesh):
    ny, nz = grp_rows(mesh)
    return jax.shard_map(
        functools.partial(per_device, ny, nz),
        mesh=mesh,
        in_specs=(
            P("grp", "tp"),
            P("grp", None, "tp"),
            P("grp", None, "tp", None, None),
            P("grp", None, "tp", None, None),
            P("grp"),
            P("grp"),
            P("grp"),
            P("tp", None),
        ),
        out_specs=P("grp", "tp"),
        check_vma=False,
    )
```

```python
import functools

import jax
import jax.numpy as jnp
from jax import lax
from jax.experimental import pallas as pl
from jax.experimental.pallas import tpu as pltpu
from jax.sharding import PartitionSpec as P

MESH = pl.DeviceIdType.MESH
LONG_AT = 1024


def attend(queries, cache, count, fresh):
    row_count = queries.shape[0]
    kv_heads = cache.shape[2]
    head_width = cache.shape[4] // 2
    half = cache.shape[3]
    group_size = queries.shape[1] // (kv_heads * head_width)
    score_scale = head_width ** (-0.5)
    head_rows = queries.reshape(row_count, kv_heads, group_size, head_width)
    blank = jnp.zeros_like(head_rows)
    wide_rows = jnp.stack(
        [
            jnp.concatenate([head_rows, blank], axis=-1),
            jnp.concatenate([blank, head_rows], axis=-1),
        ],
        axis=3,
    )
    key_rows = cache[:, 0]
    value_rows = cache[:, 1]
    scores = (
        jnp.einsum("nkgjc,nkpc->nkgjp", wide_rows, key_rows, preferred_element_type=jnp.float32)
        * score_scale
    )
    position = 2 * jnp.arange(half)[None, :] + jnp.arange(2)[:, None]
    inside = (position[None] < count[:, None, None])[:, None, None]
    top_score = jnp.max(jnp.where(inside, scores, -1e30), axis=(-2, -1))
    if fresh is not None:
        fresh_key = fresh[:, 0].reshape(row_count, kv_heads, head_width)
        fresh_score = (
            jnp.einsum("nkgd,nkd->nkg", head_rows, fresh_key, preferred_element_type=jnp.float32)
            * score_scale
        )
        top_score = jnp.maximum(top_score, fresh_score)
    weights = jnp.where(
        inside, jnp.exp(scores - top_score[..., None, None]), 0.0
    ).astype(jnp.bfloat16)
    weight_sum = jnp.sum(weights.astype(jnp.float32), axis=(-2, -1))
    both = jnp.einsum(
        "nkgjp,nkpc->nkgjc", weights, value_rows, preferred_element_type=jnp.float32
    )
    mixed_sum = both[..., 0, :head_width] + both[..., 1, head_width:]
    if fresh is not None:
        fresh_weight = lax.optimization_barrier(
            jnp.exp(fresh_score - top_score).astype(jnp.bfloat16)
        ).astype(jnp.float32)
        weight_sum = weight_sum + fresh_weight
        fresh_value = fresh[:, 1].reshape(row_count, kv_heads, 1, head_width).astype(jnp.float32)
        mixed_sum = mixed_sum + fresh_weight[..., None] * fresh_value
    return (
        top_score.reshape(row_count, -1),
        weight_sum.reshape(row_count, -1),
        mixed_sum.reshape(row_count, -1, head_width),
    )


def gather_kernel(n, x_ref, out_ref, held, send_sem, recv_sem):
    me = lax.axis_index("grp")
    col = lax.axis_index("tp")

    barrier = pltpu.get_barrier_semaphore()

    def greet(k, carry):
        peer = lax.rem(me + k, n)
        pl.semaphore_signal(barrier, inc=1, device_id=(peer, col), device_id_type=MESH)
        return carry

    lax.fori_loop(1, n, greet, 0)
    pl.semaphore_wait(barrier, n - 1)

    def copy_to(k):
        peer = lax.rem(me + k, n)
        return pltpu.make_async_remote_copy(
            src_ref=x_ref,
            dst_ref=held.at[me],
            send_sem=send_sem.at[k],
            recv_sem=recv_sem.at[k],
            device_id=(peer, col),
            device_id_type=MESH,
        )

    def copy_from(k):
        source = lax.rem(me + n - k, n)
        return pltpu.make_async_remote_copy(
            src_ref=x_ref,
            dst_ref=held.at[source],
            send_sem=send_sem.at[k],
            recv_sem=recv_sem.at[k],
            device_id=(source, col),
            device_id_type=MESH,
        )

    def start(k, carry):
        copy_to(k).start()
        return carry

    lax.fori_loop(1, n, start, 0)

    def finish(k, carry):
        copy_to(k).wait_send()
        copy_from(k).wait_recv()
        return carry

    lax.fori_loop(1, n, finish, 0)
    held[me] = x_ref[...]
    out_ref[...] = held[...]


def gather_grp(x, n, cid):
    return pl.pallas_call(
        functools.partial(gather_kernel, n),
        out_shape=jax.ShapeDtypeStruct((n,) + x.shape, x.dtype),
        in_specs=[pl.BlockSpec(memory_space=pltpu.VMEM)],
        out_specs=pl.BlockSpec(memory_space=pltpu.VMEM),
        scratch_shapes=[
            pltpu.VMEM((n,) + x.shape, x.dtype),
            pltpu.SemaphoreType.DMA((n,)),
            pltpu.SemaphoreType.DMA((n,)),
        ],
        compiler_params=pltpu.CompilerParams(collective_id=cid, has_side_effects=True),
    )(x)


def far_first(i, size):
    half = size // 2
    return half + i // 2 if i % 2 == 0 else half - (i + 1) // 2


def fanout(ny, nz, me, col, src, dst, send, recv):
    my_y = me // nz
    my_z = me % nz
    order = [(far_first(a, ny), far_first(b, nz)) for a in range(ny) for b in range(nz)][:-1]

    def copy(k, peer, slot):
        return pltpu.make_async_remote_copy(
            src_ref=src,
            dst_ref=dst.at[slot],
            send_sem=send.at[k],
            recv_sem=recv.at[k],
            device_id=(peer, col),
            device_id_type=MESH,
        )

    targets = []
    for k, (dy, dz) in enumerate(order):
        peer = lax.rem(my_y + dy, ny) * nz + lax.rem(my_z + dz, nz)
        out = copy(k, peer, me)
        out.start()
        targets.append(out)

    def finish():
        for k, (dy, dz) in enumerate(order):
            targets[k].wait_send()
            source = lax.rem(my_y + (ny - dy), ny) * nz + lax.rem(my_z + (nz - dz), nz)
            copy(k, source, source).wait_recv()

    return finish


def attend_tile(wide, keys, values, count, fresh_k=None, fresh_v=None):
    rows = wide.shape[0]
    scores = lax.dot_general(
        wide, keys, (((1,), (1,)), ((), ())), preferred_element_type=jnp.float32
    ) * 0.125
    half = rows // 2
    row = lax.broadcasted_iota(jnp.int32, scores.shape, 0)
    lane = lax.broadcasted_iota(jnp.int32, scores.shape, 1)
    position = 2 * lane + jnp.where(row >= half, 1, 0)
    inside = position.astype(jnp.float32) < count
    top = jnp.max(jnp.where(inside, scores, -1e30), axis=1, keepdims=True)
    top = jnp.maximum(top, pltpu.roll(top, half, 0))
    if fresh_k is not None:
        fresh_score = jnp.sum(
            wide.astype(jnp.float32) * fresh_k.astype(jnp.float32), axis=1, keepdims=True
        ) * 0.125
        top = jnp.maximum(top, fresh_score)
    weights = jnp.where(inside, jnp.exp(scores - top), 0.0).astype(jnp.bfloat16)
    total = jnp.sum(weights.astype(jnp.float32), axis=1, keepdims=True)
    total = total + pltpu.roll(total, half, 0)
    both = jnp.dot(weights, values, preferred_element_type=jnp.float32)
    mixed = both + pltpu.roll(pltpu.roll(both, half, 0), 64, 1)
    if fresh_k is not None:
        fresh_w = jnp.exp(fresh_score - top).astype(jnp.bfloat16).astype(jnp.float32)
        total = total + fresh_w
        mixed = mixed + fresh_w * fresh_v
    return top, total, mixed


def pair_rows(top, total, mixed, h):
    lane = lax.broadcasted_iota(jnp.int32, (1, mixed.shape[1]), 1)
    left = lane < 64
    g = 2 * h
    u = jnp.where(left, mixed[g : g + 1, :], mixed[g + 5 : g + 6, :])
    m = jnp.where(left, top[g : g + 1, :], top[g + 1 : g + 2, :])
    l = jnp.where(left, total[g : g + 1, :], total[g + 1 : g + 2, :])
    return u, m, l


def widen(pieces, heads):
    lane = lax.broadcasted_iota(jnp.int32, (2 * heads, 128), 1)
    row = lax.broadcasted_iota(jnp.int32, (2 * heads, 128), 0)
    low = lane < 64
    wide = jnp.zeros((2 * heads, 128), jnp.float32)
    for h in range(heads // 2):
        a = pieces[h]
        turned = pltpu.roll(a, 64, 1)
        g = 2 * h
        wide = jnp.where((row == g) & low, a, wide)
        wide = jnp.where((row == g + 1) & low, turned, wide)
        wide = jnp.where((row == heads + g) & ~low, turned, wide)
        wide = jnp.where((row == heads + g + 1) & ~low, a, wide)
    return wide.astype(jnp.bfloat16)


def whole_kernel(ny, nz, n_tp, slots, lengths_ref, splits_ref, helpers_ref, queries_ref, kv_ref,
                 home_hbm, help_hbm, w_hbm, out_ref, sent_ref, home_ref, help_ref, w_ref, local,
                 got1, got2, back, stat, part, held, send1, recv1, send2, recv2, send3, recv3):
    n = ny * nz
    me = lax.axis_index("grp")
    col = lax.axis_index("tp")
    rows = queries_ref.shape[0]
    heads = w_ref.shape[0] // 64
    qw = heads * 64

    pairs = heads // 2
    pick_row = lax.broadcasted_iota(jnp.int32, (slots, rows), 0)
    pick_col = lax.broadcasted_iota(jnp.int32, (slots, rows), 1)
    code_lane = lax.broadcasted_iota(jnp.int32, (1, 128), 1)
    pick = jnp.zeros((slots, rows), jnp.float32)
    code = jnp.zeros((1, 128), jnp.float32)
    rank = jnp.int32(0)
    for r in range(rows):
        is_long = lengths_ref[r] > LONG_AT
        count = lengths_ref[r] - splits_ref[r]
        pick = jnp.where((pick_row == rank) & (pick_col == r) & is_long, 1.0, pick)
        code = jnp.where((code_lane == rank) & is_long, (count // 32).astype(jnp.float32), code)
        code = jnp.where(
            (code_lane == slots + rank) & is_long, (count % 32).astype(jnp.float32), code
        )
        rank = rank + is_long.astype(jnp.int32)
    long_q = jnp.dot(pick.astype(jnp.bfloat16), queries_ref[...], preferred_element_type=jnp.float32)
    pay_row = lax.broadcasted_iota(jnp.int32, sent_ref.shape, 0)
    pay = jnp.where(pay_row == slots * pairs, code, 0.0)
    for k in range(slots):
        for h in range(pairs):
            pay = jnp.where(pay_row == k * pairs + h, long_q[k : k + 1, h * 128 : (h + 1) * 128], pay)
    sent_ref[...] = pay.astype(sent_ref.dtype)
    width = out_ref.shape[1]

    barrier = pltpu.get_barrier_semaphore()

    my_y = me // nz
    my_z = me % nz
    for a in range(ny):
        for b in range(nz):
            dy, dz = far_first(a, ny), far_first(b, nz)
            if dy == 0 and dz == 0:
                continue
            peer = lax.rem(my_y + dy, ny) * nz + lax.rem(my_z + dz, nz)
            pl.semaphore_signal(barrier, inc=1, device_id=(peer, col), device_id_type=MESH)
    for k in range(1, n_tp):
        peer = lax.rem(col + k, n_tp)
        pl.semaphore_signal(barrier, inc=1, device_id=(me, peer), device_id_type=MESH)
    loads = [
        pltpu.make_async_copy(hbm, vmem, local.at[i])
        for i, (hbm, vmem) in enumerate(
            [(home_hbm, home_ref), (help_hbm, help_ref), (w_hbm, w_ref)]
        )
    ]
    for load in loads:
        load.start()
    pl.semaphore_wait(barrier, (n - 1) + (n_tp - 1))

    wait1 = fanout(ny, nz, me, col, sent_ref, got1, send1, recv1)
    lane = lax.broadcasted_iota(jnp.int32, (1, 128), 1)
    low = lane < 64
    def home_rows(first, last):
        for r in range(first, last):
            key = kv_ref[r, 0:1, :].astype(jnp.float32)
            value = kv_ref[r, 1:2, :].astype(jnp.float32)
            fresh_k = jnp.concatenate([key, key], axis=1).astype(jnp.bfloat16)
            fresh_v = jnp.concatenate([value, value], axis=1)
            count = splits_ref[r].astype(jnp.float32)
            top, total, mixed = attend_tile(
                widen([queries_ref[r : r + 1, h * 128 : (h + 1) * 128].astype(jnp.float32) for h in range(pairs)], heads),
                home_ref[r, 0, 0],
                home_ref[r, 1, 0],
                count,
                fresh_k,
                fresh_v,
            )
            for h in range(pairs):
                u, m, l = pair_rows(top, total, mixed, h)
                stat[0, h, r : r + 1, :] = u
                stat[1, h, r : r + 1, :] = m
                stat[2, h, r : r + 1, :] = l

    loads[0].wait()
    home_rows(0, rows // 2)
    wait1()
    loads[1].wait()

    partner = helpers_ref[0] // rows
    block = got1[partner].astype(jnp.float32)
    codes = block[slots * pairs : slots * pairs + 1, :]
    stat_lane = lax.broadcasted_iota(jnp.int32, (1, 128), 1)
    stat_row = jnp.zeros((1, 128), jnp.float32)
    for k in range(slots):
        count = codes[:, k : k + 1] * 32.0 + codes[:, slots + k : slots + k + 1]
        pieces = [block[k * pairs + h : k * pairs + h + 1, :] for h in range(pairs)]
        top, total, mixed = attend_tile(
            widen(pieces, heads), help_ref[k, 0, 0], help_ref[k, 1, 0], count
        )
        for h in range(pairs):
            u, m, l = pair_rows(top, total, mixed, h)
            back[k * pairs + h : k * pairs + h + 1, :] = u
        for g in range(heads):
            stat_row = jnp.where(stat_lane == k * heads + g, top[g : g + 1, :], stat_row)
            stat_row = jnp.where(
                stat_lane == (slots + k) * heads + g, total[g : g + 1, :], stat_row
            )
    back[slots * pairs : slots * pairs + 1, :] = stat_row

    wait2 = fanout(ny, nz, me, col, back, got2, send2, recv2)
    home_rows(rows // 2, rows)

    sel_row = lax.broadcasted_iota(jnp.int32, (rows, slots), 0)
    sel_col = lax.broadcasted_iota(jnp.int32, (rows, slots), 1)
    fsel = jnp.zeros((rows, slots), jnp.float32)
    rank = jnp.int32(0)
    for r in range(rows):
        is_long = lengths_ref[r] > LONG_AT
        fsel = jnp.where((sel_row == r) & (sel_col == rank) & is_long, 1.0, fsel)
        rank = rank + is_long.astype(jnp.int32)
    has = fsel[:, 0:1]
    for k in range(1, slots):
        has = has + fsel[:, k : k + 1]
    wait2()

    loads[2].wait()
    theirs = got2[partner]
    stats = theirs[slots * pairs : slots * pairs + 1, :]
    left = lax.broadcasted_iota(jnp.int32, (1, 128), 1) < 64
    mixes = []
    for h in range(pairs):
        far_u = fsel[:, 0:1] * theirs[h : h + 1, :]
        for k in range(1, slots):
            far_u = far_u + fsel[:, k : k + 1] * theirs[k * pairs + h : k * pairs + h + 1, :]

        def pick_stat(base):
            x = None
            for k in range(slots):
                j = base + k * heads + 2 * h
                val = jnp.where(left, stats[:, j : j + 1], stats[:, j + 1 : j + 2])
                x = fsel[:, k : k + 1] * val if x is None else x + fsel[:, k : k + 1] * val
            return x

        far_m = jnp.where(has > 0.0, pick_stat(0), -1e30)
        far_l = pick_stat(slots * heads)
        home_u = stat[0, h]
        home_m = stat[1, h]
        home_l = stat[2, h]
        top = jnp.maximum(home_m, far_m)
        home_e = jnp.exp(home_m - top)
        far_e = jnp.exp(far_m - top)
        mix = (home_u * home_e + far_u * far_e) / (home_l * home_e + far_l * far_e)
        mixes.append(mix.astype(jnp.bfloat16))
    part[...] = jnp.dot(
        jnp.concatenate(mixes, axis=1), w_ref[...], preferred_element_type=jnp.float32
    )

    sends = []
    for k in range(1, n_tp):
        peer = lax.rem(col + k, n_tp)
        cols = pl.ds(pl.multiple_of(peer * width, width), width)
        copy = pltpu.make_async_remote_copy(
            src_ref=part.at[:, cols],
            dst_ref=held.at[k],
            send_sem=send3.at[k],
            recv_sem=recv3.at[k],
            device_id=(me, peer),
            device_id_type=MESH,
        )
        copy.start()
        sends.append(copy)
    own = pl.ds(pl.multiple_of(col * width, width), width)
    total = part[:, own]
    for copy in sends:
        copy.wait_send()
        copy.wait_recv()
    for k in range(1, n_tp):
        total = total + held[k]
    out_ref[...] = total.astype(out_ref.dtype)


def per_device(ny, nz, queries, new_kv, home_cache, help_cache, lengths, split_at, helper_req, out_weight):
    n_grp = lax.axis_size("grp")
    n_tp = lax.axis_size("tp")
    row_count, width = queries.shape
    slots = help_cache.shape[0]
    pairs = width // 128
    lanes = 128

    sent_shape = (slots * pairs + 1, lanes)

    out_cols = out_weight.shape[1] // n_tp
    vmem = pl.BlockSpec(memory_space=pltpu.VMEM)
    smem = pl.BlockSpec(memory_space=pltpu.SMEM)
    back_rows = slots * pairs + 1
    return pl.pallas_call(
        functools.partial(whole_kernel, ny, nz, n_tp, slots),
        out_shape=jax.ShapeDtypeStruct((row_count, out_cols), jnp.bfloat16),
        in_specs=[smem] * 3 + [vmem] * 2 + [pl.BlockSpec(memory_space=pl.ANY)] * 3,
        out_specs=vmem,
        scratch_shapes=[
            pltpu.VMEM(sent_shape, jnp.bfloat16),
            pltpu.VMEM(home_cache.shape, home_cache.dtype),
            pltpu.VMEM(help_cache.shape, help_cache.dtype),
            pltpu.VMEM(out_weight.shape, out_weight.dtype),
            pltpu.SemaphoreType.DMA((3,)),
            pltpu.VMEM((n_grp,) + sent_shape, jnp.bfloat16),
            pltpu.VMEM((n_grp, back_rows, lanes), jnp.float32),
            pltpu.VMEM((back_rows, lanes), jnp.float32),
            pltpu.VMEM((3, pairs, row_count, lanes), jnp.float32),
            pltpu.VMEM((row_count, out_weight.shape[1]), jnp.float32),
            pltpu.VMEM((n_tp, row_count, out_cols), jnp.float32),
            pltpu.SemaphoreType.DMA((n_grp,)),
            pltpu.SemaphoreType.DMA((n_grp,)),
            pltpu.SemaphoreType.DMA((n_grp,)),
            pltpu.SemaphoreType.DMA((n_grp,)),
            pltpu.SemaphoreType.DMA((n_tp,)),
            pltpu.SemaphoreType.DMA((n_tp,)),
        ],
        compiler_params=pltpu.CompilerParams(collective_id=0, has_side_effects=True),
    )(lengths, split_at, helper_req, queries, new_kv, home_cache, help_cache, out_weight)


def grp_rows(mesh):
    column = list(mesh.devices[:, 0])
    n = len(column)
    coords = [getattr(d, "coords", None) for d in column]
    if coords[0] is not None:
        nz = 1
        while nz < n and coords[nz][1] == coords[0][1]:
            nz += 1
    else:
        nz = 1
        while nz * nz < n:
            nz *= 2
    return n // nz, nz


def solution(mesh):
    ny, nz = grp_rows(mesh)
    return jax.shard_map(
        functools.partial(per_device, ny, nz),
        mesh=mesh,
        in_specs=(
            P("grp", "tp"),
            P("grp", None, "tp"),
            P("grp", None, "tp", None, None),
            P("grp", None, "tp", None, None),
            P("grp"),
            P("grp"),
            P("grp"),
            P("tp", None),
        ),
        out_specs=P("grp", "tp"),
        check_vma=False,
    )
```

```python
import functools

import jax
import jax.numpy as jnp
from jax import lax
from jax.experimental import pallas as pl
from jax.experimental.pallas import tpu as pltpu
from jax.sharding import PartitionSpec as P

MESH = pl.DeviceIdType.MESH
LONG_AT = 1024


def attend(queries, cache, count, fresh):
    row_count = queries.shape[0]
    kv_heads = cache.shape[2]
    head_width = cache.shape[4] // 2
    half = cache.shape[3]
    group_size = queries.shape[1] // (kv_heads * head_width)
    score_scale = head_width ** (-0.5)
    head_rows = queries.reshape(row_count, kv_heads, group_size, head_width)
    blank = jnp.zeros_like(head_rows)
    wide_rows = jnp.stack(
        [
            jnp.concatenate([head_rows, blank], axis=-1),
            jnp.concatenate([blank, head_rows], axis=-1),
        ],
        axis=3,
    )
    key_rows = cache[:, 0]
    value_rows = cache[:, 1]
    scores = (
        jnp.einsum("nkgjc,nkpc->nkgjp", wide_rows, key_rows, preferred_element_type=jnp.float32)
        * score_scale
    )
    position = 2 * jnp.arange(half)[None, :] + jnp.arange(2)[:, None]
    inside = (position[None] < count[:, None, None])[:, None, None]
    top_score = jnp.max(jnp.where(inside, scores, -1e30), axis=(-2, -1))
    if fresh is not None:
        fresh_key = fresh[:, 0].reshape(row_count, kv_heads, head_width)
        fresh_score = (
            jnp.einsum("nkgd,nkd->nkg", head_rows, fresh_key, preferred_element_type=jnp.float32)
            * score_scale
        )
        top_score = jnp.maximum(top_score, fresh_score)
    weights = jnp.where(
        inside, jnp.exp(scores - top_score[..., None, None]), 0.0
    ).astype(jnp.bfloat16)
    weight_sum = jnp.sum(weights.astype(jnp.float32), axis=(-2, -1))
    both = jnp.einsum(
        "nkgjp,nkpc->nkgjc", weights, value_rows, preferred_element_type=jnp.float32
    )
    mixed_sum = both[..., 0, :head_width] + both[..., 1, head_width:]
    if fresh is not None:
        fresh_weight = lax.optimization_barrier(
            jnp.exp(fresh_score - top_score).astype(jnp.bfloat16)
        ).astype(jnp.float32)
        weight_sum = weight_sum + fresh_weight
        fresh_value = fresh[:, 1].reshape(row_count, kv_heads, 1, head_width).astype(jnp.float32)
        mixed_sum = mixed_sum + fresh_weight[..., None] * fresh_value
    return (
        top_score.reshape(row_count, -1),
        weight_sum.reshape(row_count, -1),
        mixed_sum.reshape(row_count, -1, head_width),
    )


def gather_kernel(n, x_ref, out_ref, held, send_sem, recv_sem):
    me = lax.axis_index("grp")
    col = lax.axis_index("tp")

    barrier = pltpu.get_barrier_semaphore()

    def greet(k, carry):
        peer = lax.rem(me + k, n)
        pl.semaphore_signal(barrier, inc=1, device_id=(peer, col), device_id_type=MESH)
        return carry

    lax.fori_loop(1, n, greet, 0)
    pl.semaphore_wait(barrier, n - 1)

    def copy_to(k):
        peer = lax.rem(me + k, n)
        return pltpu.make_async_remote_copy(
            src_ref=x_ref,
            dst_ref=held.at[me],
            send_sem=send_sem.at[k],
            recv_sem=recv_sem.at[k],
            device_id=(peer, col),
            device_id_type=MESH,
        )

    def copy_from(k):
        source = lax.rem(me + n - k, n)
        return pltpu.make_async_remote_copy(
            src_ref=x_ref,
            dst_ref=held.at[source],
            send_sem=send_sem.at[k],
            recv_sem=recv_sem.at[k],
            device_id=(source, col),
            device_id_type=MESH,
        )

    def start(k, carry):
        copy_to(k).start()
        return carry

    lax.fori_loop(1, n, start, 0)

    def finish(k, carry):
        copy_to(k).wait_send()
        copy_from(k).wait_recv()
        return carry

    lax.fori_loop(1, n, finish, 0)
    held[me] = x_ref[...]
    out_ref[...] = held[...]


def gather_grp(x, n, cid):
    return pl.pallas_call(
        functools.partial(gather_kernel, n),
        out_shape=jax.ShapeDtypeStruct((n,) + x.shape, x.dtype),
        in_specs=[pl.BlockSpec(memory_space=pltpu.VMEM)],
        out_specs=pl.BlockSpec(memory_space=pltpu.VMEM),
        scratch_shapes=[
            pltpu.VMEM((n,) + x.shape, x.dtype),
            pltpu.SemaphoreType.DMA((n,)),
            pltpu.SemaphoreType.DMA((n,)),
        ],
        compiler_params=pltpu.CompilerParams(collective_id=cid, has_side_effects=True),
    )(x)


def far_first(i, size):
    half = size // 2
    return half + i // 2 if i % 2 == 0 else half - (i + 1) // 2


def fanout(ny, nz, me, col, src, dst, send, recv):
    my_y = me // nz
    my_z = me % nz
    order = [(far_first(a, ny), far_first(b, nz)) for a in range(ny) for b in range(nz)][:-1]

    def copy(k, peer, slot):
        return pltpu.make_async_remote_copy(
            src_ref=src,
            dst_ref=dst.at[slot],
            send_sem=send.at[k],
            recv_sem=recv.at[k],
            device_id=(peer, col),
            device_id_type=MESH,
        )

    targets = []
    for k, (dy, dz) in enumerate(order):
        peer = lax.rem(my_y + dy, ny) * nz + lax.rem(my_z + dz, nz)
        out = copy(k, peer, me)
        out.start()
        targets.append(out)

    def finish():
        for k, (dy, dz) in enumerate(order):
            targets[k].wait_send()
            source = lax.rem(my_y + (ny - dy), ny) * nz + lax.rem(my_z + (nz - dz), nz)
            copy(k, source, source).wait_recv()

    return finish


def attend_tile(wide, keys, values, count, fresh_k=None, fresh_v=None):
    rows = wide.shape[0]
    scores = lax.dot_general(
        wide, keys, (((1,), (1,)), ((), ())), preferred_element_type=jnp.float32
    ) * 0.125
    half = rows // 2
    row = lax.broadcasted_iota(jnp.int32, scores.shape, 0)
    lane = lax.broadcasted_iota(jnp.int32, scores.shape, 1)
    position = 2 * lane + jnp.where(row >= half, 1, 0)
    inside = position.astype(jnp.float32) < count
    top = jnp.max(jnp.where(inside, scores, -1e30), axis=1, keepdims=True)
    top = jnp.maximum(top, pltpu.roll(top, half, 0))
    if fresh_k is not None:
        fresh_score = jnp.sum(
            wide.astype(jnp.float32) * fresh_k.astype(jnp.float32), axis=1, keepdims=True
        ) * 0.125
        top = jnp.maximum(top, fresh_score)
    weights = jnp.where(inside, jnp.exp(scores - top), 0.0).astype(jnp.bfloat16)
    total = jnp.sum(weights.astype(jnp.float32), axis=1, keepdims=True)
    total = total + pltpu.roll(total, half, 0)
    both = jnp.dot(weights, values, preferred_element_type=jnp.float32)
    mixed = both + pltpu.roll(pltpu.roll(both, half, 0), 64, 1)
    if fresh_k is not None:
        fresh_w = jnp.exp(fresh_score - top).astype(jnp.bfloat16).astype(jnp.float32)
        total = total + fresh_w
        mixed = mixed + fresh_w * fresh_v
    return top, total, mixed


def pair_rows(top, total, mixed, h):
    lane = lax.broadcasted_iota(jnp.int32, (1, mixed.shape[1]), 1)
    left = lane < 64
    g = 2 * h
    u = jnp.where(left, mixed[g : g + 1, :], mixed[g + 5 : g + 6, :])
    m = jnp.where(left, top[g : g + 1, :], top[g + 1 : g + 2, :])
    l = jnp.where(left, total[g : g + 1, :], total[g + 1 : g + 2, :])
    return u, m, l


def widen(pieces, heads):
    lane = lax.broadcasted_iota(jnp.int32, (2 * heads, 128), 1)
    row = lax.broadcasted_iota(jnp.int32, (2 * heads, 128), 0)
    low = lane < 64
    wide = jnp.zeros((2 * heads, 128), jnp.float32)
    for h in range(heads // 2):
        a = pieces[h]
        turned = pltpu.roll(a, 64, 1)
        g = 2 * h
        wide = jnp.where((row == g) & low, a, wide)
        wide = jnp.where((row == g + 1) & low, turned, wide)
        wide = jnp.where((row == heads + g) & ~low, turned, wide)
        wide = jnp.where((row == heads + g + 1) & ~low, a, wide)
    return wide.astype(jnp.bfloat16)


def whole_kernel(ny, nz, n_tp, slots, lengths_ref, splits_ref, helpers_ref, queries_ref, kv_ref,
                 home_hbm, help_hbm, w_hbm, out_ref, sent_ref, home_ref, help_ref, w_ref, local,
                 got1, got2, back, stat, part, held, send1, recv1, send2, recv2, send3, recv3):
    n = ny * nz
    me = lax.axis_index("grp")
    col = lax.axis_index("tp")
    rows = queries_ref.shape[0]
    heads = w_ref.shape[0] // 64
    qw = heads * 64

    pairs = heads // 2
    pick_row = lax.broadcasted_iota(jnp.int32, (slots, rows), 0)
    pick_col = lax.broadcasted_iota(jnp.int32, (slots, rows), 1)
    code_lane = lax.broadcasted_iota(jnp.int32, (1, 128), 1)
    pick = jnp.zeros((slots, rows), jnp.float32)
    code = jnp.zeros((1, 128), jnp.float32)
    rank = jnp.int32(0)
    for r in range(rows):
        is_long = lengths_ref[r] > LONG_AT
        count = lengths_ref[r] - splits_ref[r]
        pick = jnp.where((pick_row == rank) & (pick_col == r) & is_long, 1.0, pick)
        code = jnp.where((code_lane == rank) & is_long, (count // 32).astype(jnp.float32), code)
        code = jnp.where(
            (code_lane == slots + rank) & is_long, (count % 32).astype(jnp.float32), code
        )
        rank = rank + is_long.astype(jnp.int32)
    long_q = jnp.dot(pick.astype(jnp.bfloat16), queries_ref[...], preferred_element_type=jnp.float32)
    pay_row = lax.broadcasted_iota(jnp.int32, sent_ref.shape, 0)
    pay = jnp.where(pay_row == slots * pairs, code, 0.0)
    for k in range(slots):
        for h in range(pairs):
            pay = jnp.where(pay_row == k * pairs + h, long_q[k : k + 1, h * 128 : (h + 1) * 128], pay)
    sent_ref[...] = pay.astype(sent_ref.dtype)
    width = out_ref.shape[1]

    barrier = pltpu.get_barrier_semaphore()

    my_y = me // nz
    my_z = me % nz
    for a in range(ny):
        for b in range(nz):
            dy, dz = far_first(a, ny), far_first(b, nz)
            if dy == 0 and dz == 0:
                continue
            peer = lax.rem(my_y + dy, ny) * nz + lax.rem(my_z + dz, nz)
            pl.semaphore_signal(barrier, inc=1, device_id=(peer, col), device_id_type=MESH)
    for k in range(1, n_tp):
        peer = lax.rem(col + k, n_tp)
        pl.semaphore_signal(barrier, inc=1, device_id=(me, peer), device_id_type=MESH)
    loads = [
        pltpu.make_async_copy(hbm, vmem, local.at[i])
        for i, (hbm, vmem) in enumerate(
            [(home_hbm, home_ref), (help_hbm, help_ref), (w_hbm, w_ref)]
        )
    ]
    for load in loads:
        load.start()
    pl.semaphore_wait(barrier, (n - 1) + (n_tp - 1))

    wait1 = fanout(ny, nz, me, col, sent_ref, got1, send1, recv1)
    lane = lax.broadcasted_iota(jnp.int32, (1, 128), 1)
    low = lane < 64
    loads[0].wait()
    for r in range(rows):
        key = kv_ref[r, 0:1, :].astype(jnp.float32)
        value = kv_ref[r, 1:2, :].astype(jnp.float32)
        fresh_k = jnp.concatenate([key, key], axis=1).astype(jnp.bfloat16)
        fresh_v = jnp.concatenate([value, value], axis=1)
        count = splits_ref[r].astype(jnp.float32)
        top, total, mixed = attend_tile(
            widen([queries_ref[r : r + 1, h * 128 : (h + 1) * 128].astype(jnp.float32) for h in range(pairs)], heads),
            home_ref[r, 0, 0],
            home_ref[r, 1, 0],
            count,
            fresh_k,
            fresh_v,
        )
        for h in range(pairs):
            u, m, l = pair_rows(top, total, mixed, h)
            stat[0, h, r : r + 1, :] = u
            stat[1, h, r : r + 1, :] = m
            stat[2, h, r : r + 1, :] = l
    wait1()
    loads[1].wait()

    partner = helpers_ref[0] // rows
    block = got1[partner].astype(jnp.float32)
    codes = block[slots * pairs : slots * pairs + 1, :]
    stat_lane = lax.broadcasted_iota(jnp.int32, (1, 128), 1)
    stat_row = jnp.zeros((1, 128), jnp.float32)
    for k in range(slots):
        count = codes[:, k : k + 1] * 32.0 + codes[:, slots + k : slots + k + 1]
        pieces = [block[k * pairs + h : k * pairs + h + 1, :] for h in range(pairs)]
        top, total, mixed = attend_tile(
            widen(pieces, heads), help_ref[k, 0, 0], help_ref[k, 1, 0], count
        )
        for h in range(pairs):
            u, m, l = pair_rows(top, total, mixed, h)
            back[k * pairs + h : k * pairs + h + 1, :] = u
        for g in range(heads):
            stat_row = jnp.where(stat_lane == k * heads + g, top[g : g + 1, :], stat_row)
            stat_row = jnp.where(
                stat_lane == (slots + k) * heads + g, total[g : g + 1, :], stat_row
            )
    back[slots * pairs : slots * pairs + 1, :] = stat_row

    wait2 = fanout(ny, nz, me, col, back, got2, send2, recv2)

    sel_row = lax.broadcasted_iota(jnp.int32, (rows, slots), 0)
    sel_col = lax.broadcasted_iota(jnp.int32, (rows, slots), 1)
    fsel = jnp.zeros((rows, slots), jnp.float32)
    rank = jnp.int32(0)
    for r in range(rows):
        is_long = lengths_ref[r] > LONG_AT
        fsel = jnp.where((sel_row == r) & (sel_col == rank) & is_long, 1.0, fsel)
        rank = rank + is_long.astype(jnp.int32)
    has = fsel[:, 0:1]
    for k in range(1, slots):
        has = has + fsel[:, k : k + 1]
    wait2()

    loads[2].wait()
    theirs = got2[partner]
    stats = theirs[slots * pairs : slots * pairs + 1, :]
    left = lax.broadcasted_iota(jnp.int32, (1, 128), 1) < 64
    mixes = []
    for h in range(pairs):
        far_u = fsel[:, 0:1] * theirs[h : h + 1, :]
        for k in range(1, slots):
            far_u = far_u + fsel[:, k : k + 1] * theirs[k * pairs + h : k * pairs + h + 1, :]

        def pick_stat(base):
            x = None
            for k in range(slots):
                j = base + k * heads + 2 * h
                val = jnp.where(left, stats[:, j : j + 1], stats[:, j + 1 : j + 2])
                x = fsel[:, k : k + 1] * val if x is None else x + fsel[:, k : k + 1] * val
            return x

        far_m = jnp.where(has > 0.0, pick_stat(0), -1e30)
        far_l = pick_stat(slots * heads)
        home_u = stat[0, h]
        home_m = stat[1, h]
        home_l = stat[2, h]
        top = jnp.maximum(home_m, far_m)
        home_e = jnp.exp(home_m - top)
        far_e = jnp.exp(far_m - top)
        mix = (home_u * home_e + far_u * far_e) / (home_l * home_e + far_l * far_e)
        mixes.append(mix.astype(jnp.bfloat16))
    projected = jnp.dot(
        jnp.concatenate(mixes, axis=1), w_ref[...], preferred_element_type=jnp.float32
    )
    for j in range(n_tp):
        part[j] = projected[:, j * width : (j + 1) * width]

    sends = []
    for k in range(1, n_tp):
        peer = lax.rem(col + k, n_tp)
        cols = pl.ds(pl.multiple_of(peer * width, width), width)
        copy = pltpu.make_async_remote_copy(
            src_ref=part.at[peer],
            dst_ref=held.at[k],
            send_sem=send3.at[k],
            recv_sem=recv3.at[k],
            device_id=(me, peer),
            device_id_type=MESH,
        )
        copy.start()
        sends.append(copy)
    own = pl.ds(pl.multiple_of(col * width, width), width)
    total = part[col]
    for copy in sends:
        copy.wait_send()
        copy.wait_recv()
    for k in range(1, n_tp):
        total = total + held[k]
    out_ref[...] = total.astype(out_ref.dtype)


def per_device(ny, nz, queries, new_kv, home_cache, help_cache, lengths, split_at, helper_req, out_weight):
    n_grp = lax.axis_size("grp")
    n_tp = lax.axis_size("tp")
    row_count, width = queries.shape
    slots = help_cache.shape[0]
    pairs = width // 128
    lanes = 128

    sent_shape = (slots * pairs + 1, lanes)

    out_cols = out_weight.shape[1] // n_tp
    vmem = pl.BlockSpec(memory_space=pltpu.VMEM)
    smem = pl.BlockSpec(memory_space=pltpu.SMEM)
    back_rows = slots * pairs + 1
    return pl.pallas_call(
        functools.partial(whole_kernel, ny, nz, n_tp, slots),
        out_shape=jax.ShapeDtypeStruct((row_count, out_cols), jnp.bfloat16),
        in_specs=[smem] * 3 + [vmem] * 2 + [pl.BlockSpec(memory_space=pl.ANY)] * 3,
        out_specs=vmem,
        scratch_shapes=[
            pltpu.VMEM(sent_shape, jnp.bfloat16),
            pltpu.VMEM(home_cache.shape, home_cache.dtype),
            pltpu.VMEM(help_cache.shape, help_cache.dtype),
            pltpu.VMEM(out_weight.shape, out_weight.dtype),
            pltpu.SemaphoreType.DMA((3,)),
            pltpu.VMEM((n_grp,) + sent_shape, jnp.bfloat16),
            pltpu.VMEM((n_grp, back_rows, lanes), jnp.float32),
            pltpu.VMEM((back_rows, lanes), jnp.float32),
            pltpu.VMEM((3, pairs, row_count, lanes), jnp.float32),
            pltpu.VMEM((n_tp, row_count, out_cols), jnp.float32),
            pltpu.VMEM((n_tp, row_count, out_cols), jnp.float32),
            pltpu.SemaphoreType.DMA((n_grp,)),
            pltpu.SemaphoreType.DMA((n_grp,)),
            pltpu.SemaphoreType.DMA((n_grp,)),
            pltpu.SemaphoreType.DMA((n_grp,)),
            pltpu.SemaphoreType.DMA((n_tp,)),
            pltpu.SemaphoreType.DMA((n_tp,)),
        ],
        compiler_params=pltpu.CompilerParams(collective_id=0, has_side_effects=True),
    )(lengths, split_at, helper_req, queries, new_kv, home_cache, help_cache, out_weight)


def grp_rows(mesh):
    column = list(mesh.devices[:, 0])
    n = len(column)
    coords = [getattr(d, "coords", None) for d in column]
    if coords[0] is not None:
        nz = 1
        while nz < n and coords[nz][1] == coords[0][1]:
            nz += 1
    else:
        nz = 1
        while nz * nz < n:
            nz *= 2
    return n // nz, nz


def solution(mesh):
    ny, nz = grp_rows(mesh)
    return jax.shard_map(
        functools.partial(per_device, ny, nz),
        mesh=mesh,
        in_specs=(
            P("grp", "tp"),
            P("grp", None, "tp"),
            P("grp", None, "tp", None, None),
            P("grp", None, "tp", None, None),
            P("grp"),
            P("grp"),
            P("grp"),
            P("tp", None),
        ),
        out_specs=P("grp", "tp"),
        check_vma=False,
    )
```
